256 devices in a mesh: row: 16 (over x_hi, z), col: 16 (over y, x_lo, core).
Axes of the slice: x: 4 (x_hi: 2, x_lo: 2; x = x_hi * 2 + x_lo), y: 4, z: 8, core: 2. Of those that a mesh axis runs over, the one named last changes fastest.
Arguments:
- panel_values: bfloat16 [65536, 256], P(('row', 'col')), may hold values from -6 to 6
- near_tiles: bfloat16 [8192, 256, 256], P(('row', 'col')), may hold values from -0.01953125 to 0.01953125
- far_left: bfloat16 [32768, 64, 256], P(('row', 'col')), may hold values from -0.0390625 to 0.0390625
- far_right: bfloat16 [32768, 64, 256], P(('row', 'col')), may hold values from -0.375 to 0.375
- near_rows: int32 [8192], P(('row', 'col')), may hold values from 0 to 255, as said below
- far_rows: int32 [32768], P(('row', 'col')), may hold values from 0 to 255, as said below
Outputs:
- panel_product: bfloat16 [65536, 256], P(('row', 'col'))
The draws below stay inside these ranges and needn't reach their ends.
Inputs may be any that keep to these rules, and one draw needn't show every extreme that they name: `near_rows`: entries of the device at grid position (i, j) lie in its row group, clusters i * 16 * 1 to (i + 1) * 16 - 1. `far_rows`: entries of the device at grid position (i, j) lie in its row group, clusters i * 16 * 1 to (i + 1) * 16 - 1.
All inputs are finite; a program needn't handle non-finite values.
Results may differ from the reference program's by a relative error of at most 0.0046.
Values may be sent and summed in bfloat16 or wider, within the bound.
A program may use at most 192 MiB of HBM per device.

```python
import jax
import jax.numpy as jnp
from jax import lax

TILE = 256
RANK = 64
NRHS = 256
CL_DEV = 1
DPC = 2
LPC = 8
NPAN = 65536
DSL = 32
LSL = 128
N_ROW = 16
N_COL = 16


def cluster_rows(key, slots):
    total = N_ROW * N_COL * slots
    place = jnp.arange(total, dtype=jnp.int32)
    device = place // slots
    group = N_COL * CL_DEV
    local = jax.random.randint(key, (total,), 0, group, dtype=jnp.int32)
    within = place % slots
    local = jnp.where(within == 0, group - 1, jnp.where(within == 1, 0, local))
    return (device // N_COL * group + local).astype(jnp.int32)


def draw_near_rows(key, part):
    return cluster_rows(jax.random.fold_in(key, 11), DSL)


def draw_far_rows(key, part):
    return cluster_rows(jax.random.fold_in(key, 23), LSL)


def shard_levels(own_key, extent, shards, smallest, top_value):
    gain, own = 1.0, jax.random.fold_in(own_key, 6)
    for position, blocks in shards:
        heights = jnp.exp(jax.random.uniform(jax.random.fold_in(own, position), (blocks,), jnp.float32, smallest / len(shards), top_value / len(shards)))
        gain = gain * jnp.repeat(heights, extent[position] // blocks).reshape([-1 if axis == position else 1 for axis in range(len(extent))])
    return gain


def noise(key, extent, deviation, reach, pieces=(), kind=jnp.bfloat16):
    level = shard_levels(key, extent, pieces, -0.22, 0.18) if pieces else 1.0
    result = jax.random.normal(key, extent, jnp.float32) * deviation * level
    return jnp.minimum(jnp.maximum(result, -reach), reach).astype(kind)


def setup_inputs(seed: int = 0) -> dict:
    splits = jax.random.split(jax.random.key(seed), 7)
    return {
        "panel_values": noise(splits[0], (NPAN, NRHS), 1.0, 6.0, ((0, 256),)),
        "near_tiles": noise(splits[1], (N_ROW * N_COL * DSL, TILE, TILE), (TILE * 2 * N_ROW * (DPC + LPC)) ** -0.5, 0.01953125, ((0, 256),)),
        "far_left": noise(splits[2], (N_ROW * N_COL * LSL, RANK, TILE), (RANK * 2 * N_ROW * (DPC + LPC)) ** -0.5, 0.0390625, ((0, 256),)),
        "far_right": noise(splits[3], (N_ROW * N_COL * LSL, RANK, TILE), TILE ** -0.5, 0.375, ((0, 256),)),
        "near_rows": draw_near_rows(jax.random.fold_in(splits[6], 71), 0),
        "far_rows": draw_far_rows(jax.random.fold_in(splits[6], 71), 0),
    }


def forward_terms(tiles, left, right, near_local, far_local, colx, groups):
    count = colx.shape[0]
    hp = lax.Precision.HIGHEST
    dense = tiles.reshape(count, DPC, TILE, TILE).astype(jnp.float32)
    near_out = jnp.einsum("cdij,cjn->cdin", dense, colx.astype(jnp.float32), precision=hp)
    near_out = near_out.reshape(count * DPC, TILE, NRHS)
    right_f = right.reshape(count, LPC, RANK, TILE).astype(jnp.float32)
    coef = jnp.einsum("cdkt,ctn->cdkn", right_f, colx.astype(jnp.float32), precision=hp).astype(jnp.bfloat16)
    coef = lax.optimization_barrier(coef)
    left_f = left.reshape(count, LPC, RANK, TILE).astype(jnp.float32)
    far_out = jnp.einsum("cdkt,cdkn->cdtn", left_f, coef.astype(jnp.float32), precision=hp)
    far_out = far_out.reshape(count * LPC, TILE, NRHS)
    labels = jnp.arange(groups, dtype=jnp.int32)
    near_hot = (near_local[:, None] == labels[None, :]).astype(jnp.float32)
    far_hot = (far_local[:, None] == labels[None, :]).astype(jnp.float32)
    total = jnp.einsum("sg,stn->gtn", near_hot, near_out, precision=hp)
    total = total + jnp.einsum("sg,stn->gtn", far_hot, far_out, precision=hp)
    return total


def back_terms(tiles, left, right, near_input, far_input, count):
    hp = lax.Precision.HIGHEST
    near_out = jnp.einsum("sij,sin->sjn", tiles.astype(jnp.float32), near_input.astype(jnp.float32), precision=hp)
    near_sum = near_out.reshape(count, DPC, TILE, NRHS).sum(axis=1)
    coef = jnp.einsum("skt,stn->skn", left.astype(jnp.float32), far_input.astype(jnp.float32), precision=hp).astype(jnp.bfloat16)
    coef = lax.optimization_barrier(coef)
    far_out = jnp.einsum("skt,skn->stn", right.astype(jnp.float32), coef.astype(jnp.float32), precision=hp)
    far_sum = far_out.reshape(count, LPC, TILE, NRHS).sum(axis=1)
    return near_sum + far_sum


def reference(panel_values, near_tiles, far_left, far_right, near_rows, far_rows):
    span = CL_DEV * TILE
    grid = panel_values.reshape(N_ROW, N_COL, span, NRHS)
    groups = N_COL * CL_DEV
    colcount = N_ROW * CL_DEV
    dense_slots = DPC * CL_DEV * N_ROW
    far_slots = LPC * CL_DEV * N_ROW

    def visit(device, accum):
        device = jnp.asarray(device).astype(jnp.int32)
        row_pos = (device // N_COL).astype(jnp.int32)
        col_pos = (device % N_COL).astype(jnp.int32)
        rowx = lax.dynamic_index_in_dim(grid, row_pos, 0, keepdims=False).reshape(groups, TILE, NRHS)
        colx = lax.dynamic_index_in_dim(grid, col_pos, 1, keepdims=False).reshape(colcount, TILE, NRHS)
        tiles = lax.dynamic_slice_in_dim(near_tiles, (device * dense_slots).astype(jnp.int32), dense_slots, 0)
        left = lax.dynamic_slice_in_dim(far_left, (device * far_slots).astype(jnp.int32), far_slots, 0)
        right = lax.dynamic_slice_in_dim(far_right, (device * far_slots).astype(jnp.int32), far_slots, 0)
        base = (row_pos * groups).astype(jnp.int32)
        near_local = (lax.dynamic_slice_in_dim(near_rows, (device * dense_slots).astype(jnp.int32), dense_slots, 0) - base).astype(jnp.int32)
        far_local = (lax.dynamic_slice_in_dim(far_rows, (device * far_slots).astype(jnp.int32), far_slots, 0) - base).astype(jnp.int32)
        forward = forward_terms(tiles, left, right, near_local, far_local, colx, groups)
        near_input = jnp.take(rowx, near_local, axis=0)
        far_input = jnp.take(rowx, far_local, axis=0)
        backward = back_terms(tiles, left, right, near_input, far_input, colcount)
        row_block = lax.dynamic_index_in_dim(accum, row_pos, 0, keepdims=False) + forward.reshape(N_COL, span, NRHS)
        accum = lax.dynamic_update_index_in_dim(accum, row_block, row_pos, 0)
        col_block = lax.dynamic_index_in_dim(accum, col_pos, 1, keepdims=False) + backward.reshape(N_ROW, span, NRHS)
        accum = lax.dynamic_update_index_in_dim(accum, col_block, col_pos, 1)
        return accum

    accum = lax.fori_loop(0, N_ROW * N_COL, visit, jnp.zeros((N_ROW, N_COL, span, NRHS), jnp.float32))
    return accum.reshape(N_ROW * N_COL * span, NRHS).astype(jnp.bfloat16)
```

```python
import jax
import jax.numpy as jnp
from jax import lax
from jax.experimental import pallas as pl
from jax.experimental.pallas import tpu as pltpu
from jax.sharding import PartitionSpec as P

TILE = 256
RANK = 64
NRHS = 256
DPC = 2
LPC = 8

TN = (((0,), (0,)), ((), ()))


def local_kernel(near_idx, far_idx, tiles_ref, left_ref, right_ref, colx_ref, rowx_ref, f_ref, b_ref):
    k = pl.program_id(0)

    @pl.when(k == 0)
    def _():
        f_ref[...] = jnp.zeros_like(f_ref)

    xc = colx_ref[0]
    acc = jnp.zeros((TILE, NRHS), jnp.float32)
    for d in range(DPC):
        r = near_idx[k * DPC + d]
        t = tiles_ref[d]
        f_ref[r] += jnp.dot(t, xc, preferred_element_type=jnp.float32)
        acc += lax.dot_general(t, rowx_ref[r], TN, preferred_element_type=jnp.float32)
    for d in range(LPC):
        r = far_idx[k * LPC + d]
        right = right_ref[d]
        left = left_ref[d]
        coef = jnp.dot(right, xc, preferred_element_type=jnp.float32).astype(jnp.bfloat16)
        f_ref[r] += lax.dot_general(left, coef, TN, preferred_element_type=jnp.float32)
        tcoef = jnp.dot(left, rowx_ref[r], preferred_element_type=jnp.float32).astype(jnp.bfloat16)
        acc += lax.dot_general(right, tcoef, TN, preferred_element_type=jnp.float32)
    b_ref[0] = acc


def local_products(near_local, far_local, near_tiles, far_left, far_right, colx, rowx):
    count = colx.shape[0]
    groups = rowx.shape[0]
    grid_spec = pltpu.PrefetchScalarGridSpec(
        num_scalar_prefetch=2,
        grid=(count,),
        in_specs=[
            pl.BlockSpec((DPC, TILE, TILE), lambda k, a, b: (k, 0, 0)),
            pl.BlockSpec((LPC, RANK, TILE), lambda k, a, b: (k, 0, 0)),
            pl.BlockSpec((LPC, RANK, TILE), lambda k, a, b: (k, 0, 0)),
            pl.BlockSpec((1, TILE, NRHS), lambda k, a, b: (k, 0, 0)),
            pl.BlockSpec((groups, TILE, NRHS), lambda k, a, b: (0, 0, 0)),
        ],
        out_specs=[
            pl.BlockSpec((groups, TILE, NRHS), lambda k, a, b: (0, 0, 0)),
            pl.BlockSpec((1, TILE, NRHS), lambda k, a, b: (k, 0, 0)),
        ],
    )
    flops = 2 * TILE * TILE * NRHS * near_tiles.shape[0] * 2 + 2 * RANK * TILE * NRHS * far_left.shape[0] * 4
    return pl.pallas_call(
        local_kernel,
        grid_spec=grid_spec,
        out_shape=[
            jax.ShapeDtypeStruct((groups, TILE, NRHS), jnp.float32),
            jax.ShapeDtypeStruct((count, TILE, NRHS), jnp.float32),
        ],
        compiler_params=pltpu.CompilerParams(
            dimension_semantics=("arbitrary",), vmem_limit_bytes=48 * 1024 * 1024
        ),
        cost_estimate=pl.CostEstimate(flops=flops, bytes_accessed=24 * 1024 * 1024, transcendentals=0),
    )(near_local, far_local, near_tiles, far_left, far_right, colx, rowx)


def per_device(panel_values, near_tiles, far_left, far_right, near_rows, far_rows):
    n_row = lax.axis_size("row")
    n_col = lax.axis_size("col")
    clusters = panel_values.shape[0] // TILE
    groups = n_col * clusters
    colcount = n_row * clusters
    row_base = lax.axis_index("row") * groups
    near_local = near_rows - row_base
    far_local = far_rows - row_base
    row_slab = lax.all_gather(panel_values, "col", axis=0, tiled=True)
    rowx = row_slab.reshape(groups, TILE, NRHS)
    col_slab = lax.all_gather(panel_values, "row", axis=0, tiled=True)
    colx = col_slab.reshape(colcount, TILE, NRHS)
    forward, backward = local_products(near_local, far_local, near_tiles, far_left, far_right, colx, rowx)
    own_back = lax.psum_scatter(backward.reshape(colcount * TILE, NRHS), "row", scatter_dimension=0, tiled=True)
    own_forward = lax.psum_scatter(forward.reshape(groups * TILE, NRHS), "col", scatter_dimension=0, tiled=True)
    return (own_forward + own_back).astype(jnp.bfloat16)


def solution(mesh):
    placed = (
        P(("row", "col"), None),
        P(("row", "col"), None, None),
        P(("row", "col"), None, None),
        P(("row", "col"), None, None),
        P(("row", "col")),
        P(("row", "col")),
    )
    return jax.shard_map(
        per_device, mesh=mesh, in_specs=placed, out_specs=P(("row", "col"), None), check_vma=False
    )
```

```python
import functools

import jax
import jax.numpy as jnp
from jax import lax
from jax.experimental import pallas as pl
from jax.experimental.pallas import tpu as pltpu
from jax.sharding import PartitionSpec as P

TILE = 256
RANK = 64
NRHS = 256
DPC = 2
LPC = 8

TN = (((0,), (0,)), ((), ()))


def local_kernel(near_idx, far_idx, tiles_ref, left_ref, right_ref, colx_ref, rowx_ref, f_ref, b_ref):
    k = pl.program_id(0)

    @pl.when(k == 0)
    def _():
        f_ref[...] = jnp.zeros_like(f_ref)

    xc = colx_ref[0]
    acc = jnp.zeros((TILE, NRHS), jnp.float32)
    for d in range(DPC):
        r = near_idx[k * DPC + d]
        t = tiles_ref[d]
        f_ref[r] += jnp.dot(t, xc, preferred_element_type=jnp.float32)
        acc += lax.dot_general(t, rowx_ref[r], TN, preferred_element_type=jnp.float32)
    for d in range(LPC):
        r = far_idx[k * LPC + d]
        right = right_ref[d]
        left = left_ref[d]
        coef = jnp.dot(right, xc, preferred_element_type=jnp.float32).astype(jnp.bfloat16)
        f_ref[r] += lax.dot_general(left, coef, TN, preferred_element_type=jnp.float32)
        tcoef = jnp.dot(left, rowx_ref[r], preferred_element_type=jnp.float32).astype(jnp.bfloat16)
        acc += lax.dot_general(right, tcoef, TN, preferred_element_type=jnp.float32)
    b_ref[0] = acc


def local_products(near_local, far_local, near_tiles, far_left, far_right, colx, rowx):
    count = colx.shape[0]
    groups = rowx.shape[0]
    grid_spec = pltpu.PrefetchScalarGridSpec(
        num_scalar_prefetch=2,
        grid=(count,),
        in_specs=[
            pl.BlockSpec((DPC, TILE, TILE), lambda k, a, b: (k, 0, 0)),
            pl.BlockSpec((LPC, RANK, TILE), lambda k, a, b: (k, 0, 0)),
            pl.BlockSpec((LPC, RANK, TILE), lambda k, a, b: (k, 0, 0)),
            pl.BlockSpec((1, TILE, NRHS), lambda k, a, b: (k, 0, 0)),
            pl.BlockSpec((groups, TILE, NRHS), lambda k, a, b: (0, 0, 0)),
        ],
        out_specs=[
            pl.BlockSpec((groups, TILE, NRHS), lambda k, a, b: (0, 0, 0)),
            pl.BlockSpec((1, TILE, NRHS), lambda k, a, b: (k, 0, 0)),
        ],
    )
    flops = 2 * TILE * TILE * NRHS * near_tiles.shape[0] * 2 + 2 * RANK * TILE * NRHS * far_left.shape[0] * 4
    return pl.pallas_call(
        local_kernel,
        grid_spec=grid_spec,
        out_shape=[
            jax.ShapeDtypeStruct((groups, TILE, NRHS), jnp.float32),
            jax.ShapeDtypeStruct((count, TILE, NRHS), jnp.float32),
        ],
        compiler_params=pltpu.CompilerParams(
            dimension_semantics=("arbitrary",), vmem_limit_bytes=48 * 1024 * 1024
        ),
        cost_estimate=pl.CostEstimate(flops=flops, bytes_accessed=24 * 1024 * 1024, transcendentals=0),
    )(near_local, far_local, near_tiles, far_left, far_right, colx, rowx)


MESH_ID = pl.DeviceIdType.MESH


def peers(nr, nc):
    i = lax.axis_index("row")
    j = lax.axis_index("col")
    cols = [(i, lax.rem(j + o, nc)) for o in range(1, nc)]
    rows = [(lax.rem(i + o, nr), j) for o in range(1, nr)]
    return i, j, cols, rows


def enter(cols, rows):
    barrier = pltpu.get_barrier_semaphore()
    for dev in cols + rows:
        pl.semaphore_signal(barrier, 1, device_id=dev, device_id_type=MESH_ID)
    pl.semaphore_wait(barrier, len(cols) + len(rows))


def gather_kernel(nr, nc, x_ref, rowx_ref, colx_ref, send_sem, recv_sem, local_sem):
    i, j, cols, rows = peers(nr, nc)
    enter(cols, rows)
    copies = []
    for n, dev in enumerate(cols):
        copies.append(pltpu.make_async_remote_copy(
            x_ref, rowx_ref.at[j], send_sem.at[n], recv_sem.at[n], device_id=dev, device_id_type=MESH_ID))
    for n, dev in enumerate(rows):
        q = len(cols) + n
        copies.append(pltpu.make_async_remote_copy(
            x_ref, colx_ref.at[i], send_sem.at[q], recv_sem.at[q], device_id=dev, device_id_type=MESH_ID))
    for c in copies:
        c.start()
    own_row = pltpu.make_async_copy(x_ref, rowx_ref.at[j], local_sem.at[0])
    own_col = pltpu.make_async_copy(x_ref, colx_ref.at[i], local_sem.at[1])
    own_row.start()
    own_col.start()
    for c in copies:
        c.wait()
    own_row.wait()
    own_col.wait()


def gather_slabs(x, nr, nc):
    tile = x.shape
    peers_n = nr + nc - 2
    return pl.pallas_call(
        functools.partial(gather_kernel, nr, nc),
        out_shape=[
            jax.ShapeDtypeStruct((nc,) + tile, x.dtype),
            jax.ShapeDtypeStruct((nr,) + tile, x.dtype),
        ],
        in_specs=[pl.BlockSpec(memory_space=pl.ANY)],
        out_specs=[pl.BlockSpec(memory_space=pl.ANY)] * 2,
        scratch_shapes=[
            pltpu.SemaphoreType.DMA((peers_n,)),
            pltpu.SemaphoreType.DMA((peers_n,)),
            pltpu.SemaphoreType.DMA((2,)),
        ],
        compiler_params=pltpu.CompilerParams(collective_id=0, has_side_effects=True),
    )(x)


def scatter_kernel(nr, nc, f_ref, b_ref, out_ref, recv_f, recv_b, send_sem, recv_sem, local_sem):
    i, j, cols, rows = peers(nr, nc)
    enter(cols, rows)
    copies = []
    for n, dev in enumerate(cols):
        copies.append(pltpu.make_async_remote_copy(
            f_ref.at[dev[1]], recv_f.at[n + 1], send_sem.at[n], recv_sem.at[n],
            device_id=dev, device_id_type=MESH_ID))
    for n, dev in enumerate(rows):
        q = len(cols) + n
        copies.append(pltpu.make_async_remote_copy(
            b_ref.at[dev[0]], recv_b.at[n + 1], send_sem.at[q], recv_sem.at[q],
            device_id=dev, device_id_type=MESH_ID))
    for c in copies:
        c.start()
    own_f = pltpu.make_async_copy(f_ref.at[j], recv_f.at[0], local_sem.at[0])
    own_b = pltpu.make_async_copy(b_ref.at[i], recv_b.at[0], local_sem.at[1])
    own_f.start()
    own_b.start()
    for c in copies:
        c.wait()
    own_f.wait()
    own_b.wait()
    acc = recv_f[0] + recv_b[0]
    for n in range(1, nc):
        acc = acc + recv_f[n]
    for n in range(1, nr):
        acc = acc + recv_b[n]
    out_ref[...] = acc.astype(out_ref.dtype)


def scatter_sum(forward, backward, nr, nc):
    tile = forward.shape[1:]
    peers_n = nr + nc - 2
    return pl.pallas_call(
        functools.partial(scatter_kernel, nr, nc),
        out_shape=jax.ShapeDtypeStruct(tile, jnp.bfloat16),
        in_specs=[pl.BlockSpec(memory_space=pl.ANY)] * 2,
        out_specs=pl.BlockSpec(memory_space=pltpu.VMEM),
        scratch_shapes=[
            pltpu.VMEM((nc,) + tile, jnp.float32),
            pltpu.VMEM((nr,) + tile, jnp.float32),
            pltpu.SemaphoreType.DMA((peers_n,)),
            pltpu.SemaphoreType.DMA((peers_n,)),
            pltpu.SemaphoreType.DMA((2,)),
        ],
        compiler_params=pltpu.CompilerParams(
            collective_id=1, has_side_effects=True, vmem_limit_bytes=32 * 1024 * 1024),
    )(forward, backward)


def per_device(panel_values, near_tiles, far_left, far_right, near_rows, far_rows):
    n_row = lax.axis_size("row")
    n_col = lax.axis_size("col")
    clusters = panel_values.shape[0] // TILE
    groups = n_col * clusters
    colcount = n_row * clusters
    row_base = lax.axis_index("row") * groups
    near_local = near_rows - row_base
    far_local = far_rows - row_base
    rowx, colx = gather_slabs(panel_values, n_row, n_col)
    forward, backward = local_products(near_local, far_local, near_tiles, far_left, far_right, colx, rowx)
    return scatter_sum(forward, backward, n_row, n_col)


def solution(mesh):
    placed = (
        P(("row", "col"), None),
        P(("row", "col"), None, None),
        P(("row", "col"), None, None),
        P(("row", "col"), None, None),
        P(("row", "col")),
        P(("row", "col")),
    )
    return jax.shard_map(
        per_device, mesh=mesh, in_specs=placed, out_specs=P(("row", "col"), None), check_vma=False
    )
```

```python
import functools

import jax
import jax.numpy as jnp
from jax import lax
from jax.experimental import pallas as pl
from jax.experimental.pallas import tpu as pltpu
from jax.sharding import PartitionSpec as P

TILE = 256
RANK = 64
NRHS = 256
DPC = 2
LPC = 8

TN = (((0,), (0,)), ((), ()))


def local_kernel(near_idx, far_idx, tiles_ref, left_ref, right_ref, colx_ref, rowx_ref, f_ref, b_ref):
    k = pl.program_id(0)

    @pl.when(k == 0)
    def _():
        f_ref[...] = jnp.zeros_like(f_ref)

    xc = colx_ref[0]
    acc = jnp.zeros((TILE, NRHS), jnp.float32)
    for d in range(DPC):
        r = near_idx[k * DPC + d]
        t = tiles_ref[d]
        f_ref[r] += jnp.dot(t, xc, preferred_element_type=jnp.float32)
        acc += lax.dot_general(t, rowx_ref[r], TN, preferred_element_type=jnp.float32)
    for d in range(LPC):
        r = far_idx[k * LPC + d]
        right = right_ref[d]
        left = left_ref[d]
        coef = jnp.dot(right, xc, preferred_element_type=jnp.float32).astype(jnp.bfloat16)
        f_ref[r] += lax.dot_general(left, coef, TN, preferred_element_type=jnp.float32)
        tcoef = jnp.dot(left, rowx_ref[r], preferred_element_type=jnp.float32).astype(jnp.bfloat16)
        acc += lax.dot_general(right, tcoef, TN, preferred_element_type=jnp.float32)
    b_ref[0] = acc


def local_products(near_local, far_local, near_tiles, far_left, far_right, colx, rowx):
    count = colx.shape[0]
    groups = rowx.shape[0]
    grid_spec = pltpu.PrefetchScalarGridSpec(
        num_scalar_prefetch=2,
        grid=(count,),
        in_specs=[
            pl.BlockSpec((DPC, TILE, TILE), lambda k, a, b: (k, 0, 0)),
            pl.BlockSpec((LPC, RANK, TILE), lambda k, a, b: (k, 0, 0)),
            pl.BlockSpec((LPC, RANK, TILE), lambda k, a, b: (k, 0, 0)),
            pl.BlockSpec((1, TILE, NRHS), lambda k, a, b: (k, 0, 0)),
            pl.BlockSpec((groups, TILE, NRHS), lambda k, a, b: (0, 0, 0)),
        ],
        out_specs=[
            pl.BlockSpec((groups, TILE, NRHS), lambda k, a, b: (0, 0, 0)),
            pl.BlockSpec((1, TILE, NRHS), lambda k, a, b: (k, 0, 0)),
        ],
    )
    flops = 2 * TILE * TILE * NRHS * near_tiles.shape[0] * 2 + 2 * RANK * TILE * NRHS * far_left.shape[0] * 4
    return pl.pallas_call(
        local_kernel,
        grid_spec=grid_spec,
        out_shape=[
            jax.ShapeDtypeStruct((groups, TILE, NRHS), jnp.float32),
            jax.ShapeDtypeStruct((count, TILE, NRHS), jnp.float32),
        ],
        compiler_params=pltpu.CompilerParams(
            dimension_semantics=("arbitrary",), vmem_limit_bytes=48 * 1024 * 1024
        ),
        cost_estimate=pl.CostEstimate(flops=flops, bytes_accessed=24 * 1024 * 1024, transcendentals=0),
    )(near_local, far_local, near_tiles, far_left, far_right, colx, rowx)


MESH_ID = pl.DeviceIdType.MESH


def layout(nr, nc):
    i = lax.axis_index("row")
    j = lax.axis_index("col")
    half = nr // 2
    xh = i // half
    z = lax.rem(i, half)
    cols = [(i, lax.rem(j + o, nc)) for o in range(1, nc)]
    right = (xh * half + lax.rem(z + 1, half), j)
    left = (xh * half + lax.rem(z + half - 1, half), j)
    partner = (lax.rem(i + half, nr), j)
    return i, j, half, xh, z, cols, right, left, partner


def enter(devices):
    barrier = pltpu.get_barrier_semaphore()
    for dev in devices:
        pl.semaphore_signal(barrier, 1, device_id=dev, device_id_type=MESH_ID)
    pl.semaphore_wait(barrier, len(devices))


def remote(src, dst, ssem, rsem, dev):
    return pltpu.make_async_remote_copy(src, dst, ssem, rsem, device_id=dev, device_id_type=MESH_ID)


def gather_kernel(nr, nc, x_ref, rowx_ref, colx_ref, col_send, col_recv, ring_send, ring_recv, local_sem):
    i, j, half, xh, z, cols, right, left, partner = layout(nr, nc)
    cw = half // 2
    ccw = half - 1 - cw
    enter(cols + [right, left, partner])
    col_copies = [remote(x_ref, rowx_ref.at[j], col_send.at[n], col_recv.at[n], dev) for n, dev in enumerate(cols)]
    for c in col_copies:
        c.start()
    other = remote(x_ref, colx_ref.at[xh, z], ring_send.at[0], ring_recv.at[0], partner)
    other.start()
    own_row = pltpu.make_async_copy(x_ref, rowx_ref.at[j], local_sem.at[0])
    own_col = pltpu.make_async_copy(x_ref, colx_ref.at[xh, z], local_sem.at[1])
    own_row.start()
    own_col.start()
    own_col.wait()
    other.wait()
    ring = []
    prev_cw = prev_ccw = None
    for t in range(1, cw + 1):
        origin = lax.rem(z - t + 1 + half, half)
        if prev_cw is not None:
            prev_cw.wait_recv()
        c = remote(colx_ref.at[:, origin], colx_ref.at[:, origin], ring_send.at[t], ring_recv.at[t], right)
        c.start()
        ring.append(c)
        prev_cw = c
        if t <= ccw:
            origin = lax.rem(z + t - 1, half)
            if prev_ccw is not None:
                prev_ccw.wait_recv()
            c = remote(colx_ref.at[:, origin], colx_ref.at[:, origin], ring_send.at[cw + t],
                       ring_recv.at[cw + t], left)
            c.start()
            ring.append(c)
            prev_ccw = c
    for c in ring:
        c.wait_send()
    prev_cw.wait_recv()
    prev_ccw.wait_recv()
    for c in col_copies:
        c.wait()
    own_row.wait()


def gather_slabs(x, nr, nc):
    tile = x.shape
    half = nr // 2
    return pl.pallas_call(
        functools.partial(gather_kernel, nr, nc),
        out_shape=[
            jax.ShapeDtypeStruct((nc,) + tile, x.dtype),
            jax.ShapeDtypeStruct((2, half) + tile, x.dtype),
        ],
        in_specs=[pl.BlockSpec(memory_space=pl.ANY)],
        out_specs=[pl.BlockSpec(memory_space=pl.ANY)] * 2,
        scratch_shapes=[
            pltpu.SemaphoreType.DMA((nc - 1,)),
            pltpu.SemaphoreType.DMA((nc - 1,)),
            pltpu.SemaphoreType.DMA((half,)),
            pltpu.SemaphoreType.DMA((half,)),
            pltpu.SemaphoreType.DMA((2,)),
        ],
        compiler_params=pltpu.CompilerParams(collective_id=0, has_side_effects=True),
    )(x)


def scatter_kernel(nr, nc, f_ref, b_ref, out_ref, recv_f, ring_in, ring_out, x_in, x_out,
                   col_send, col_recv, ring_send, ring_recv, local_sem):
    i, j, half, xh, z, cols, right, left, partner = layout(nr, nc)
    cw = half // 2
    ccw = half - 1 - cw
    enter(cols + [right, left, partner])
    col_copies = [
        remote(f_ref.at[dev[1]], recv_f.at[n + 1], col_send.at[n], col_recv.at[n], dev) for n, dev in enumerate(cols)
    ]
    for c in col_copies:
        c.start()
    sends = []
    arrivals = {}
    for t in range(1, cw + 1):
        for way in range(2):
            if way == 1 and t > ccw:
                continue
            if way == 0:
                target = lax.rem(z + cw + 1 - t, half)
                slot, dev = t - 1, right
            else:
                target = lax.rem(z + half - (ccw + 1 - t), half)
                slot, dev = cw + t - 1, left
            if t == 1:
                src = b_ref.at[:, target]
            else:
                arrivals[(way, t - 1)].wait_recv()
                ring_out[slot] = ring_in[slot - 1] + b_ref[:, target]
                src = ring_out.at[slot]
            c = remote(src, ring_in.at[slot], ring_send.at[slot], ring_recv.at[slot], dev)
            c.start()
            sends.append(c)
            arrivals[(way, t)] = c
    arrivals[(0, cw)].wait_recv()
    arrivals[(1, ccw)].wait_recv()
    away = 1 - xh
    x_out[...] = ring_in[cw - 1, away] + ring_in[cw + ccw - 1, away] + b_ref[away, z]
    cross = remote(x_out, x_in, ring_send.at[half - 1], ring_recv.at[half - 1], partner)
    cross.start()
    for c in sends:
        c.wait_send()
    for c in col_copies:
        c.wait()
    cross.wait()
    acc = ring_in[cw - 1, xh] + ring_in[cw + ccw - 1, xh] + b_ref[xh, z] + x_in[...] + f_ref[j]
    for n in range(1, nc):
        acc = acc + recv_f[n]
    out_ref[...] = acc.astype(out_ref.dtype)


def scatter_sum(forward, backward, nr, nc):
    tile = forward.shape[1:]
    half = nr // 2
    cw = half // 2
    steps = half - 1
    vmem = pltpu.VMEM
    return pl.pallas_call(
        functools.partial(scatter_kernel, nr, nc),
        out_shape=jax.ShapeDtypeStruct(tile, jnp.bfloat16),
        in_specs=[pl.BlockSpec(memory_space=vmem)] * 2,
        out_specs=pl.BlockSpec(memory_space=vmem),
        scratch_shapes=[
            vmem((nc,) + tile, jnp.float32),
            vmem((steps, 2) + tile, jnp.float32),
            vmem((steps, 2) + tile, jnp.float32),
            vmem(tile, jnp.float32),
            vmem(tile, jnp.float32),
            pltpu.SemaphoreType.DMA((nc - 1,)),
            pltpu.SemaphoreType.DMA((nc - 1,)),
            pltpu.SemaphoreType.DMA((half,)),
            pltpu.SemaphoreType.DMA((half,)),
            pltpu.SemaphoreType.DMA((2,)),
        ],
        compiler_params=pltpu.CompilerParams(
            collective_id=1, has_side_effects=True, vmem_limit_bytes=48 * 1024 * 1024),
    )(forward, backward.reshape((2, half) + tile))


def per_device(panel_values, near_tiles, far_left, far_right, near_rows, far_rows):
    n_row = lax.axis_size("row")
    n_col = lax.axis_size("col")
    clusters = panel_values.shape[0] // TILE
    groups = n_col * clusters
    colcount = n_row * clusters
    row_base = lax.axis_index("row") * groups
    near_local = near_rows - row_base
    far_local = far_rows - row_base
    rowx, colx = gather_slabs(panel_values, n_row, n_col)
    colx = colx.reshape(colcount, TILE, NRHS)
    forward, backward = local_products(near_local, far_local, near_tiles, far_left, far_right, colx, rowx)
    return scatter_sum(forward, backward, n_row, n_col)


def solution(mesh):
    placed = (
        P(("row", "col"), None),
        P(("row", "col"), None, None),
        P(("row", "col"), None, None),
        P(("row", "col"), None, None),
        P(("row", "col")),
        P(("row", "col")),
    )
    return jax.shard_map(
        per_device, mesh=mesh, in_specs=placed, out_specs=P(("row", "col"), None), check_vma=False
    )
```

```python
import functools

import jax
import jax.numpy as jnp
from jax import lax
from jax.experimental import pallas as pl
from jax.experimental.pallas import tpu as pltpu
from jax.sharding import PartitionSpec as P

TILE = 256
RANK = 64
NRHS = 256
DPC = 2
LPC = 8

TN = (((0,), (0,)), ((), ()))


def local_kernel(near_idx, far_idx, tiles_ref, left_ref, right_ref, colx_ref, rowx_ref, f_ref, b_ref,
                 near_x, far_t):
    k = pl.program_id(0)

    @pl.when(k == 0)
    def _():
        f_ref[...] = jnp.zeros_like(f_ref)

    xc = colx_ref[0]
    tiles = tiles_ref[...].reshape(DPC * TILE, TILE)
    near_f = jnp.dot(tiles, xc, preferred_element_type=jnp.float32)
    for d in range(DPC):
        r = near_idx[k * DPC + d]
        f_ref[r] += near_f[d * TILE:(d + 1) * TILE]
        near_x[d * TILE:(d + 1) * TILE] = rowx_ref[r]
    right = right_ref[...].reshape(LPC * RANK, TILE)
    coef = jnp.dot(right, xc, preferred_element_type=jnp.float32).astype(jnp.bfloat16)
    for d in range(LPC):
        r = far_idx[k * LPC + d]
        left = left_ref[d]
        f_ref[r] += lax.dot_general(left, coef[d * RANK:(d + 1) * RANK], TN, preferred_element_type=jnp.float32)
        far_t[d * RANK:(d + 1) * RANK] = jnp.dot(
            left, rowx_ref[r], preferred_element_type=jnp.float32).astype(jnp.bfloat16)
    acc = lax.dot_general(tiles, near_x[...], TN, preferred_element_type=jnp.float32)
    acc += lax.dot_general(right, far_t[...], TN, preferred_element_type=jnp.float32)
    b_ref[0] = acc


def local_products(near_local, far_local, near_tiles, far_left, far_right, colx, rowx):
    count = colx.shape[0]
    groups = rowx.shape[0]
    grid_spec = pltpu.PrefetchScalarGridSpec(
        num_scalar_prefetch=2,
        grid=(count,),
        in_specs=[
            pl.BlockSpec((DPC, TILE, TILE), lambda k, a, b: (k, 0, 0)),
            pl.BlockSpec((LPC, RANK, TILE), lambda k, a, b: (k, 0, 0)),
            pl.BlockSpec((LPC, RANK, TILE), lambda k, a, b: (k, 0, 0)),
            pl.BlockSpec((1, TILE, NRHS), lambda k, a, b: (k, 0, 0)),
            pl.BlockSpec((groups, TILE, NRHS), lambda k, a, b: (0, 0, 0)),
        ],
        out_specs=[
            pl.BlockSpec((groups, TILE, NRHS), lambda k, a, b: (0, 0, 0)),
            pl.BlockSpec((1, TILE, NRHS), lambda k, a, b: (k, 0, 0)),
        ],
        scratch_shapes=[
            pltpu.VMEM((DPC * TILE, NRHS), jnp.bfloat16),
            pltpu.VMEM((LPC * RANK, NRHS), jnp.bfloat16),
        ],
    )
    flops = 2 * TILE * TILE * NRHS * near_tiles.shape[0] * 2 + 2 * RANK * TILE * NRHS * far_left.shape[0] * 4
    return pl.pallas_call(
        local_kernel,
        grid_spec=grid_spec,
        out_shape=[
            jax.ShapeDtypeStruct((groups, TILE, NRHS), jnp.float32),
            jax.ShapeDtypeStruct((count, TILE, NRHS), jnp.float32),
        ],
        compiler_params=pltpu.CompilerParams(
            dimension_semantics=("arbitrary",), vmem_limit_bytes=48 * 1024 * 1024
        ),
        cost_estimate=pl.CostEstimate(flops=flops, bytes_accessed=24 * 1024 * 1024, transcendentals=0),
    )(near_local, far_local, near_tiles, far_left, far_right, colx, rowx)


MESH_ID = pl.DeviceIdType.MESH


def layout(nr, nc):
    i = lax.axis_index("row")
    j = lax.axis_index("col")
    half = nr // 2
    xh = i // half
    z = lax.rem(i, half)
    cols = [(i, lax.rem(j + o, nc)) for o in range(1, nc)]
    right = (xh * half + lax.rem(z + 1, half), j)
    left = (xh * half + lax.rem(z + half - 1, half), j)
    partner = (lax.rem(i + half, nr), j)
    return i, j, half, xh, z, cols, right, left, partner


def enter(devices):
    barrier = pltpu.get_barrier_semaphore()
    for dev in devices:
        pl.semaphore_signal(barrier, 1, device_id=dev, device_id_type=MESH_ID)
    pl.semaphore_wait(barrier, len(devices))


def remote(src, dst, ssem, rsem, dev):
    return pltpu.make_async_remote_copy(src, dst, ssem, rsem, device_id=dev, device_id_type=MESH_ID)


def gather_kernel(nr, nc, x_ref, rowx_ref, colx_ref, col_send, col_recv, ring_send, ring_recv, local_sem):
    i, j, half, xh, z, cols, right, left, partner = layout(nr, nc)
    cw = half // 2
    ccw = half - 1 - cw
    enter(cols + [right, left, partner])
    col_copies = [remote(x_ref, rowx_ref.at[j], col_send.at[n], col_recv.at[n], dev) for n, dev in enumerate(cols)]
    for c in col_copies:
        c.start()
    other = remote(x_ref, colx_ref.at[xh, z], ring_send.at[0], ring_recv.at[0], partner)
    other.start()
    own_row = pltpu.make_async_copy(x_ref, rowx_ref.at[j], local_sem.at[0])
    own_col = pltpu.make_async_copy(x_ref, colx_ref.at[xh, z], local_sem.at[1])
    own_row.start()
    own_col.start()
    own_col.wait()
    other.wait()
    ring = []
    prev_cw = prev_ccw = None
    for t in range(1, cw + 1):
        origin = lax.rem(z - t + 1 + half, half)
        if prev_cw is not None:
            prev_cw.wait_recv()
        c = remote(colx_ref.at[:, origin], colx_ref.at[:, origin], ring_send.at[t], ring_recv.at[t], right)
        c.start()
        ring.append(c)
        prev_cw = c
        if t <= ccw:
            origin = lax.rem(z + t - 1, half)
            if prev_ccw is not None:
                prev_ccw.wait_recv()
            c = remote(colx_ref.at[:, origin], colx_ref.at[:, origin], ring_send.at[cw + t],
                       ring_recv.at[cw + t], left)
            c.start()
            ring.append(c)
            prev_ccw = c
    for c in ring:
        c.wait_send()
    prev_cw.wait_recv()
    prev_ccw.wait_recv()
    for c in col_copies:
        c.wait()
    own_row.wait()


def gather_slabs(x, nr, nc):
    tile = x.shape
    half = nr // 2
    return pl.pallas_call(
        functools.partial(gather_kernel, nr, nc),
        out_shape=[
            jax.ShapeDtypeStruct((nc,) + tile, x.dtype),
            jax.ShapeDtypeStruct((2, half) + tile, x.dtype),
        ],
        in_specs=[pl.BlockSpec(memory_space=pl.ANY)],
        out_specs=[pl.BlockSpec(memory_space=pl.ANY)] * 2,
        scratch_shapes=[
            pltpu.SemaphoreType.DMA((nc - 1,)),
            pltpu.SemaphoreType.DMA((nc - 1,)),
            pltpu.SemaphoreType.DMA((half,)),
            pltpu.SemaphoreType.DMA((half,)),
            pltpu.SemaphoreType.DMA((2,)),
        ],
        compiler_params=pltpu.CompilerParams(collective_id=0, has_side_effects=True),
    )(x)


def scatter_kernel(nr, nc, f_ref, b_ref, out_ref, recv_f, ring_in, ring_out, x_in, x_out,
                   col_send, col_recv, ring_send, ring_recv, local_sem):
    i, j, half, xh, z, cols, right, left, partner = layout(nr, nc)
    cw = half // 2
    ccw = half - 1 - cw
    enter(cols + [right, left, partner])
    col_copies = [
        remote(f_ref.at[dev[1]], recv_f.at[n + 1], col_send.at[n], col_recv.at[n], dev) for n, dev in enumerate(cols)
    ]
    for c in col_copies:
        c.start()
    sends = []
    arrivals = {}
    for t in range(1, cw + 1):
        for way in range(2):
            if way == 1 and t > ccw:
                continue
            if way == 0:
                target = lax.rem(z + cw + 1 - t, half)
                slot, dev = t - 1, right
            else:
                target = lax.rem(z + half - (ccw + 1 - t), half)
                slot, dev = cw + t - 1, left
            if t == 1:
                src = b_ref.at[:, target]
            else:
                arrivals[(way, t - 1)].wait_recv()
                ring_out[slot] = ring_in[slot - 1] + b_ref[:, target]
                src = ring_out.at[slot]
            c = remote(src, ring_in.at[slot], ring_send.at[slot], ring_recv.at[slot], dev)
            c.start()
            sends.append(c)
            arrivals[(way, t)] = c
    arrivals[(0, cw)].wait_recv()
    arrivals[(1, ccw)].wait_recv()
    away = 1 - xh
    x_out[...] = ring_in[cw - 1, away] + ring_in[cw + ccw - 1, away] + b_ref[away, z]
    cross = remote(x_out, x_in, ring_send.at[half - 1], ring_recv.at[half - 1], partner)
    cross.start()
    for c in sends:
        c.wait_send()
    for c in col_copies:
        c.wait()
    cross.wait()
    acc = ring_in[cw - 1, xh] + ring_in[cw + ccw - 1, xh] + b_ref[xh, z] + x_in[...] + f_ref[j]
    for n in range(1, nc):
        acc = acc + recv_f[n]
    out_ref[...] = acc.astype(out_ref.dtype)


def scatter_sum(forward, backward, nr, nc):
    tile = forward.shape[1:]
    half = nr // 2
    cw = half // 2
    steps = half - 1
    vmem = pltpu.VMEM
    return pl.pallas_call(
        functools.partial(scatter_kernel, nr, nc),
        out_shape=jax.ShapeDtypeStruct(tile, jnp.bfloat16),
        in_specs=[pl.BlockSpec(memory_space=vmem)] * 2,
        out_specs=pl.BlockSpec(memory_space=vmem),
        scratch_shapes=[
            vmem((nc,) + tile, jnp.float32),
            vmem((steps, 2) + tile, jnp.float32),
            vmem((steps, 2) + tile, jnp.float32),
            vmem(tile, jnp.float32),
            vmem(tile, jnp.float32),
            pltpu.SemaphoreType.DMA((nc - 1,)),
            pltpu.SemaphoreType.DMA((nc - 1,)),
            pltpu.SemaphoreType.DMA((half,)),
            pltpu.SemaphoreType.DMA((half,)),
            pltpu.SemaphoreType.DMA((2,)),
        ],
        compiler_params=pltpu.CompilerParams(
            collective_id=1, has_side_effects=True, vmem_limit_bytes=48 * 1024 * 1024),
    )(forward, backward.reshape((2, half) + tile))


def per_device(panel_values, near_tiles, far_left, far_right, near_rows, far_rows):
    n_row = lax.axis_size("row")
    n_col = lax.axis_size("col")
    clusters = panel_values.shape[0] // TILE
    groups = n_col * clusters
    colcount = n_row * clusters
    row_base = lax.axis_index("row") * groups
    near_local = near_rows - row_base
    far_local = far_rows - row_base
    rowx, colx = gather_slabs(panel_values, n_row, n_col)
    colx = colx.reshape(colcount, TILE, NRHS)
    forward, backward = local_products(near_local, far_local, near_tiles, far_left, far_right, colx, rowx)
    return scatter_sum(forward, backward, n_row, n_col)


def solution(mesh):
    placed = (
        P(("row", "col"), None),
        P(("row", "col"), None, None),
        P(("row", "col"), None, None),
        P(("row", "col"), None, None),
        P(("row", "col")),
        P(("row", "col")),
    )
    return jax.shard_map(
        per_device, mesh=mesh, in_specs=placed, out_specs=P(("row", "col"), None), check_vma=False
    )
```

```python
import functools

import jax
import jax.numpy as jnp
from jax import lax
from jax.experimental import pallas as pl
from jax.experimental.pallas import tpu as pltpu
from jax.sharding import PartitionSpec as P

TILE = 256
RANK = 64
NRHS = 256
DPC = 2
LPC = 8

TN = (((0,), (0,)), ((), ()))


def local_kernel(near_idx, far_idx, tiles_ref, left_ref, right_ref, colx_ref, rowx_ref, f_ref, b_ref,
                 near_x, far_t):
    k = pl.program_id(0)

    @pl.when(k == 0)
    def _():
        f_ref[...] = jnp.zeros_like(f_ref)

    xc = colx_ref[0]
    tiles = tiles_ref[...].reshape(DPC * TILE, TILE)
    near_f = jnp.dot(tiles, xc, preferred_element_type=jnp.float32)
    for d in range(DPC):
        r = near_idx[k * DPC + d]
        f_ref[r] += near_f[d * TILE:(d + 1) * TILE]
        near_x[d * TILE:(d + 1) * TILE] = rowx_ref[r]
    right = right_ref[...].reshape(LPC * RANK, TILE)
    coef = jnp.dot(right, xc, preferred_element_type=jnp.float32).astype(jnp.bfloat16)
    for d in range(LPC):
        r = far_idx[k * LPC + d]
        left = left_ref[d]
        f_ref[r] += lax.dot_general(left, coef[d * RANK:(d + 1) * RANK], TN, preferred_element_type=jnp.float32)
        far_t[d * RANK:(d + 1) * RANK] = jnp.dot(
            left, rowx_ref[r], preferred_element_type=jnp.float32).astype(jnp.bfloat16)
    acc = lax.dot_general(tiles, near_x[...], TN, preferred_element_type=jnp.float32)
    acc += lax.dot_general(right, far_t[...], TN, preferred_element_type=jnp.float32)
    b_ref[0] = acc


def local_products(near_local, far_local, near_tiles, far_left, far_right, colx, rowx):
    count = colx.shape[0]
    groups = rowx.shape[0]
    grid_spec = pltpu.PrefetchScalarGridSpec(
        num_scalar_prefetch=2,
        grid=(count,),
        in_specs=[
            pl.BlockSpec((DPC, TILE, TILE), lambda k, a, b: (k, 0, 0)),
            pl.BlockSpec((LPC, RANK, TILE), lambda k, a, b: (k, 0, 0)),
            pl.BlockSpec((LPC, RANK, TILE), lambda k, a, b: (k, 0, 0)),
            pl.BlockSpec((1, TILE, NRHS), lambda k, a, b: (k, 0, 0)),
            pl.BlockSpec((groups, TILE, NRHS), lambda k, a, b: (0, 0, 0)),
        ],
        out_specs=[
            pl.BlockSpec((groups, TILE, NRHS), lambda k, a, b: (0, 0, 0)),
            pl.BlockSpec((1, TILE, NRHS), lambda k, a, b: (k, 0, 0)),
        ],
        scratch_shapes=[
            pltpu.VMEM((DPC * TILE, NRHS), jnp.bfloat16),
            pltpu.VMEM((LPC * RANK, NRHS), jnp.bfloat16),
        ],
    )
    flops = 2 * TILE * TILE * NRHS * near_tiles.shape[0] * 2 + 2 * RANK * TILE * NRHS * far_left.shape[0] * 4
    return pl.pallas_call(
        local_kernel,
        grid_spec=grid_spec,
        out_shape=[
            jax.ShapeDtypeStruct((groups, TILE, NRHS), jnp.float32),
            jax.ShapeDtypeStruct((count, TILE, NRHS), jnp.float32),
        ],
        compiler_params=pltpu.CompilerParams(
            dimension_semantics=("arbitrary",), vmem_limit_bytes=48 * 1024 * 1024
        ),
        cost_estimate=pl.CostEstimate(flops=flops, bytes_accessed=24 * 1024 * 1024, transcendentals=0),
    )(near_local, far_local, near_tiles, far_left, far_right, colx, rowx)


MESH_ID = pl.DeviceIdType.MESH


def layout(nr, nc):
    i = lax.axis_index("row")
    j = lax.axis_index("col")
    half = nr // 2
    xh = i // half
    z = lax.rem(i, half)
    chips = nc // 2
    core = lax.rem(j, 2)
    chip = j // 2
    cols = [(i, 2 * lax.rem(chip + o, chips) + core) for o in range(1, chips)]
    cols.append((i, 2 * chip + 1 - core))
    right = (xh * half + lax.rem(z + 1, half), j)
    left = (xh * half + lax.rem(z + half - 1, half), j)
    partner = (lax.rem(i + half, nr), j)
    return i, j, half, xh, z, cols, right, left, partner


def enter(devices):
    barrier = pltpu.get_barrier_semaphore()
    for dev in devices:
        pl.semaphore_signal(barrier, 1, device_id=dev, device_id_type=MESH_ID)
    pl.semaphore_wait(barrier, len(devices))


def remote(src, dst, ssem, rsem, dev):
    return pltpu.make_async_remote_copy(src, dst, ssem, rsem, device_id=dev, device_id_type=MESH_ID)


def gather_kernel(nr, nc, x_ref, rowx_ref, colx_ref, col_send, col_recv, ring_send, ring_recv, local_sem):
    i, j, half, xh, z, cols, right, left, partner = layout(nr, nc)
    cw = half // 2
    ccw = half - 1 - cw
    enter(cols + [right, left, partner])
    chips = nc // 2
    core = lax.rem(j, 2)
    chip = j // 2
    col_copies = [remote(x_ref, rowx_ref.at[j], col_send.at[n], col_recv.at[n], dev) for n, dev in enumerate(cols)]
    for c in col_copies:
        c.start()
    other = remote(x_ref, colx_ref.at[xh, z], ring_send.at[0], ring_recv.at[0], partner)
    other.start()
    own_row = pltpu.make_async_copy(x_ref, rowx_ref.at[j], local_sem.at[0])
    own_col = pltpu.make_async_copy(x_ref, colx_ref.at[xh, z], local_sem.at[1])
    own_row.start()
    own_col.start()
    own_col.wait()
    other.wait()
    ring = []
    prev_cw = prev_ccw = None
    for t in range(1, cw + 1):
        origin = lax.rem(z - t + 1 + half, half)
        if prev_cw is not None:
            prev_cw.wait_recv()
        c = remote(colx_ref.at[:, origin], colx_ref.at[:, origin], ring_send.at[t], ring_recv.at[t], right)
        c.start()
        ring.append(c)
        prev_cw = c
        if t <= ccw:
            origin = lax.rem(z + t - 1, half)
            if prev_ccw is not None:
                prev_ccw.wait_recv()
            c = remote(colx_ref.at[:, origin], colx_ref.at[:, origin], ring_send.at[cw + t],
                       ring_recv.at[cw + t], left)
            c.start()
            ring.append(c)
            prev_ccw = c
    for c in ring:
        c.wait_send()
    prev_cw.wait_recv()
    prev_ccw.wait_recv()
    mate = cols[-1]
    for o in range(1, chips):
        origin = 2 * lax.rem(chip + chips - o, chips) + core
        col_copies[o - 1].wait_recv()
        c = remote(rowx_ref.at[origin], rowx_ref.at[origin], col_send.at[chips + o - 1],
                   col_recv.at[chips + o - 1], mate)
        c.start()
        col_copies.append(c)
    for c in col_copies:
        c.wait_send()
    for c in col_copies[chips - 1:]:
        c.wait_recv()
    own_row.wait()


def gather_slabs(x, nr, nc):
    tile = x.shape
    half = nr // 2
    return pl.pallas_call(
        functools.partial(gather_kernel, nr, nc),
        out_shape=[
            jax.ShapeDtypeStruct((nc,) + tile, x.dtype),
            jax.ShapeDtypeStruct((2, half) + tile, x.dtype),
        ],
        in_specs=[pl.BlockSpec(memory_space=pl.ANY)],
        out_specs=[pl.BlockSpec(memory_space=pl.ANY)] * 2,
        scratch_shapes=[
            pltpu.SemaphoreType.DMA((nc - 1,)),
            pltpu.SemaphoreType.DMA((nc - 1,)),
            pltpu.SemaphoreType.DMA((half,)),
            pltpu.SemaphoreType.DMA((half,)),
            pltpu.SemaphoreType.DMA((2,)),
        ],
        compiler_params=pltpu.CompilerParams(collective_id=0, has_side_effects=True),
    )(x)


def scatter_kernel(nr, nc, f_ref, b_ref, out_ref, recv_f, pre, stage, ring_in, ring_out, x_in, x_out,
                   col_send, col_recv, ring_send, ring_recv, local_sem):
    i, j, half, xh, z, cols, right, left, partner = layout(nr, nc)
    cw = half // 2
    ccw = half - 1 - cw
    enter(cols + [right, left, partner])
    chips = nc // 2
    core = lax.rem(j, 2)
    chip = j // 2
    mate = cols[-1]
    handed = [2 * lax.rem(chip + o, chips) + 1 - core for o in range(1, chips)] + [mate[1]]
    col_copies = [remote(f_ref.at[m], pre.at[n], col_send.at[n], col_recv.at[n], mate) for n, m in enumerate(handed)]
    for c in col_copies:
        c.start()
    sends = []
    arrivals = {}
    for t in range(1, cw + 1):
        for way in range(2):
            if way == 1 and t > ccw:
                continue
            if way == 0:
                target = lax.rem(z + cw + 1 - t, half)
                slot, dev = t - 1, right
            else:
                target = lax.rem(z + half - (ccw + 1 - t), half)
                slot, dev = cw + t - 1, left
            if t == 1:
                src = b_ref.at[:, target]
            else:
                arrivals[(way, t - 1)].wait_recv()
                ring_out[slot] = ring_in[slot - 1] + b_ref[:, target]
                src = ring_out.at[slot]
            c = remote(src, ring_in.at[slot], ring_send.at[slot], ring_recv.at[slot], dev)
            c.start()
            sends.append(c)
            arrivals[(way, t)] = c
    for c in col_copies:
        c.wait_recv()
    for o in range(1, chips):
        dev = cols[o - 1]
        stage[o - 1] = f_ref[dev[1]] + pre[o - 1]
        c = remote(stage.at[o - 1], recv_f.at[o - 1], col_send.at[chips + o - 1], col_recv.at[chips + o - 1], dev)
        c.start()
        col_copies.append(c)
    arrivals[(0, cw)].wait_recv()
    arrivals[(1, ccw)].wait_recv()
    away = 1 - xh
    x_out[...] = ring_in[cw - 1, away] + ring_in[cw + ccw - 1, away] + b_ref[away, z]
    cross = remote(x_out, x_in, ring_send.at[half - 1], ring_recv.at[half - 1], partner)
    cross.start()
    for c in sends:
        c.wait_send()
    for c in col_copies:
        c.wait_send()
    for c in col_copies[chips:]:
        c.wait_recv()
    cross.wait()
    acc = ring_in[cw - 1, xh] + ring_in[cw + ccw - 1, xh] + b_ref[xh, z] + x_in[...] + f_ref[j] + pre[chips - 1]
    for n in range(chips - 1):
        acc = acc + recv_f[n]
    out_ref[...] = acc.astype(out_ref.dtype)


def scatter_sum(forward, backward, nr, nc):
    tile = forward.shape[1:]
    half = nr // 2
    cw = half // 2
    steps = half - 1
    vmem = pltpu.VMEM
    return pl.pallas_call(
        functools.partial(scatter_kernel, nr, nc),
        out_shape=jax.ShapeDtypeStruct(tile, jnp.bfloat16),
        in_specs=[pl.BlockSpec(memory_space=vmem)] * 2,
        out_specs=pl.BlockSpec(memory_space=vmem),
        scratch_shapes=[
            vmem((nc // 2 - 1,) + tile, jnp.float32),
            vmem((nc // 2,) + tile, jnp.float32),
            vmem((nc // 2 - 1,) + tile, jnp.float32),
            vmem((steps, 2) + tile, jnp.float32),
            vmem((steps, 2) + tile, jnp.float32),
            vmem(tile, jnp.float32),
            vmem(tile, jnp.float32),
            pltpu.SemaphoreType.DMA((nc - 1,)),
            pltpu.SemaphoreType.DMA((nc - 1,)),
            pltpu.SemaphoreType.DMA((half,)),
            pltpu.SemaphoreType.DMA((half,)),
            pltpu.SemaphoreType.DMA((2,)),
        ],
        compiler_params=pltpu.CompilerParams(
            collective_id=1, has_side_effects=True, vmem_limit_bytes=48 * 1024 * 1024),
    )(forward, backward.reshape((2, half) + tile))


def per_device(panel_values, near_tiles, far_left, far_right, near_rows, far_rows):
    n_row = lax.axis_size("row")
    n_col = lax.axis_size("col")
    clusters = panel_values.shape[0] // TILE
    groups = n_col * clusters
    colcount = n_row * clusters
    row_base = lax.axis_index("row") * groups
    near_local = near_rows - row_base
    far_local = far_rows - row_base
    rowx, colx = gather_slabs(panel_values, n_row, n_col)
    colx = colx.reshape(colcount, TILE, NRHS)
    forward, backward = local_products(near_local, far_local, near_tiles, far_left, far_right, colx, rowx)
    return scatter_sum(forward, backward, n_row, n_col)


def solution(mesh):
    placed = (
        P(("row", "col"), None),
        P(("row", "col"), None, None),
        P(("row", "col"), None, None),
        P(("row", "col"), None, None),
        P(("row", "col")),
        P(("row", "col")),
    )
    return jax.shard_map(
        per_device, mesh=mesh, in_specs=placed, out_specs=P(("row", "col"), None), check_vma=False
    )
```

```python
import functools

import jax
import jax.numpy as jnp
from jax import lax
from jax.experimental import pallas as pl
from jax.experimental.pallas import tpu as pltpu
from jax.sharding import PartitionSpec as P

TILE = 256
RANK = 64
NRHS = 256
DPC = 2
LPC = 8

TN = (((0,), (0,)), ((), ()))


def local_kernel(near_idx, far_idx, tiles_ref, left_ref, right_ref, colx_ref, rowx_ref, f_ref, b_ref,
                 near_x, far_t):
    k = pl.program_id(0)

    @pl.when(k == 0)
    def _():
        f_ref[...] = jnp.zeros_like(f_ref)

    xc = colx_ref[0]
    tiles = tiles_ref[...].reshape(DPC * TILE, TILE)
    near_f = jnp.dot(tiles, xc, preferred_element_type=jnp.float32)
    for d in range(DPC):
        r = near_idx[k * DPC + d]
        f_ref[r] += near_f[d * TILE:(d + 1) * TILE]
        near_x[d * TILE:(d + 1) * TILE] = rowx_ref[r]
    right = right_ref[...].reshape(LPC * RANK, TILE)
    coef = jnp.dot(right, xc, preferred_element_type=jnp.float32).astype(jnp.bfloat16)
    for d in range(LPC):
        r = far_idx[k * LPC + d]
        left = left_ref[d]
        f_ref[r] += lax.dot_general(left, coef[d * RANK:(d + 1) * RANK], TN, preferred_element_type=jnp.float32)
        far_t[d * RANK:(d + 1) * RANK] = jnp.dot(
            left, rowx_ref[r], preferred_element_type=jnp.float32).astype(jnp.bfloat16)
    acc = lax.dot_general(tiles, near_x[...], TN, preferred_element_type=jnp.float32)
    acc += lax.dot_general(right, far_t[...], TN, preferred_element_type=jnp.float32)
    b_ref[0] = acc


def local_products(near_local, far_local, near_tiles, far_left, far_right, colx, rowx):
    count = colx.shape[0]
    groups = rowx.shape[0]
    grid_spec = pltpu.PrefetchScalarGridSpec(
        num_scalar_prefetch=2,
        grid=(count,),
        in_specs=[
            pl.BlockSpec((DPC, TILE, TILE), lambda k, a, b: (k, 0, 0)),
            pl.BlockSpec((LPC, RANK, TILE), lambda k, a, b: (k, 0, 0)),
            pl.BlockSpec((LPC, RANK, TILE), lambda k, a, b: (k, 0, 0)),
            pl.BlockSpec((1, TILE, NRHS), lambda k, a, b: (k, 0, 0)),
            pl.BlockSpec((groups, TILE, NRHS), lambda k, a, b: (0, 0, 0)),
        ],
        out_specs=[
            pl.BlockSpec((groups, TILE, NRHS), lambda k, a, b: (0, 0, 0)),
            pl.BlockSpec((1, TILE, NRHS), lambda k, a, b: (k, 0, 0)),
        ],
        scratch_shapes=[
            pltpu.VMEM((DPC * TILE, NRHS), jnp.bfloat16),
            pltpu.VMEM((LPC * RANK, NRHS), jnp.bfloat16),
        ],
    )
    flops = 2 * TILE * TILE * NRHS * near_tiles.shape[0] * 2 + 2 * RANK * TILE * NRHS * far_left.shape[0] * 4
    return pl.pallas_call(
        local_kernel,
        grid_spec=grid_spec,
        out_shape=[
            jax.ShapeDtypeStruct((groups, TILE, NRHS), jnp.float32),
            jax.ShapeDtypeStruct((count, TILE, NRHS), jnp.float32),
        ],
        compiler_params=pltpu.CompilerParams(
            dimension_semantics=("arbitrary",), vmem_limit_bytes=48 * 1024 * 1024
        ),
        cost_estimate=pl.CostEstimate(flops=flops, bytes_accessed=24 * 1024 * 1024, transcendentals=0),
    )(near_local, far_local, near_tiles, far_left, far_right, colx, rowx)


MESH_ID = pl.DeviceIdType.MESH


def layout(nr, nc):
    i = lax.axis_index("row")
    j = lax.axis_index("col")
    half = nr // 2
    xh = i // half
    z = lax.rem(i, half)
    chips = nc // 2
    core = lax.rem(j, 2)
    chip = j // 2
    cols = [(i, 2 * lax.rem(chip + o, chips) + core) for o in range(1, chips)]
    cols.append((i, 2 * chip + 1 - core))
    right = (xh * half + lax.rem(z + 1, half), j)
    left = (xh * half + lax.rem(z + half - 1, half), j)
    partner = (lax.rem(i + half, nr), j)
    return i, j, half, xh, z, cols, right, left, partner


def enter(devices):
    barrier = pltpu.get_barrier_semaphore()
    for dev in devices:
        pl.semaphore_signal(barrier, 1, device_id=dev, device_id_type=MESH_ID)
    pl.semaphore_wait(barrier, len(devices))


def remote(src, dst, ssem, rsem, dev):
    return pltpu.make_async_remote_copy(src, dst, ssem, rsem, device_id=dev, device_id_type=MESH_ID)


def gather_kernel(nr, nc, x_ref, rowx_ref, colx_ref, col_send, col_recv, ring_send, ring_recv, local_sem):
    i, j, half, xh, z, cols, right, left, partner = layout(nr, nc)
    cw = half // 2
    ccw = half - 1 - cw
    enter(cols + [right, left, partner])
    chips = nc // 2
    core = lax.rem(j, 2)
    chip = j // 2
    col_copies = [remote(x_ref, rowx_ref.at[j], col_send.at[n], col_recv.at[n], dev) for n, dev in enumerate(cols)]
    for c in col_copies:
        c.start()
    other = remote(x_ref, colx_ref.at[xh, z], ring_send.at[0], ring_recv.at[0], partner)
    other.start()
    own_row = pltpu.make_async_copy(x_ref, rowx_ref.at[j], local_sem.at[0])
    own_col = pltpu.make_async_copy(x_ref, colx_ref.at[xh, z], local_sem.at[1])
    own_row.start()
    own_col.start()
    mate = cols[-1]
    ring = []
    state = {}

    def ring_step(t):
        if t == 1:
            own_col.wait()
            other.wait()
        for way in range(2):
            if way == 1 and t > ccw:
                continue
            if way == 0:
                origin = lax.rem(z - t + 1 + half, half)
                sem, dev = t, right
            else:
                origin = lax.rem(z + t - 1, half)
                sem, dev = cw + t, left
            if t > 1:
                state[way].wait_recv()
            c = remote(colx_ref.at[:, origin], colx_ref.at[:, origin], ring_send.at[sem], ring_recv.at[sem], dev)
            c.start()
            ring.append(c)
            state[way] = c

    def col_step(o):
        origin = 2 * lax.rem(chip + chips - o, chips) + core
        col_copies[o - 1].wait_recv()
        c = remote(rowx_ref.at[origin], rowx_ref.at[origin], col_send.at[chips + o - 1],
                   col_recv.at[chips + o - 1], mate)
        c.start()
        col_copies.append(c)

    for n in range(max(cw, chips - 1)):
        if n < cw:
            ring_step(n + 1)
        if n < chips - 1:
            col_step(n + 1)
    for c in ring:
        c.wait_send()
    state[0].wait_recv()
    state[1].wait_recv()
    for c in col_copies:
        c.wait_send()
    for c in col_copies[chips - 1:]:
        c.wait_recv()
    own_row.wait()


def gather_slabs(x, nr, nc):
    tile = x.shape
    half = nr // 2
    return pl.pallas_call(
        functools.partial(gather_kernel, nr, nc),
        out_shape=[
            jax.ShapeDtypeStruct((nc,) + tile, x.dtype),
            jax.ShapeDtypeStruct((2, half) + tile, x.dtype),
        ],
        in_specs=[pl.BlockSpec(memory_space=pl.ANY)],
        out_specs=[pl.BlockSpec(memory_space=pl.ANY)] * 2,
        scratch_shapes=[
            pltpu.SemaphoreType.DMA((nc - 1,)),
            pltpu.SemaphoreType.DMA((nc - 1,)),
            pltpu.SemaphoreType.DMA((half,)),
            pltpu.SemaphoreType.DMA((half,)),
            pltpu.SemaphoreType.DMA((2,)),
        ],
        compiler_params=pltpu.CompilerParams(collective_id=0, has_side_effects=True),
    )(x)


def scatter_kernel(nr, nc, f_ref, b_ref, out_ref, recv_f, pre, stage, ring_in, ring_out, x_in, x_out,
                   col_send, col_recv, ring_send, ring_recv, local_sem):
    i, j, half, xh, z, cols, right, left, partner = layout(nr, nc)
    cw = half // 2
    ccw = half - 1 - cw
    enter(cols + [right, left, partner])
    chips = nc // 2
    core = lax.rem(j, 2)
    chip = j // 2
    mate = cols[-1]
    handed = [2 * lax.rem(chip + o, chips) + 1 - core for o in range(1, chips)] + [mate[1]]
    col_copies = [remote(f_ref.at[m], pre.at[n], col_send.at[n], col_recv.at[n], mate) for n, m in enumerate(handed)]
    for c in col_copies:
        c.start()
    sends = []
    arrivals = {}

    def ring_step(t):
        for way in range(2):
            if way == 1 and t > ccw:
                continue
            if way == 0:
                target = lax.rem(z + cw + 1 - t, half)
                slot, dev = t - 1, right
            else:
                target = lax.rem(z + half - (ccw + 1 - t), half)
                slot, dev = cw + t - 1, left
            if t == 1:
                src = b_ref.at[:, target]
            else:
                arrivals[(way, t - 1)].wait_recv()
                ring_out[slot] = ring_in[slot - 1] + b_ref[:, target]
                src = ring_out.at[slot]
            c = remote(src, ring_in.at[slot], ring_send.at[slot], ring_recv.at[slot], dev)
            c.start()
            sends.append(c)
            arrivals[(way, t)] = c

    def col_step(o):
        dev = cols[o - 1]
        col_copies[o - 1].wait_recv()
        stage[o - 1] = f_ref[dev[1]] + pre[o - 1]
        c = remote(stage.at[o - 1], recv_f.at[o - 1], col_send.at[chips + o - 1], col_recv.at[chips + o - 1], dev)
        c.start()
        col_copies.append(c)

    for n in range(max(cw, chips - 1)):
        if n < cw:
            ring_step(n + 1)
        if n < chips - 1:
            col_step(n + 1)
    col_copies[chips - 1].wait_recv()
    arrivals[(0, cw)].wait_recv()
    arrivals[(1, ccw)].wait_recv()
    away = 1 - xh
    x_out[...] = ring_in[cw - 1, away] + ring_in[cw + ccw - 1, away] + b_ref[away, z]
    cross = remote(x_out, x_in, ring_send.at[half - 1], ring_recv.at[half - 1], partner)
    cross.start()
    for c in sends:
        c.wait_send()
    for c in col_copies:
        c.wait_send()
    for c in col_copies[chips:]:
        c.wait_recv()
    cross.wait()
    acc = ring_in[cw - 1, xh] + ring_in[cw + ccw - 1, xh] + b_ref[xh, z] + x_in[...] + f_ref[j] + pre[chips - 1]
    for n in range(chips - 1):
        acc = acc + recv_f[n]
    out_ref[...] = acc.astype(out_ref.dtype)


def scatter_sum(forward, backward, nr, nc):
    tile = forward.shape[1:]
    half = nr // 2
    cw = half // 2
    steps = half - 1
    vmem = pltpu.VMEM
    return pl.pallas_call(
        functools.partial(scatter_kernel, nr, nc),
        out_shape=jax.ShapeDtypeStruct(tile, jnp.bfloat16),
        in_specs=[pl.BlockSpec(memory_space=vmem)] * 2,
        out_specs=pl.BlockSpec(memory_space=vmem),
        scratch_shapes=[
            vmem((nc // 2 - 1,) + tile, jnp.float32),
            vmem((nc // 2,) + tile, jnp.float32),
            vmem((nc // 2 - 1,) + tile, jnp.float32),
            vmem((steps, 2) + tile, jnp.float32),
            vmem((steps, 2) + tile, jnp.float32),
            vmem(tile, jnp.float32),
            vmem(tile, jnp.float32),
            pltpu.SemaphoreType.DMA((nc - 1,)),
            pltpu.SemaphoreType.DMA((nc - 1,)),
            pltpu.SemaphoreType.DMA((half,)),
            pltpu.SemaphoreType.DMA((half,)),
            pltpu.SemaphoreType.DMA((2,)),
        ],
        compiler_params=pltpu.CompilerParams(
            collective_id=1, has_side_effects=True, vmem_limit_bytes=48 * 1024 * 1024),
    )(forward, backward.reshape((2, half) + tile))


def per_device(panel_values, near_tiles, far_left, far_right, near_rows, far_rows):
    n_row = lax.axis_size("row")
    n_col = lax.axis_size("col")
    clusters = panel_values.shape[0] // TILE
    groups = n_col * clusters
    colcount = n_row * clusters
    row_base = lax.axis_index("row") * groups
    near_local = near_rows - row_base
    far_local = far_rows - row_base
    rowx, colx = gather_slabs(panel_values, n_row, n_col)
    colx = colx.reshape(colcount, TILE, NRHS)
    forward, backward = local_products(near_local, far_local, near_tiles, far_left, far_right, colx, rowx)
    return scatter_sum(forward, backward, n_row, n_col)


def solution(mesh):
    placed = (
        P(("row", "col"), None),
        P(("row", "col"), None, None),
        P(("row", "col"), None, None),
        P(("row", "col"), None, None),
        P(("row", "col")),
        P(("row", "col")),
    )
    return jax.shard_map(
        per_device, mesh=mesh, in_specs=placed, out_specs=P(("row", "col"), None), check_vma=False
    )
```

```python
import functools

import jax
import jax.numpy as jnp
from jax import lax
from jax.experimental import pallas as pl
from jax.experimental.pallas import tpu as pltpu
from jax.sharding import PartitionSpec as P

TILE = 256
RANK = 64
NRHS = 256
DPC = 2
LPC = 8

TN = (((0,), (0,)), ((), ()))


def local_kernel(half, near_idx, far_idx, tiles_ref, left_ref, right_ref, slab_ref, out_ref, near_x, far_t):
    k = pl.program_id(0)
    base = slab_ref.shape[0] - 2
    fb = out_ref.shape[0] - 2

    @pl.when(k == 0)
    def _():
        out_ref[0:fb] = jnp.zeros(out_ref.shape[1:], jnp.float32)[None].repeat(fb, 0)

    xc = slab_ref[base + k // half, lax.rem(k, half)]
    tiles = tiles_ref[...].reshape(DPC * TILE, TILE)
    near_f = jnp.dot(tiles, xc, preferred_element_type=jnp.float32)
    for d in range(DPC):
        r = near_idx[k * DPC + d]
        out_ref[r // half, lax.rem(r, half)] += near_f[d * TILE:(d + 1) * TILE]
        near_x[d * TILE:(d + 1) * TILE] = slab_ref[r // half, lax.rem(r, half)]
    right = right_ref[...].reshape(LPC * RANK, TILE)
    coef = jnp.dot(right, xc, preferred_element_type=jnp.float32).astype(jnp.bfloat16)
    for d in range(LPC):
        r = far_idx[k * LPC + d]
        left = left_ref[d]
        out_ref[r // half, lax.rem(r, half)] += lax.dot_general(
            left, coef[d * RANK:(d + 1) * RANK], TN, preferred_element_type=jnp.float32)
        far_t[d * RANK:(d + 1) * RANK] = jnp.dot(
            left, slab_ref[r // half, lax.rem(r, half)], preferred_element_type=jnp.float32).astype(jnp.bfloat16)
    acc = lax.dot_general(tiles, near_x[...], TN, preferred_element_type=jnp.float32)
    acc += lax.dot_general(right, far_t[...], TN, preferred_element_type=jnp.float32)
    out_ref[fb + k // half, lax.rem(k, half)] = acc


def local_products(near_local, far_local, near_tiles, far_left, far_right, slab, count, groups):
    half = slab.shape[1]
    grid_spec = pltpu.PrefetchScalarGridSpec(
        num_scalar_prefetch=2,
        grid=(count,),
        in_specs=[
            pl.BlockSpec((DPC, TILE, TILE), lambda k, a, b: (k, 0, 0)),
            pl.BlockSpec((LPC, RANK, TILE), lambda k, a, b: (k, 0, 0)),
            pl.BlockSpec((LPC, RANK, TILE), lambda k, a, b: (k, 0, 0)),
            pl.BlockSpec(memory_space=pltpu.VMEM),
        ],
        out_specs=pl.BlockSpec(memory_space=pltpu.VMEM),
        scratch_shapes=[
            pltpu.VMEM((DPC * TILE, NRHS), jnp.bfloat16),
            pltpu.VMEM((LPC * RANK, NRHS), jnp.bfloat16),
        ],
    )
    flops = 2 * TILE * TILE * NRHS * near_tiles.shape[0] * 2 + 2 * RANK * TILE * NRHS * far_left.shape[0] * 4
    return pl.pallas_call(
        functools.partial(local_kernel, half),
        grid_spec=grid_spec,
        out_shape=jax.ShapeDtypeStruct((groups // half + 2, half, TILE, NRHS), jnp.float32),
        compiler_params=pltpu.CompilerParams(
            dimension_semantics=("arbitrary",), vmem_limit_bytes=48 * 1024 * 1024
        ),
        cost_estimate=pl.CostEstimate(flops=flops, bytes_accessed=24 * 1024 * 1024, transcendentals=0),
    )(near_local, far_local, near_tiles, far_left, far_right, slab)


MESH_ID = pl.DeviceIdType.MESH


def layout(nr, nc):
    i = lax.axis_index("row")
    j = lax.axis_index("col")
    half = nr // 2
    xh = i // half
    z = lax.rem(i, half)
    chips = nc // 2
    core = lax.rem(j, 2)
    chip = j // 2
    cols = [(i, 2 * lax.rem(chip + o, chips) + core) for o in range(1, chips)]
    cols.append((i, 2 * chip + 1 - core))
    right = (xh * half + lax.rem(z + 1, half), j)
    left = (xh * half + lax.rem(z + half - 1, half), j)
    partner = (lax.rem(i + half, nr), j)
    return i, j, half, xh, z, cols, right, left, partner


def enter(devices):
    barrier = pltpu.get_barrier_semaphore()
    for dev in devices:
        pl.semaphore_signal(barrier, 1, device_id=dev, device_id_type=MESH_ID)
    pl.semaphore_wait(barrier, len(devices))


def remote(src, dst, ssem, rsem, dev):
    return pltpu.make_async_remote_copy(src, dst, ssem, rsem, device_id=dev, device_id_type=MESH_ID)


def gather_kernel(nr, nc, x_ref, slab_ref, col_send, col_recv, ring_send, ring_recv, local_sem):
    i, j, half, xh, z, cols, right, left, partner = layout(nr, nc)
    cw = half // 2
    ccw = half - 1 - cw
    enter(cols + [right, left, partner])
    chips = nc // 2
    core = lax.rem(j, 2)
    chip = j // 2
    base = nc // half
    mine = slab_ref.at[j // half, lax.rem(j, half)]
    col_copies = [remote(x_ref, mine, col_send.at[n], col_recv.at[n], dev) for n, dev in enumerate(cols)]
    for c in col_copies:
        c.start()
    other = remote(x_ref, slab_ref.at[base + xh, z], ring_send.at[0], ring_recv.at[0], partner)
    other.start()
    own_row = pltpu.make_async_copy(x_ref, mine, local_sem.at[0])
    own_col = pltpu.make_async_copy(x_ref, slab_ref.at[base + xh, z], local_sem.at[1])
    own_row.start()
    own_col.start()
    mate = cols[-1]
    ring = []
    state = {}

    def ring_step(t):
        if t == 1:
            own_col.wait()
            other.wait()
        for way in range(2):
            if way == 1 and t > ccw:
                continue
            if way == 0:
                origin = lax.rem(z - t + 1 + half, half)
                sem, dev = t, right
            else:
                origin = lax.rem(z + t - 1, half)
                sem, dev = cw + t, left
            if t > 1:
                state[way].wait_recv()
            c = remote(slab_ref.at[base:base + 2, origin], slab_ref.at[base:base + 2, origin], ring_send.at[sem], ring_recv.at[sem], dev)
            c.start()
            ring.append(c)
            state[way] = c

    def col_step(o):
        origin = 2 * lax.rem(chip + chips - o, chips) + core
        col_copies[o - 1].wait_recv()
        c = remote(slab_ref.at[origin // half, lax.rem(origin, half)], slab_ref.at[origin // half, lax.rem(origin, half)], col_send.at[chips + o - 1],
                   col_recv.at[chips + o - 1], mate)
        c.start()
        col_copies.append(c)

    for n in range(max(cw, chips - 1)):
        if n < cw:
            ring_step(n + 1)
        if n < chips - 1:
            col_step(n + 1)
    for c in ring:
        c.wait_send()
    state[0].wait_recv()
    state[1].wait_recv()
    for c in col_copies:
        c.wait_send()
    for c in col_copies[chips - 1:]:
        c.wait_recv()
    own_row.wait()


def gather_slabs(x, nr, nc):
    tile = x.shape
    half = nr // 2
    return pl.pallas_call(
        functools.partial(gather_kernel, nr, nc),
        out_shape=jax.ShapeDtypeStruct((nc // half + 2, half) + tile, x.dtype),
        in_specs=[pl.BlockSpec(memory_space=pl.ANY)],
        out_specs=pl.BlockSpec(memory_space=pltpu.VMEM),
        scratch_shapes=[
            pltpu.SemaphoreType.DMA((nc - 1,)),
            pltpu.SemaphoreType.DMA((nc - 1,)),
            pltpu.SemaphoreType.DMA((half,)),
            pltpu.SemaphoreType.DMA((half,)),
            pltpu.SemaphoreType.DMA((2,)),
        ],
        compiler_params=pltpu.CompilerParams(collective_id=0, has_side_effects=True),
    )(x)


def scatter_kernel(nr, nc, p_ref, out_ref, recv_f, pre, stage, ring_in, ring_out, x_in, x_out,
                   col_send, col_recv, ring_send, ring_recv, local_sem):
    i, j, half, xh, z, cols, right, left, partner = layout(nr, nc)
    cw = half // 2
    ccw = half - 1 - cw
    enter(cols + [right, left, partner])
    chips = nc // 2
    core = lax.rem(j, 2)
    chip = j // 2
    fb = nc // half
    mate = cols[-1]
    handed = [2 * lax.rem(chip + o, chips) + 1 - core for o in range(1, chips)] + [mate[1]]
    col_copies = [remote(p_ref.at[m // half, lax.rem(m, half)], pre.at[n], col_send.at[n], col_recv.at[n], mate) for n, m in enumerate(handed)]
    for c in col_copies:
        c.start()
    sends = []
    arrivals = {}

    def ring_step(t):
        for way in range(2):
            if way == 1 and t > ccw:
                continue
            if way == 0:
                target = lax.rem(z + cw + 1 - t, half)
                slot, dev = t - 1, right
            else:
                target = lax.rem(z + half - (ccw + 1 - t), half)
                slot, dev = cw + t - 1, left
            if t == 1:
                src = p_ref.at[fb:fb + 2, target]
            else:
                arrivals[(way, t - 1)].wait_recv()
                ring_out[slot] = ring_in[slot - 1] + p_ref[fb:fb + 2, target]
                src = ring_out.at[slot]
            c = remote(src, ring_in.at[slot], ring_send.at[slot], ring_recv.at[slot], dev)
            c.start()
            sends.append(c)
            arrivals[(way, t)] = c

    def col_step(o):
        dev = cols[o - 1]
        col_copies[o - 1].wait_recv()
        stage[o - 1] = p_ref[dev[1] // half, lax.rem(dev[1], half)] + pre[o - 1]
        c = remote(stage.at[o - 1], recv_f.at[o - 1], col_send.at[chips + o - 1], col_recv.at[chips + o - 1], dev)
        c.start()
        col_copies.append(c)

    for n in range(max(cw, chips - 1)):
        if n < cw:
            ring_step(n + 1)
        if n < chips - 1:
            col_step(n + 1)
    col_copies[chips - 1].wait_recv()
    arrivals[(0, cw)].wait_recv()
    arrivals[(1, ccw)].wait_recv()
    away = 1 - xh
    x_out[...] = ring_in[cw - 1, away] + ring_in[cw + ccw - 1, away] + p_ref[fb + away, z]
    cross = remote(x_out, x_in, ring_send.at[half - 1], ring_recv.at[half - 1], partner)
    cross.start()
    for c in sends:
        c.wait_send()
    for c in col_copies:
        c.wait_send()
    for c in col_copies[chips:]:
        c.wait_recv()
    cross.wait()
    acc = ring_in[cw - 1, xh] + ring_in[cw + ccw - 1, xh] + p_ref[fb + xh, z] + x_in[...] + p_ref[j // half, lax.rem(j, half)] + pre[chips - 1]
    for n in range(chips - 1):
        acc = acc + recv_f[n]
    out_ref[...] = acc.astype(out_ref.dtype)


def scatter_sum(partial, nr, nc):
    tile = partial.shape[2:]
    half = nr // 2
    cw = half // 2
    steps = half - 1
    vmem = pltpu.VMEM
    return pl.pallas_call(
        functools.partial(scatter_kernel, nr, nc),
        out_shape=jax.ShapeDtypeStruct(tile, jnp.bfloat16),
        in_specs=[pl.BlockSpec(memory_space=vmem)],
        out_specs=pl.BlockSpec(memory_space=vmem),
        scratch_shapes=[
            vmem((nc // 2 - 1,) + tile, jnp.float32),
            vmem((nc // 2,) + tile, jnp.float32),
            vmem((nc // 2 - 1,) + tile, jnp.float32),
            vmem((steps, 2) + tile, jnp.float32),
            vmem((steps, 2) + tile, jnp.float32),
            vmem(tile, jnp.float32),
            vmem(tile, jnp.float32),
            pltpu.SemaphoreType.DMA((nc - 1,)),
            pltpu.SemaphoreType.DMA((nc - 1,)),
            pltpu.SemaphoreType.DMA((half,)),
            pltpu.SemaphoreType.DMA((half,)),
            pltpu.SemaphoreType.DMA((2,)),
        ],
        compiler_params=pltpu.CompilerParams(
            collective_id=1, has_side_effects=True, vmem_limit_bytes=48 * 1024 * 1024),
    )(partial)


def per_device(panel_values, near_tiles, far_left, far_right, near_rows, far_rows):
    n_row = lax.axis_size("row")
    n_col = lax.axis_size("col")
    clusters = panel_values.shape[0] // TILE
    groups = n_col * clusters
    colcount = n_row * clusters
    row_base = lax.axis_index("row") * groups
    near_local = near_rows - row_base
    far_local = far_rows - row_base
    slab = gather_slabs(panel_values, n_row, n_col)
    partial = local_products(near_local, far_local, near_tiles, far_left, far_right, slab, colcount, groups)
    return scatter_sum(partial, n_row, n_col)


def solution(mesh):
    placed = (
        P(("row", "col"), None),
        P(("row", "col"), None, None),
        P(("row", "col"), None, None),
        P(("row", "col"), None, None),
        P(("row", "col")),
        P(("row", "col")),
    )
    return jax.shard_map(
        per_device, mesh=mesh, in_specs=placed, out_specs=P(("row", "col"), None), check_vma=False
    )
```

```python
import functools

import jax
import jax.numpy as jnp
from jax import lax
from jax.experimental import pallas as pl
from jax.experimental.pallas import tpu as pltpu
from jax.sharding import PartitionSpec as P

TILE = 256
RANK = 64
NRHS = 256
DPC = 2
LPC = 8

TN = (((0,), (0,)), ((), ()))


def local_kernel(half, near_idx, far_idx, tiles_ref, left_ref, right_ref, slab_ref, out_ref):
    k = pl.program_id(0)
    base = slab_ref.shape[0] - 2

    @pl.when(k == 0)
    def _():
        out_ref[...] = jnp.zeros_like(out_ref)

    xc = slab_ref[base + k // half, lax.rem(k, half)]
    tiles = tiles_ref[...].reshape(DPC * TILE, TILE)
    near_f = jnp.dot(tiles, xc, preferred_element_type=jnp.float32)
    for d in range(DPC):
        r = near_idx[k * DPC + d]
        out_ref[r // half, lax.rem(r, half)] += near_f[d * TILE:(d + 1) * TILE]
    right = right_ref[...].reshape(LPC * RANK, TILE)
    coef = jnp.dot(right, xc, preferred_element_type=jnp.float32).astype(jnp.bfloat16)
    for d in range(LPC):
        r = far_idx[k * LPC + d]
        out_ref[r // half, lax.rem(r, half)] += lax.dot_general(
            left_ref[d], coef[d * RANK:(d + 1) * RANK], TN, preferred_element_type=jnp.float32)


def local_products(near_local, far_local, near_tiles, far_left, far_right, slab, count, groups):
    half = slab.shape[1]
    grid_spec = pltpu.PrefetchScalarGridSpec(
        num_scalar_prefetch=2,
        grid=(count,),
        in_specs=[
            pl.BlockSpec((DPC, TILE, TILE), lambda k, a, b: (k, 0, 0)),
            pl.BlockSpec((LPC, RANK, TILE), lambda k, a, b: (k, 0, 0)),
            pl.BlockSpec((LPC, RANK, TILE), lambda k, a, b: (k, 0, 0)),
            pl.BlockSpec(memory_space=pltpu.VMEM),
        ],
        out_specs=pl.BlockSpec(memory_space=pltpu.VMEM),
    )
    flops = 2 * TILE * TILE * NRHS * near_tiles.shape[0] + 2 * RANK * TILE * NRHS * far_left.shape[0] * 2
    return pl.pallas_call(
        functools.partial(local_kernel, half),
        grid_spec=grid_spec,
        out_shape=jax.ShapeDtypeStruct((groups // half, half, TILE, NRHS), jnp.float32),
        compiler_params=pltpu.CompilerParams(
            dimension_semantics=("arbitrary",), vmem_limit_bytes=48 * 1024 * 1024
        ),
        cost_estimate=pl.CostEstimate(flops=flops, bytes_accessed=16 * 1024 * 1024, transcendentals=0),
    )(near_local, far_local, near_tiles, far_left, far_right, slab)


MESH_ID = pl.DeviceIdType.MESH


def layout(nr, nc):
    i = lax.axis_index("row")
    j = lax.axis_index("col")
    half = nr // 2
    xh = i // half
    z = lax.rem(i, half)
    chips = nc // 2
    core = lax.rem(j, 2)
    chip = j // 2
    cols = [(i, 2 * lax.rem(chip + o, chips) + core) for o in range(1, chips)]
    cols.append((i, 2 * chip + 1 - core))
    right = (xh * half + lax.rem(z + 1, half), j)
    left = (xh * half + lax.rem(z + half - 1, half), j)
    partner = (lax.rem(i + half, nr), j)
    return i, j, half, xh, z, cols, right, left, partner


def enter(devices):
    barrier = pltpu.get_barrier_semaphore()
    for dev in devices:
        pl.semaphore_signal(barrier, 1, device_id=dev, device_id_type=MESH_ID)
    pl.semaphore_wait(barrier, len(devices))


def remote(src, dst, ssem, rsem, dev):
    return pltpu.make_async_remote_copy(src, dst, ssem, rsem, device_id=dev, device_id_type=MESH_ID)


def gather_kernel(nr, nc, x_ref, slab_ref, col_send, col_recv, ring_send, ring_recv, local_sem):
    i, j, half, xh, z, cols, right, left, partner = layout(nr, nc)
    cw = half // 2
    ccw = half - 1 - cw
    enter(cols + [right, left, partner])
    chips = nc // 2
    core = lax.rem(j, 2)
    chip = j // 2
    base = nc // half
    mine = slab_ref.at[j // half, lax.rem(j, half)]
    col_copies = [remote(x_ref, mine, col_send.at[n], col_recv.at[n], dev) for n, dev in enumerate(cols)]
    for c in col_copies:
        c.start()
    other = remote(x_ref, slab_ref.at[base + xh, z], ring_send.at[0], ring_recv.at[0], partner)
    other.start()
    own_row = pltpu.make_async_copy(x_ref, mine, local_sem.at[0])
    own_col = pltpu.make_async_copy(x_ref, slab_ref.at[base + xh, z], local_sem.at[1])
    own_row.start()
    own_col.start()
    mate = cols[-1]
    ring = []
    state = {}

    def ring_step(t):
        if t == 1:
            own_col.wait()
            other.wait()
        for way in range(2):
            if way == 1 and t > ccw:
                continue
            if way == 0:
                origin = lax.rem(z - t + 1 + half, half)
                sem, dev = t, right
            else:
                origin = lax.rem(z + t - 1, half)
                sem, dev = cw + t, left
            if t > 1:
                state[way].wait_recv()
            c = remote(slab_ref.at[base:base + 2, origin], slab_ref.at[base:base + 2, origin], ring_send.at[sem], ring_recv.at[sem], dev)
            c.start()
            ring.append(c)
            state[way] = c

    def col_step(o):
        origin = 2 * lax.rem(chip + chips - o, chips) + core
        col_copies[o - 1].wait_recv()
        c = remote(slab_ref.at[origin // half, lax.rem(origin, half)], slab_ref.at[origin // half, lax.rem(origin, half)], col_send.at[chips + o - 1],
                   col_recv.at[chips + o - 1], mate)
        c.start()
        col_copies.append(c)

    for n in range(max(cw, chips - 1)):
        if n < cw:
            ring_step(n + 1)
        if n < chips - 1:
            col_step(n + 1)
    for c in ring:
        c.wait_send()
    state[0].wait_recv()
    state[1].wait_recv()
    for c in col_copies:
        c.wait_send()
    for c in col_copies[chips - 1:]:
        c.wait_recv()
    own_row.wait()


def gather_slabs(x, nr, nc):
    tile = x.shape
    half = nr // 2
    return pl.pallas_call(
        functools.partial(gather_kernel, nr, nc),
        out_shape=jax.ShapeDtypeStruct((nc // half + 2, half) + tile, x.dtype),
        in_specs=[pl.BlockSpec(memory_space=pl.ANY)],
        out_specs=pl.BlockSpec(memory_space=pltpu.VMEM),
        scratch_shapes=[
            pltpu.SemaphoreType.DMA((nc - 1,)),
            pltpu.SemaphoreType.DMA((nc - 1,)),
            pltpu.SemaphoreType.DMA((half,)),
            pltpu.SemaphoreType.DMA((half,)),
            pltpu.SemaphoreType.DMA((2,)),
        ],
        compiler_params=pltpu.CompilerParams(collective_id=0, has_side_effects=True),
    )(x)


def scatter_kernel(nr, nc, near_idx, far_idx, p_ref, slab_ref, tiles_hbm, left_hbm, right_hbm, out_ref,
                   tiles_v, left_v, right_v, b_buf, near_x, far_t, recv_f, pre, stage, ring_in, ring_out, x_in, x_out,
                   col_send, col_recv, ring_send, ring_recv, local_sem):
    i, j, half, xh, z, cols, right, left, partner = layout(nr, nc)
    cw = half // 2
    ccw = half - 1 - cw
    loads = [pltpu.make_async_copy(src, dst, local_sem.at[n])
             for n, (src, dst) in enumerate([(tiles_hbm, tiles_v), (right_hbm, right_v), (left_hbm, left_v)])]
    for c in loads:
        c.start()
    enter(cols + [right, left, partner])
    chips = nc // 2
    core = lax.rem(j, 2)
    chip = j // 2
    mate = cols[-1]
    handed = [2 * lax.rem(chip + o, chips) + 1 - core for o in range(1, chips)] + [mate[1]]
    col_copies = [remote(p_ref.at[m // half, lax.rem(m, half)], pre.at[n], col_send.at[n], col_recv.at[n], mate) for n, m in enumerate(handed)]
    for c in col_copies:
        c.start()
    sends = []
    arrivals = {}
    for c in loads:
        c.wait()

    def back(xhp, target):
        k = xhp * half + target
        tiles = tiles_v[pl.ds(k * DPC, DPC)].reshape(DPC * TILE, TILE)
        for d in range(DPC):
            near_x[d * TILE:(d + 1) * TILE] = slab_ref[near_idx[k * DPC + d]]
        rfac = right_v[pl.ds(k * LPC, LPC)].reshape(LPC * RANK, TILE)
        for d in range(LPC):
            far_t[d * RANK:(d + 1) * RANK] = jnp.dot(
                left_v[k * LPC + d], slab_ref[far_idx[k * LPC + d]], preferred_element_type=jnp.float32
            ).astype(jnp.bfloat16)
        acc = lax.dot_general(tiles, near_x[...], TN, preferred_element_type=jnp.float32)
        acc += lax.dot_general(rfac, far_t[...], TN, preferred_element_type=jnp.float32)
        b_buf[xhp, target] = acc

    def ring_step(t):
        for way in range(2):
            if way == 1 and t > ccw:
                continue
            if way == 0:
                target = lax.rem(z + cw + 1 - t, half)
                slot, dev = t - 1, right
            else:
                target = lax.rem(z + half - (ccw + 1 - t), half)
                slot, dev = cw + t - 1, left
            back(0, target)
            back(1, target)
            if t == 1:
                src = b_buf.at[:, target]
            else:
                arrivals[(way, t - 1)].wait_recv()
                ring_out[slot] = ring_in[slot - 1] + b_buf[:, target]
                src = ring_out.at[slot]
            c = remote(src, ring_in.at[slot], ring_send.at[slot], ring_recv.at[slot], dev)
            c.start()
            sends.append(c)
            arrivals[(way, t)] = c

    def col_step(o):
        dev = cols[o - 1]
        col_copies[o - 1].wait_recv()
        stage[o - 1] = p_ref[dev[1] // half, lax.rem(dev[1], half)] + pre[o - 1]
        c = remote(stage.at[o - 1], recv_f.at[o - 1], col_send.at[chips + o - 1], col_recv.at[chips + o - 1], dev)
        c.start()
        col_copies.append(c)

    for n in range(max(cw, chips - 1)):
        if n < cw:
            ring_step(n + 1)
        if n < chips - 1:
            col_step(n + 1)
    back(0, z)
    back(1, z)
    col_copies[chips - 1].wait_recv()
    arrivals[(0, cw)].wait_recv()
    arrivals[(1, ccw)].wait_recv()
    away = 1 - xh
    x_out[...] = ring_in[cw - 1, away] + ring_in[cw + ccw - 1, away] + b_buf[away, z]
    cross = remote(x_out, x_in, ring_send.at[half - 1], ring_recv.at[half - 1], partner)
    cross.start()
    for c in sends:
        c.wait_send()
    for c in col_copies:
        c.wait_send()
    for c in col_copies[chips:]:
        c.wait_recv()
    cross.wait()
    acc = ring_in[cw - 1, xh] + ring_in[cw + ccw - 1, xh] + b_buf[xh, z] + x_in[...] + p_ref[j // half, lax.rem(j, half)] + pre[chips - 1]
    for n in range(chips - 1):
        acc = acc + recv_f[n]
    out_ref[...] = acc.astype(out_ref.dtype)


def scatter_sum(partial, slab, near_local, far_local, near_tiles, far_left, far_right, nr, nc):
    tile = partial.shape[2:]
    half = nr // 2
    cw = half // 2
    steps = half - 1
    vmem = pltpu.VMEM
    return pl.pallas_call(
        functools.partial(scatter_kernel, nr, nc),
        out_shape=jax.ShapeDtypeStruct(tile, jnp.bfloat16),
        in_specs=[pl.BlockSpec(memory_space=pltpu.SMEM)] * 2
        + [pl.BlockSpec(memory_space=vmem)] * 2
        + [pl.BlockSpec(memory_space=pl.ANY)] * 3,
        out_specs=pl.BlockSpec(memory_space=vmem),
        scratch_shapes=[
            vmem(near_tiles.shape, near_tiles.dtype),
            vmem(far_left.shape, far_left.dtype),
            vmem(far_right.shape, far_right.dtype),
            vmem((2, half) + tile, jnp.float32),
            vmem((DPC * TILE, NRHS), jnp.bfloat16),
            vmem((LPC * RANK, NRHS), jnp.bfloat16),
            vmem((nc // 2 - 1,) + tile, jnp.float32),
            vmem((nc // 2,) + tile, jnp.float32),
            vmem((nc // 2 - 1,) + tile, jnp.float32),
            vmem((steps, 2) + tile, jnp.float32),
            vmem((steps, 2) + tile, jnp.float32),
            vmem(tile, jnp.float32),
            vmem(tile, jnp.float32),
            pltpu.SemaphoreType.DMA((nc - 1,)),
            pltpu.SemaphoreType.DMA((nc - 1,)),
            pltpu.SemaphoreType.DMA((half,)),
            pltpu.SemaphoreType.DMA((half,)),
            pltpu.SemaphoreType.DMA((3,)),
        ],
        compiler_params=pltpu.CompilerParams(
            collective_id=1, has_side_effects=True, vmem_limit_bytes=60 * 1024 * 1024),
    )(near_local, far_local, partial, slab.reshape((-1,) + tile), near_tiles, far_left, far_right)


def per_device(panel_values, near_tiles, far_left, far_right, near_rows, far_rows):
    n_row = lax.axis_size("row")
    n_col = lax.axis_size("col")
    clusters = panel_values.shape[0] // TILE
    groups = n_col * clusters
    colcount = n_row * clusters
    row_base = lax.axis_index("row") * groups
    near_local = near_rows - row_base
    far_local = far_rows - row_base
    slab = gather_slabs(panel_values, n_row, n_col)
    partial = local_products(near_local, far_local, near_tiles, far_left, far_right, slab, colcount, groups)
    return scatter_sum(partial, slab, near_local, far_local, near_tiles, far_left, far_right, n_row, n_col)


def solution(mesh):
    placed = (
        P(("row", "col"), None),
        P(("row", "col"), None, None),
        P(("row", "col"), None, None),
        P(("row", "col"), None, None),
        P(("row", "col")),
        P(("row", "col")),
    )
    return jax.shard_map(
        per_device, mesh=mesh, in_specs=placed, out_specs=P(("row", "col"), None), check_vma=False
    )
```

```python
import functools

import jax
import jax.numpy as jnp
from jax import lax
from jax.experimental import pallas as pl
from jax.experimental.pallas import tpu as pltpu
from jax.sharding import PartitionSpec as P

TILE = 256
RANK = 64
NRHS = 256
DPC = 2
LPC = 8

TN = (((0,), (0,)), ((), ()))


def local_kernel(half, per, near_idx, far_idx, tiles_ref, left_ref, right_ref, slab_ref, out_ref):
    step = pl.program_id(0)
    base = slab_ref.shape[0] - 2

    @pl.when(step == 0)
    def _():
        out_ref[...] = jnp.zeros_like(out_ref)

    for kk in range(per):
        k = step * per + kk
        xc = slab_ref[base + k // half, lax.rem(k, half)]
        tiles = tiles_ref[kk * DPC:(kk + 1) * DPC].reshape(DPC * TILE, TILE)
        near_f = jnp.dot(tiles, xc, preferred_element_type=jnp.float32)
        for d in range(DPC):
            r = near_idx[k * DPC + d]
            out_ref[r // half, lax.rem(r, half)] += near_f[d * TILE:(d + 1) * TILE]
        right = right_ref[kk * LPC:(kk + 1) * LPC].reshape(LPC * RANK, TILE)
        coef = jnp.dot(right, xc, preferred_element_type=jnp.float32).astype(jnp.bfloat16)
        for d in range(LPC):
            r = far_idx[k * LPC + d]
            out_ref[r // half, lax.rem(r, half)] += lax.dot_general(
                left_ref[kk * LPC + d], coef[d * RANK:(d + 1) * RANK], TN, preferred_element_type=jnp.float32)


def local_products(near_local, far_local, near_tiles, far_left, far_right, slab, count, groups):
    half = slab.shape[1]
    per = 4 if count % 4 == 0 else 1
    grid_spec = pltpu.PrefetchScalarGridSpec(
        num_scalar_prefetch=2,
        grid=(count // per,),
        in_specs=[
            pl.BlockSpec((per * DPC, TILE, TILE), lambda k, a, b: (k, 0, 0)),
            pl.BlockSpec((per * LPC, RANK, TILE), lambda k, a, b: (k, 0, 0)),
            pl.BlockSpec((per * LPC, RANK, TILE), lambda k, a, b: (k, 0, 0)),
            pl.BlockSpec(memory_space=pltpu.VMEM),
        ],
        out_specs=pl.BlockSpec(memory_space=pltpu.VMEM),
    )
    flops = 2 * TILE * TILE * NRHS * near_tiles.shape[0] + 2 * RANK * TILE * NRHS * far_left.shape[0] * 2
    return pl.pallas_call(
        functools.partial(local_kernel, half, per),
        grid_spec=grid_spec,
        out_shape=jax.ShapeDtypeStruct((groups // half, half, TILE, NRHS), jnp.float32),
        compiler_params=pltpu.CompilerParams(
            dimension_semantics=("arbitrary",), vmem_limit_bytes=48 * 1024 * 1024
        ),
        cost_estimate=pl.CostEstimate(flops=flops, bytes_accessed=16 * 1024 * 1024, transcendentals=0),
    )(near_local, far_local, near_tiles, far_left, far_right, slab)


MESH_ID = pl.DeviceIdType.MESH


def layout(nr, nc):
    i = lax.axis_index("row")
    j = lax.axis_index("col")
    half = nr // 2
    xh = i // half
    z = lax.rem(i, half)
    chips = nc // 2
    core = lax.rem(j, 2)
    chip = j // 2
    cols = [(i, 2 * lax.rem(chip + o, chips) + core) for o in range(1, chips)]
    cols.append((i, 2 * chip + 1 - core))
    right = (xh * half + lax.rem(z + 1, half), j)
    left = (xh * half + lax.rem(z + half - 1, half), j)
    partner = (lax.rem(i + half, nr), j)
    return i, j, half, xh, z, cols, right, left, partner


def enter(devices):
    barrier = pltpu.get_barrier_semaphore()
    for dev in devices:
        pl.semaphore_signal(barrier, 1, device_id=dev, device_id_type=MESH_ID)
    pl.semaphore_wait(barrier, len(devices))


def remote(src, dst, ssem, rsem, dev):
    return pltpu.make_async_remote_copy(src, dst, ssem, rsem, device_id=dev, device_id_type=MESH_ID)


def gather_kernel(nr, nc, x_ref, slab_ref, col_send, col_recv, ring_send, ring_recv, local_sem):
    i, j, half, xh, z, cols, right, left, partner = layout(nr, nc)
    cw = half // 2
    ccw = half - 1 - cw
    enter(cols + [right, left, partner])
    chips = nc // 2
    core = lax.rem(j, 2)
    chip = j // 2
    base = nc // half
    mine = slab_ref.at[j // half, lax.rem(j, half)]
    other = remote(x_ref, slab_ref.at[base + xh, z], ring_send.at[0], ring_recv.at[0], partner)
    other.start()
    col_copies = [remote(x_ref, mine, col_send.at[n], col_recv.at[n], dev) for n, dev in enumerate(cols)]
    for c in col_copies:
        c.start()
    own_row = pltpu.make_async_copy(x_ref, mine, local_sem.at[0])
    own_col = pltpu.make_async_copy(x_ref, slab_ref.at[base + xh, z], local_sem.at[1])
    own_row.start()
    own_col.start()
    mate = cols[-1]
    ring = []
    state = {}

    def ring_step(t):
        if t == 1:
            own_col.wait()
            other.wait()
        for way in range(2):
            if way == 1 and t > ccw:
                continue
            if way == 0:
                origin = lax.rem(z - t + 1 + half, half)
                sem, dev = t, right
            else:
                origin = lax.rem(z + t - 1, half)
                sem, dev = cw + t, left
            if t > 1:
                state[way].wait_recv()
            c = remote(slab_ref.at[base:base + 2, origin], slab_ref.at[base:base + 2, origin], ring_send.at[sem], ring_recv.at[sem], dev)
            c.start()
            ring.append(c)
            state[way] = c

    def col_step(o):
        origin = 2 * lax.rem(chip + chips - o, chips) + core
        col_copies[o - 1].wait_recv()
        c = remote(slab_ref.at[origin // half, lax.rem(origin, half)], slab_ref.at[origin // half, lax.rem(origin, half)], col_send.at[chips + o - 1],
                   col_recv.at[chips + o - 1], mate)
        c.start()
        col_copies.append(c)

    for n in range(max(cw, chips - 1)):
        if n < cw:
            ring_step(n + 1)
        if n < chips - 1:
            col_step(n + 1)
    for c in ring:
        c.wait_send()
    state[0].wait_recv()
    state[1].wait_recv()
    for c in col_copies:
        c.wait_send()
    for c in col_copies[chips - 1:]:
        c.wait_recv()
    own_row.wait()


def gather_slabs(x, nr, nc):
    tile = x.shape
    half = nr // 2
    return pl.pallas_call(
        functools.partial(gather_kernel, nr, nc),
        out_shape=jax.ShapeDtypeStruct((nc // half + 2, half) + tile, x.dtype),
        in_specs=[pl.BlockSpec(memory_space=pl.ANY)],
        out_specs=pl.BlockSpec(memory_space=pltpu.VMEM),
        scratch_shapes=[
            pltpu.SemaphoreType.DMA((nc - 1,)),
            pltpu.SemaphoreType.DMA((nc - 1,)),
            pltpu.SemaphoreType.DMA((half,)),
            pltpu.SemaphoreType.DMA((half,)),
            pltpu.SemaphoreType.DMA((2,)),
        ],
        compiler_params=pltpu.CompilerParams(collective_id=0, has_side_effects=True),
    )(x)


def scatter_kernel(nr, nc, near_idx, far_idx, p_ref, slab_ref, tiles_hbm, left_hbm, right_hbm, out_ref,
                   tiles_v, left_v, right_v, b_buf, near_x, far_t, recv_f, pre, stage, ring_in, ring_out, x_in, x_out,
                   col_send, col_recv, ring_send, ring_recv, local_sem):
    i, j, half, xh, z, cols, right, left, partner = layout(nr, nc)
    cw = half // 2
    ccw = half - 1 - cw
    loads = [pltpu.make_async_copy(src, dst, local_sem.at[n])
             for n, (src, dst) in enumerate([(tiles_hbm, tiles_v), (right_hbm, right_v), (left_hbm, left_v)])]
    for c in loads:
        c.start()
    enter(cols + [right, left, partner])
    chips = nc // 2
    core = lax.rem(j, 2)
    chip = j // 2
    mate = cols[-1]
    handed = [2 * lax.rem(chip + o, chips) + 1 - core for o in range(1, chips)] + [mate[1]]
    col_copies = [remote(p_ref.at[m // half, lax.rem(m, half)], pre.at[n], col_send.at[n], col_recv.at[n], mate) for n, m in enumerate(handed)]
    for c in col_copies:
        c.start()
    sends = []
    arrivals = {}
    for c in loads:
        c.wait()

    def back(xhp, target):
        k = xhp * half + target
        tiles = tiles_v[pl.ds(k * DPC, DPC)].reshape(DPC * TILE, TILE)
        for d in range(DPC):
            near_x[d * TILE:(d + 1) * TILE] = slab_ref[near_idx[k * DPC + d]]
        rfac = right_v[pl.ds(k * LPC, LPC)].reshape(LPC * RANK, TILE)
        for d in range(LPC):
            far_t[d * RANK:(d + 1) * RANK] = jnp.dot(
                left_v[k * LPC + d], slab_ref[far_idx[k * LPC + d]], preferred_element_type=jnp.float32
            ).astype(jnp.bfloat16)
        acc = lax.dot_general(tiles, near_x[...], TN, preferred_element_type=jnp.float32)
        acc += lax.dot_general(rfac, far_t[...], TN, preferred_element_type=jnp.float32)
        b_buf[xhp, target] = acc

    def ring_step(t):
        for way in range(2):
            if way == 1 and t > ccw:
                continue
            if way == 0:
                target = lax.rem(z + cw + 1 - t, half)
                slot, dev = t - 1, right
            else:
                target = lax.rem(z + half - (ccw + 1 - t), half)
                slot, dev = cw + t - 1, left
            back(0, target)
            back(1, target)
            if t == 1:
                src = b_buf.at[:, target]
            else:
                arrivals[(way, t - 1)].wait_recv()
                ring_out[slot] = ring_in[slot - 1] + b_buf[:, target]
                src = ring_out.at[slot]
            c = remote(src, ring_in.at[slot], ring_send.at[slot], ring_recv.at[slot], dev)
            c.start()
            sends.append(c)
            arrivals[(way, t)] = c

    def col_step(o):
        dev = cols[o - 1]
        col_copies[o - 1].wait_recv()
        stage[o - 1] = p_ref[dev[1] // half, lax.rem(dev[1], half)] + pre[o - 1]
        c = remote(stage.at[o - 1], recv_f.at[o - 1], col_send.at[chips + o - 1], col_recv.at[chips + o - 1], dev)
        c.start()
        col_copies.append(c)

    for n in range(max(cw, chips - 1)):
        if n < cw:
            ring_step(n + 1)
        if n < chips - 1:
            col_step(n + 1)
    back(0, z)
    back(1, z)
    col_copies[chips - 1].wait_recv()
    arrivals[(0, cw)].wait_recv()
    arrivals[(1, ccw)].wait_recv()
    away = 1 - xh
    x_out[...] = ring_in[cw - 1, away] + ring_in[cw + ccw - 1, away] + b_buf[away, z]
    cross = remote(x_out, x_in, ring_send.at[half - 1], ring_recv.at[half - 1], partner)
    cross.start()
    for c in sends:
        c.wait_send()
    for c in col_copies:
        c.wait_send()
    for c in col_copies[chips:]:
        c.wait_recv()
    cross.wait()
    acc = ring_in[cw - 1, xh] + ring_in[cw + ccw - 1, xh] + b_buf[xh, z] + x_in[...] + p_ref[j // half, lax.rem(j, half)] + pre[chips - 1]
    for n in range(chips - 1):
        acc = acc + recv_f[n]
    out_ref[...] = acc.astype(out_ref.dtype)


def scatter_sum(partial, slab, near_local, far_local, near_tiles, far_left, far_right, nr, nc):
    tile = partial.shape[2:]
    half = nr // 2
    cw = half // 2
    steps = half - 1
    vmem = pltpu.VMEM
    return pl.pallas_call(
        functools.partial(scatter_kernel, nr, nc),
        out_shape=jax.ShapeDtypeStruct(tile, jnp.bfloat16),
        in_specs=[pl.BlockSpec(memory_space=pltpu.SMEM)] * 2
        + [pl.BlockSpec(memory_space=vmem)] * 2
        + [pl.BlockSpec(memory_space=pl.ANY)] * 3,
        out_specs=pl.BlockSpec(memory_space=vmem),
        scratch_shapes=[
            vmem(near_tiles.shape, near_tiles.dtype),
            vmem(far_left.shape, far_left.dtype),
            vmem(far_right.shape, far_right.dtype),
            vmem((2, half) + tile, jnp.float32),
            vmem((DPC * TILE, NRHS), jnp.bfloat16),
            vmem((LPC * RANK, NRHS), jnp.bfloat16),
            vmem((nc // 2 - 1,) + tile, jnp.float32),
            vmem((nc // 2,) + tile, jnp.float32),
            vmem((nc // 2 - 1,) + tile, jnp.float32),
            vmem((steps, 2) + tile, jnp.float32),
            vmem((steps, 2) + tile, jnp.float32),
            vmem(tile, jnp.float32),
            vmem(tile, jnp.float32),
            pltpu.SemaphoreType.DMA((nc - 1,)),
            pltpu.SemaphoreType.DMA((nc - 1,)),
            pltpu.SemaphoreType.DMA((half,)),
            pltpu.SemaphoreType.DMA((half,)),
            pltpu.SemaphoreType.DMA((3,)),
        ],
        compiler_params=pltpu.CompilerParams(
            collective_id=1, has_side_effects=True, vmem_limit_bytes=60 * 1024 * 1024),
    )(near_local, far_local, partial, slab.reshape((-1,) + tile), near_tiles, far_left, far_right)


def per_device(panel_values, near_tiles, far_left, far_right, near_rows, far_rows):
    n_row = lax.axis_size("row")
    n_col = lax.axis_size("col")
    clusters = panel_values.shape[0] // TILE
    groups = n_col * clusters
    colcount = n_row * clusters
    row_base = lax.axis_index("row") * groups
    near_local = near_rows - row_base
    far_local = far_rows - row_base
    slab = gather_slabs(panel_values, n_row, n_col)
    partial = local_products(near_local, far_local, near_tiles, far_left, far_right, slab, colcount, groups)
    return scatter_sum(partial, slab, near_local, far_local, near_tiles, far_left, far_right, n_row, n_col)


def solution(mesh):
    placed = (
        P(("row", "col"), None),
        P(("row", "col"), None, None),
        P(("row", "col"), None, None),
        P(("row", "col"), None, None),
        P(("row", "col")),
        P(("row", "col")),
    )
    return jax.shard_map(
        per_device, mesh=mesh, in_specs=placed, out_specs=P(("row", "col"), None), check_vma=False
    )
```

```python
import functools

import jax
import jax.numpy as jnp
from jax import lax
from jax.experimental import pallas as pl
from jax.experimental.pallas import tpu as pltpu
from jax.sharding import PartitionSpec as P

TILE = 256
RANK = 64
NRHS = 256
DPC = 2
LPC = 8

TN = (((0,), (0,)), ((), ()))


def local_kernel(half, per, near_idx, far_idx, tiles_ref, left_ref, right_ref, slab_ref, out_ref):
    step = pl.program_id(0)
    base = slab_ref.shape[0] - 2

    @pl.when(step == 0)
    def _():
        out_ref[...] = jnp.zeros_like(out_ref)

    for kk in range(per):
        k = step * per + kk
        xc = slab_ref[base + k // half, lax.rem(k, half)]
        tiles = tiles_ref[kk * DPC:(kk + 1) * DPC].reshape(DPC * TILE, TILE)
        near_f = jnp.dot(tiles, xc, preferred_element_type=jnp.float32)
        for d in range(DPC):
            r = near_idx[k * DPC + d]
            out_ref[r // half, lax.rem(r, half)] += near_f[d * TILE:(d + 1) * TILE]
        right = right_ref[kk * LPC:(kk + 1) * LPC].reshape(LPC * RANK, TILE)
        coef = jnp.dot(right, xc, preferred_element_type=jnp.float32).astype(jnp.bfloat16)
        for d in range(LPC):
            r = far_idx[k * LPC + d]
            out_ref[r // half, lax.rem(r, half)] += lax.dot_general(
                left_ref[kk * LPC + d], coef[d * RANK:(d + 1) * RANK], TN, preferred_element_type=jnp.float32)


def local_products(near_local, far_local, near_tiles, far_left, far_right, slab, count, groups):
    half = slab.shape[1]
    per = 4 if count % 4 == 0 else 1
    grid_spec = pltpu.PrefetchScalarGridSpec(
        num_scalar_prefetch=2,
        grid=(count // per,),
        in_specs=[
            pl.BlockSpec((per * DPC, TILE, TILE), lambda k, a, b: (k, 0, 0)),
            pl.BlockSpec((per * LPC, RANK, TILE), lambda k, a, b: (k, 0, 0)),
            pl.BlockSpec((per * LPC, RANK, TILE), lambda k, a, b: (k, 0, 0)),
            pl.BlockSpec(memory_space=pltpu.VMEM),
        ],
        out_specs=pl.BlockSpec(memory_space=pltpu.VMEM),
    )
    flops = 2 * TILE * TILE * NRHS * near_tiles.shape[0] + 2 * RANK * TILE * NRHS * far_left.shape[0] * 2
    return pl.pallas_call(
        functools.partial(local_kernel, half, per),
        grid_spec=grid_spec,
        out_shape=jax.ShapeDtypeStruct((groups // half, half, TILE, NRHS), jnp.float32),
        compiler_params=pltpu.CompilerParams(
            dimension_semantics=("arbitrary",), vmem_limit_bytes=48 * 1024 * 1024
        ),
        cost_estimate=pl.CostEstimate(flops=flops, bytes_accessed=16 * 1024 * 1024, transcendentals=0),
    )(near_local, far_local, near_tiles, far_left, far_right, slab)


MESH_ID = pl.DeviceIdType.MESH


def layout(nr, nc):
    i = lax.axis_index("row")
    j = lax.axis_index("col")
    half = nr // 2
    xh = i // half
    z = lax.rem(i, half)
    chips = nc // 2
    core = lax.rem(j, 2)
    chip = j // 2
    cols = [(i, 2 * lax.rem(chip + o, chips) + core) for o in range(1, chips)]
    cols.append((i, 2 * chip + 1 - core))
    right = (xh * half + lax.rem(z + 1, half), j)
    left = (xh * half + lax.rem(z + half - 1, half), j)
    partner = (lax.rem(i + half, nr), j)
    return i, j, half, xh, z, cols, right, left, partner


def enter(devices):
    barrier = pltpu.get_barrier_semaphore()
    for dev in devices:
        pl.semaphore_signal(barrier, 1, device_id=dev, device_id_type=MESH_ID)
    pl.semaphore_wait(barrier, len(devices))


def remote(src, dst, ssem, rsem, dev):
    return pltpu.make_async_remote_copy(src, dst, ssem, rsem, device_id=dev, device_id_type=MESH_ID)


def gather_kernel(nr, nc, x_ref, slab_ref, col_send, col_recv, ring_send, ring_recv, local_sem):
    i, j, half, xh, z, cols, right, left, partner = layout(nr, nc)
    cw = half // 2
    ccw = half - 1 - cw
    enter(cols + [right, left, partner])
    chips = nc // 2
    core = lax.rem(j, 2)
    chip = j // 2
    base = nc // half
    mine = slab_ref.at[j // half, lax.rem(j, half)]
    other = remote(x_ref, slab_ref.at[base + xh, z], ring_send.at[0], ring_recv.at[0], partner)
    other.start()
    col_copies = [remote(x_ref, mine, col_send.at[n], col_recv.at[n], dev) for n, dev in enumerate(cols)]
    for c in col_copies:
        c.start()
    own_row = pltpu.make_async_copy(x_ref, mine, local_sem.at[0])
    own_col = pltpu.make_async_copy(x_ref, slab_ref.at[base + xh, z], local_sem.at[1])
    own_row.start()
    own_col.start()
    mate = cols[-1]
    ring = []
    state = {}

    def ring_step(t):
        if t == 1:
            own_col.wait()
            other.wait()
        for way in range(2):
            if way == 1 and t > ccw:
                continue
            if way == 0:
                origin = lax.rem(z - t + 1 + half, half)
                sem, dev = t, right
            else:
                origin = lax.rem(z + t - 1, half)
                sem, dev = cw + t, left
            if t > 1:
                state[way].wait_recv()
            c = remote(slab_ref.at[base:base + 2, origin], slab_ref.at[base:base + 2, origin], ring_send.at[sem], ring_recv.at[sem], dev)
            c.start()
            ring.append(c)
            state[way] = c

    def col_step(o):
        origin = 2 * lax.rem(chip + chips - o, chips) + core
        col_copies[o - 1].wait_recv()
        c = remote(slab_ref.at[origin // half, lax.rem(origin, half)], slab_ref.at[origin // half, lax.rem(origin, half)], col_send.at[chips + o - 1],
                   col_recv.at[chips + o - 1], mate)
        c.start()
        col_copies.append(c)

    for n in range(max(cw, chips - 1)):
        if n < cw:
            ring_step(n + 1)
        if n < chips - 1:
            col_step(n + 1)
    for c in ring:
        c.wait_send()
    state[0].wait_recv()
    state[1].wait_recv()
    for c in col_copies:
        c.wait_send()
    for c in col_copies[chips - 1:]:
        c.wait_recv()
    own_row.wait()


def gather_slabs(x, nr, nc):
    tile = x.shape
    half = nr // 2
    return pl.pallas_call(
        functools.partial(gather_kernel, nr, nc),
        out_shape=jax.ShapeDtypeStruct((nc // half + 2, half) + tile, x.dtype),
        in_specs=[pl.BlockSpec(memory_space=pl.ANY)],
        out_specs=pl.BlockSpec(memory_space=pltpu.VMEM),
        scratch_shapes=[
            pltpu.SemaphoreType.DMA((nc - 1,)),
            pltpu.SemaphoreType.DMA((nc - 1,)),
            pltpu.SemaphoreType.DMA((half,)),
            pltpu.SemaphoreType.DMA((half,)),
            pltpu.SemaphoreType.DMA((2,)),
        ],
        compiler_params=pltpu.CompilerParams(collective_id=0, has_side_effects=True),
    )(x)


def scatter_kernel(nr, nc, near_idx, far_idx, p_ref, slab_ref, tiles_hbm, left_hbm, right_hbm, out_ref,
                   tiles_v, left_v, right_v, b_buf, near_x, far_t, recv_f, pre, stage, ring_in, ring_out, x_in, x_out,
                   col_send, col_recv, ring_send, ring_recv, local_sem):
    i, j, half, xh, z, cols, right, left, partner = layout(nr, nc)
    cw = half // 2
    ccw = half - 1 - cw
    need = []
    for t in range(1, cw + 1):
        need.append(lax.rem(z + cw + 1 - t, half))
        if t <= ccw:
            need.append(lax.rem(z + half - (ccw + 1 - t), half))
    need.append(z)
    loads = []
    for p, target in enumerate(need):
        group = []
        for xhp in range(2):
            k = xhp * half + target
            for n, (src, dst, width) in enumerate(
                    [(tiles_hbm, tiles_v, DPC), (right_hbm, right_v, LPC), (left_hbm, left_v, LPC)]):
                span = pl.ds(k * width, width)
                c = pltpu.make_async_copy(src.at[span], dst.at[span], local_sem.at[p, xhp, n])
                c.start()
                group.append(c)
        loads.append(group)
    enter(cols + [right, left, partner])
    chips = nc // 2
    core = lax.rem(j, 2)
    chip = j // 2
    mate = cols[-1]
    handed = [2 * lax.rem(chip + o, chips) + 1 - core for o in range(1, chips)] + [mate[1]]
    col_copies = [remote(p_ref.at[m // half, lax.rem(m, half)], pre.at[n], col_send.at[n], col_recv.at[n], mate) for n, m in enumerate(handed)]
    sends = []
    arrivals = {}

    def fetch(p):
        for c in loads[p]:
            c.wait()

    def back(xhp, target):
        k = xhp * half + target
        tiles = tiles_v[pl.ds(k * DPC, DPC)].reshape(DPC * TILE, TILE)
        for d in range(DPC):
            near_x[d * TILE:(d + 1) * TILE] = slab_ref[near_idx[k * DPC + d]]
        rfac = right_v[pl.ds(k * LPC, LPC)].reshape(LPC * RANK, TILE)
        for d in range(LPC):
            far_t[d * RANK:(d + 1) * RANK] = jnp.dot(
                left_v[k * LPC + d], slab_ref[far_idx[k * LPC + d]], preferred_element_type=jnp.float32
            ).astype(jnp.bfloat16)
        acc = lax.dot_general(tiles, near_x[...], TN, preferred_element_type=jnp.float32)
        acc += lax.dot_general(rfac, far_t[...], TN, preferred_element_type=jnp.float32)
        b_buf[xhp, target] = acc

    def ring_step(t):
        for way in range(2):
            if way == 1 and t > ccw:
                continue
            if way == 0:
                target = lax.rem(z + cw + 1 - t, half)
                slot, dev = t - 1, right
            else:
                target = lax.rem(z + half - (ccw + 1 - t), half)
                slot, dev = cw + t - 1, left
            fetch(len(arrivals))
            back(0, target)
            back(1, target)
            if t == 1:
                src = b_buf.at[:, target]
            else:
                arrivals[(way, t - 1)].wait_recv()
                ring_out[slot] = ring_in[slot - 1] + b_buf[:, target]
                src = ring_out.at[slot]
            c = remote(src, ring_in.at[slot], ring_send.at[slot], ring_recv.at[slot], dev)
            c.start()
            sends.append(c)
            arrivals[(way, t)] = c

    def col_step(o):
        dev = cols[o - 1]
        col_copies[o - 1].wait_recv()
        stage[o - 1] = p_ref[dev[1] // half, lax.rem(dev[1], half)] + pre[o - 1]
        c = remote(stage.at[o - 1], recv_f.at[o - 1], col_send.at[chips + o - 1], col_recv.at[chips + o - 1], dev)
        c.start()
        col_copies.append(c)

    for n in range(max(cw, chips - 1)):
        if n < cw:
            ring_step(n + 1)
        if n == 0:
            for c in col_copies:
                c.start()
        if n < chips - 1:
            col_step(n + 1)
    fetch(len(need) - 1)
    back(0, z)
    back(1, z)
    col_copies[chips - 1].wait_recv()
    arrivals[(0, cw)].wait_recv()
    arrivals[(1, ccw)].wait_recv()
    away = 1 - xh
    x_out[...] = ring_in[cw - 1, away] + ring_in[cw + ccw - 1, away] + b_buf[away, z]
    cross = remote(x_out, x_in, ring_send.at[half - 1], ring_recv.at[half - 1], partner)
    cross.start()
    for c in sends:
        c.wait_send()
    for c in col_copies:
        c.wait_send()
    for c in col_copies[chips:]:
        c.wait_recv()
    cross.wait()
    acc = ring_in[cw - 1, xh] + ring_in[cw + ccw - 1, xh] + b_buf[xh, z] + x_in[...] + p_ref[j // half, lax.rem(j, half)] + pre[chips - 1]
    for n in range(chips - 1):
        acc = acc + recv_f[n]
    out_ref[...] = acc.astype(out_ref.dtype)


def scatter_sum(partial, slab, near_local, far_local, near_tiles, far_left, far_right, nr, nc):
    tile = partial.shape[2:]
    half = nr // 2
    cw = half // 2
    steps = half - 1
    vmem = pltpu.VMEM
    return pl.pallas_call(
        functools.partial(scatter_kernel, nr, nc),
        out_shape=jax.ShapeDtypeStruct(tile, jnp.bfloat16),
        in_specs=[pl.BlockSpec(memory_space=pltpu.SMEM)] * 2
        + [pl.BlockSpec(memory_space=vmem)] * 2
        + [pl.BlockSpec(memory_space=pl.ANY)] * 3,
        out_specs=pl.BlockSpec(memory_space=vmem),
        scratch_shapes=[
            vmem(near_tiles.shape, near_tiles.dtype),
            vmem(far_left.shape, far_left.dtype),
            vmem(far_right.shape, far_right.dtype),
            vmem((2, half) + tile, jnp.float32),
            vmem((DPC * TILE, NRHS), jnp.bfloat16),
            vmem((LPC * RANK, NRHS), jnp.bfloat16),
            vmem((nc // 2 - 1,) + tile, jnp.float32),
            vmem((nc // 2,) + tile, jnp.float32),
            vmem((nc // 2 - 1,) + tile, jnp.float32),
            vmem((steps, 2) + tile, jnp.float32),
            vmem((steps, 2) + tile, jnp.float32),
            vmem(tile, jnp.float32),
            vmem(tile, jnp.float32),
            pltpu.SemaphoreType.DMA((nc - 1,)),
            pltpu.SemaphoreType.DMA((nc - 1,)),
            pltpu.SemaphoreType.DMA((half,)),
            pltpu.SemaphoreType.DMA((half,)),
            pltpu.SemaphoreType.DMA((half, 2, 3)),
        ],
        compiler_params=pltpu.CompilerParams(
            collective_id=1, has_side_effects=True, vmem_limit_bytes=60 * 1024 * 1024),
    )(near_local, far_local, partial, slab.reshape((-1,) + tile), near_tiles, far_left, far_right)


def per_device(panel_values, near_tiles, far_left, far_right, near_rows, far_rows):
    n_row = lax.axis_size("row")
    n_col = lax.axis_size("col")
    clusters = panel_values.shape[0] // TILE
    groups = n_col * clusters
    colcount = n_row * clusters
    row_base = lax.axis_index("row") * groups
    near_local = near_rows - row_base
    far_local = far_rows - row_base
    slab = gather_slabs(panel_values, n_row, n_col)
    partial = local_products(near_local, far_local, near_tiles, far_left, far_right, slab, colcount, groups)
    return scatter_sum(partial, slab, near_local, far_local, near_tiles, far_left, far_right, n_row, n_col)


def solution(mesh):
    placed = (
        P(("row", "col"), None),
        P(("row", "col"), None, None),
        P(("row", "col"), None, None),
        P(("row", "col"), None, None),
        P(("row", "col")),
        P(("row", "col")),
    )
    return jax.shard_map(
        per_device, mesh=mesh, in_specs=placed, out_specs=P(("row", "col"), None), check_vma=False
    )
```

```python
import functools

import jax
import jax.numpy as jnp
from jax import lax
from jax.experimental import pallas as pl
from jax.experimental.pallas import tpu as pltpu
from jax.sharding import PartitionSpec as P

TILE = 256
RANK = 64
NRHS = 256
DPC = 2
LPC = 8

TN = (((0,), (0,)), ((), ()))


def local_kernel(half, per, near_idx, far_idx, tiles_ref, left_ref, right_ref, slab_ref, out_ref):
    step = pl.program_id(0)
    base = slab_ref.shape[0] - 2

    @pl.when(step == 0)
    def _():
        out_ref[...] = jnp.zeros_like(out_ref)

    for kk in range(per):
        k = step * per + kk
        xc = slab_ref[base + k // half, lax.rem(k, half)]
        tiles = tiles_ref[kk * DPC:(kk + 1) * DPC].reshape(DPC * TILE, TILE)
        near_f = jnp.dot(tiles, xc, preferred_element_type=jnp.float32)
        for d in range(DPC):
            r = near_idx[k * DPC + d]
            out_ref[r // half, lax.rem(r, half)] += near_f[d * TILE:(d + 1) * TILE]
        right = right_ref[kk * LPC:(kk + 1) * LPC].reshape(LPC * RANK, TILE)
        coef = jnp.dot(right, xc, preferred_element_type=jnp.float32).astype(jnp.bfloat16)
        for d in range(LPC):
            r = far_idx[k * LPC + d]
            out_ref[r // half, lax.rem(r, half)] += lax.dot_general(
                left_ref[kk * LPC + d], coef[d * RANK:(d + 1) * RANK], TN, preferred_element_type=jnp.float32)


def local_products(near_local, far_local, near_tiles, far_left, far_right, slab, count, groups):
    half = slab.shape[1]
    per = 4 if count % 4 == 0 else 1
    grid_spec = pltpu.PrefetchScalarGridSpec(
        num_scalar_prefetch=2,
        grid=(count // per,),
        in_specs=[
            pl.BlockSpec((per * DPC, TILE, TILE), lambda k, a, b: (k, 0, 0)),
            pl.BlockSpec((per * LPC, RANK, TILE), lambda k, a, b: (k, 0, 0)),
            pl.BlockSpec((per * LPC, RANK, TILE), lambda k, a, b: (k, 0, 0)),
            pl.BlockSpec(memory_space=pltpu.VMEM),
        ],
        out_specs=pl.BlockSpec(memory_space=pltpu.VMEM),
    )
    flops = 2 * TILE * TILE * NRHS * near_tiles.shape[0] + 2 * RANK * TILE * NRHS * far_left.shape[0] * 2
    return pl.pallas_call(
        functools.partial(local_kernel, half, per),
        grid_spec=grid_spec,
        out_shape=jax.ShapeDtypeStruct((groups // half, half, TILE, NRHS), jnp.float32),
        compiler_params=pltpu.CompilerParams(
            dimension_semantics=("arbitrary",), vmem_limit_bytes=48 * 1024 * 1024
        ),
        cost_estimate=pl.CostEstimate(flops=flops, bytes_accessed=16 * 1024 * 1024, transcendentals=0),
    )(near_local, far_local, near_tiles, far_left, far_right, slab)


MESH_ID = pl.DeviceIdType.MESH


def layout(nr, nc):
    i = lax.axis_index("row")
    j = lax.axis_index("col")
    half = nr // 2
    xh = i // half
    z = lax.rem(i, half)
    chips = nc // 2
    core = lax.rem(j, 2)
    chip = j // 2
    cols = [(i, 2 * lax.rem(chip + o, chips) + core) for o in range(1, chips)]
    cols.append((i, 2 * chip + 1 - core))
    right = (xh * half + lax.rem(z + 1, half), j)
    left = (xh * half + lax.rem(z + half - 1, half), j)
    partner = (lax.rem(i + half, nr), j)
    return i, j, half, xh, z, cols, right, left, partner


def enter(devices):
    barrier = pltpu.get_barrier_semaphore()
    for dev in devices:
        pl.semaphore_signal(barrier, 1, device_id=dev, device_id_type=MESH_ID)
    pl.semaphore_wait(barrier, len(devices))


def remote(src, dst, ssem, rsem, dev):
    return pltpu.make_async_remote_copy(src, dst, ssem, rsem, device_id=dev, device_id_type=MESH_ID)


def gather_kernel(nr, nc, x_ref, slab_ref, col_send, col_recv, ring_send, ring_recv, local_sem):
    i, j, half, xh, z, cols, right, left, partner = layout(nr, nc)
    cw = half // 2
    ccw = half - 1 - cw
    enter(cols + [right, left, partner])
    chips = nc // 2
    core = lax.rem(j, 2)
    chip = j // 2
    base = nc // half
    mine = slab_ref.at[j // half, lax.rem(j, half)]
    other = remote(x_ref, slab_ref.at[base + xh, z], ring_send.at[0], ring_recv.at[0], partner)
    other.start()
    col_copies = [remote(x_ref, mine, col_send.at[n], col_recv.at[n], dev) for n, dev in enumerate(cols)]
    for c in col_copies:
        c.start()
    own_row = pltpu.make_async_copy(x_ref, mine, local_sem.at[0])
    own_col = pltpu.make_async_copy(x_ref, slab_ref.at[base + xh, z], local_sem.at[1])
    own_row.start()
    own_col.start()
    mate = cols[-1]
    ring = []
    state = {}

    def ring_step(t):
        if t == 1:
            own_col.wait()
            other.wait()
        for way in range(2):
            if way == 1 and t > ccw:
                continue
            if way == 0:
                origin = lax.rem(z - t + 1 + half, half)
                sem, dev = t, right
            else:
                origin = lax.rem(z + t - 1, half)
                sem, dev = cw + t, left
            if t > 1:
                state[way].wait_recv()
            c = remote(slab_ref.at[base:base + 2, origin], slab_ref.at[base:base + 2, origin], ring_send.at[sem], ring_recv.at[sem], dev)
            c.start()
            ring.append(c)
            state[way] = c

    def col_step(o):
        origin = 2 * lax.rem(chip + chips - o, chips) + core
        col_copies[o - 1].wait_recv()
        c = remote(slab_ref.at[origin // half, lax.rem(origin, half)], slab_ref.at[origin // half, lax.rem(origin, half)], col_send.at[chips + o - 1],
                   col_recv.at[chips + o - 1], mate)
        c.start()
        col_copies.append(c)

    for n in range(max(cw, chips - 1)):
        if n < cw:
            ring_step(n + 1)
        if n < chips - 1:
            col_step(n + 1)
    for c in ring:
        c.wait_send()
    state[0].wait_recv()
    state[1].wait_recv()
    for c in col_copies:
        c.wait_send()
    for c in col_copies[chips - 1:]:
        c.wait_recv()
    own_row.wait()


def gather_slabs(x, nr, nc):
    tile = x.shape
    half = nr // 2
    return pl.pallas_call(
        functools.partial(gather_kernel, nr, nc),
        out_shape=jax.ShapeDtypeStruct((nc // half + 2, half) + tile, x.dtype),
        in_specs=[pl.BlockSpec(memory_space=pl.ANY)],
        out_specs=pl.BlockSpec(memory_space=pltpu.VMEM),
        scratch_shapes=[
            pltpu.SemaphoreType.DMA((nc - 1,)),
            pltpu.SemaphoreType.DMA((nc - 1,)),
            pltpu.SemaphoreType.DMA((half,)),
            pltpu.SemaphoreType.DMA((half,)),
            pltpu.SemaphoreType.DMA((2,)),
        ],
        compiler_params=pltpu.CompilerParams(collective_id=0, has_side_effects=True),
    )(x)


def scatter_kernel(nr, nc, near_idx, far_idx, p_ref, slab_ref, tiles_hbm, left_hbm, right_hbm, out_ref,
                   tiles_v, left_v, right_v, b_buf, near_x, far_t, recv_f, pre, stage, ring_in, ring_out, x_in, x_out,
                   col_send, col_recv, ring_send, ring_recv, local_sem):
    i, j, half, xh, z, cols, right, left, partner = layout(nr, nc)
    cw = half // 2
    ccw = half - 1 - cw
    loads = [pltpu.make_async_copy(src, dst, local_sem.at[n])
             for n, (src, dst) in enumerate([(tiles_hbm, tiles_v), (right_hbm, right_v), (left_hbm, left_v)])]
    for c in loads:
        c.start()
    enter(cols + [right, left, partner])
    chips = nc // 2
    core = lax.rem(j, 2)
    chip = j // 2
    mate = cols[-1]
    handed = [2 * lax.rem(chip + o, chips) + 1 - core for o in range(1, chips)] + [mate[1]]
    col_copies = [remote(p_ref.at[m // half, lax.rem(m, half)], pre.at[n], col_send.at[n], col_recv.at[n], mate) for n, m in enumerate(handed)]
    for c in col_copies:
        c.start()
    sends = []
    arrivals = {}
    for c in loads:
        c.wait()

    def back(xhp, target):
        k = xhp * half + target
        tiles = tiles_v[pl.ds(k * DPC, DPC)].reshape(DPC * TILE, TILE)
        for d in range(DPC):
            near_x[d * TILE:(d + 1) * TILE] = slab_ref[near_idx[k * DPC + d]]
        rfac = right_v[pl.ds(k * LPC, LPC)].reshape(LPC * RANK, TILE)
        for d in range(LPC):
            far_t[d * RANK:(d + 1) * RANK] = jnp.dot(
                left_v[k * LPC + d], slab_ref[far_idx[k * LPC + d]], preferred_element_type=jnp.float32
            ).astype(jnp.bfloat16)
        acc = lax.dot_general(tiles, near_x[...], TN, preferred_element_type=jnp.float32)
        acc += lax.dot_general(rfac, far_t[...], TN, preferred_element_type=jnp.float32)
        b_buf[xhp, target] = acc

    h2 = TILE // 2
    chains = [(right, cw, 1, 0), (left, ccw, -1, 0), (right, ccw, 1, h2), (left, cw, -1, h2)]
    slots = {}
    for t in range(1, cw + 1):
        for c, (dev, length, sign, row) in enumerate(chains):
            if t <= length:
                slots[(c, t)] = len(slots)
    ready = set()

    def ensure(off):
        if off % half not in ready:
            ready.add(off % half)
            target = lax.rem(z + off + half, half)
            back(0, target)
            back(1, target)

    def ring_step(t):
        for c, (dev, length, sign, row) in enumerate(chains):
            if t > length:
                continue
            off = sign * (length + 1 - t)
            ensure(off)
            target = lax.rem(z + off + half, half)
            slot = slots[(c, t)]
            rows = pl.ds(row, h2)
            if t == 1:
                src = b_buf.at[:, target, rows]
            else:
                arrivals[(c, t - 1)].wait_recv()
                ring_out[slot] = ring_in[slots[(c, t - 1)]] + b_buf[:, target, rows]
                src = ring_out.at[slot]
            cp = remote(src, ring_in.at[slot], ring_send.at[slot], ring_recv.at[slot], dev)
            cp.start()
            sends.append(cp)
            arrivals[(c, t)] = cp

    def col_step(o):
        dev = cols[o - 1]
        col_copies[o - 1].wait_recv()
        stage[o - 1] = p_ref[dev[1] // half, lax.rem(dev[1], half)] + pre[o - 1]
        c = remote(stage.at[o - 1], recv_f.at[o - 1], col_send.at[chips + o - 1], col_recv.at[chips + o - 1], dev)
        c.start()
        col_copies.append(c)

    for n in range(max(cw, chips - 1)):
        if n < cw:
            ring_step(n + 1)
        if n < chips - 1:
            col_step(n + 1)
    ensure(0)
    col_copies[chips - 1].wait_recv()
    lasts = []
    for c, (dev, length, sign, row) in enumerate(chains):
        arrivals[(c, length)].wait_recv()
        lasts.append(slots[(c, length)])
    away = 1 - xh
    for half_rows, (p, q) in enumerate([(lasts[0], lasts[1]), (lasts[2], lasts[3])]):
        rows = slice(half_rows * h2, (half_rows + 1) * h2)
        x_out[rows] = ring_in[p, away] + ring_in[q, away] + b_buf[away, z, rows]
    nsem = len(slots)
    cross = remote(x_out, x_in, ring_send.at[nsem], ring_recv.at[nsem], partner)
    cross.start()
    for c in sends:
        c.wait_send()
    for c in col_copies:
        c.wait_send()
    for c in col_copies[chips:]:
        c.wait_recv()
    cross.wait()
    ring_sum = jnp.concatenate(
        [ring_in[lasts[0], xh] + ring_in[lasts[1], xh], ring_in[lasts[2], xh] + ring_in[lasts[3], xh]], axis=0)
    acc = ring_sum + b_buf[xh, z] + x_in[...] + p_ref[j // half, lax.rem(j, half)] + pre[chips - 1]
    for n in range(chips - 1):
        acc = acc + recv_f[n]
    out_ref[...] = acc.astype(out_ref.dtype)


def scatter_sum(partial, slab, near_local, far_local, near_tiles, far_left, far_right, nr, nc):
    tile = partial.shape[2:]
    half = nr // 2
    cw = half // 2
    steps = half - 1
    vmem = pltpu.VMEM
    return pl.pallas_call(
        functools.partial(scatter_kernel, nr, nc),
        out_shape=jax.ShapeDtypeStruct(tile, jnp.bfloat16),
        in_specs=[pl.BlockSpec(memory_space=pltpu.SMEM)] * 2
        + [pl.BlockSpec(memory_space=vmem)] * 2
        + [pl.BlockSpec(memory_space=pl.ANY)] * 3,
        out_specs=pl.BlockSpec(memory_space=vmem),
        scratch_shapes=[
            vmem(near_tiles.shape, near_tiles.dtype),
            vmem(far_left.shape, far_left.dtype),
            vmem(far_right.shape, far_right.dtype),
            vmem((2, half) + tile, jnp.float32),
            vmem((DPC * TILE, NRHS), jnp.bfloat16),
            vmem((LPC * RANK, NRHS), jnp.bfloat16),
            vmem((nc // 2 - 1,) + tile, jnp.float32),
            vmem((nc // 2,) + tile, jnp.float32),
            vmem((nc // 2 - 1,) + tile, jnp.float32),
            vmem((2 * steps, 2, tile[0] // 2, tile[1]), jnp.float32),
            vmem((2 * steps, 2, tile[0] // 2, tile[1]), jnp.float32),
            vmem(tile, jnp.float32),
            vmem(tile, jnp.float32),
            pltpu.SemaphoreType.DMA((nc - 1,)),
            pltpu.SemaphoreType.DMA((nc - 1,)),
            pltpu.SemaphoreType.DMA((2 * steps + 1,)),
            pltpu.SemaphoreType.DMA((2 * steps + 1,)),
            pltpu.SemaphoreType.DMA((3,)),
        ],
        compiler_params=pltpu.CompilerParams(
            collective_id=1, has_side_effects=True, vmem_limit_bytes=60 * 1024 * 1024),
    )(near_local, far_local, partial, slab.reshape((-1,) + tile), near_tiles, far_left, far_right)


def per_device(panel_values, near_tiles, far_left, far_right, near_rows, far_rows):
    n_row = lax.axis_size("row")
    n_col = lax.axis_size("col")
    clusters = panel_values.shape[0] // TILE
    groups = n_col * clusters
    colcount = n_row * clusters
    row_base = lax.axis_index("row") * groups
    near_local = near_rows - row_base
    far_local = far_rows - row_base
    slab = gather_slabs(panel_values, n_row, n_col)
    partial = local_products(near_local, far_local, near_tiles, far_left, far_right, slab, colcount, groups)
    return scatter_sum(partial, slab, near_local, far_local, near_tiles, far_left, far_right, n_row, n_col)


def solution(mesh):
    placed = (
        P(("row", "col"), None),
        P(("row", "col"), None, None),
        P(("row", "col"), None, None),
        P(("row", "col"), None, None),
        P(("row", "col")),
        P(("row", "col")),
    )
    return jax.shard_map(
        per_device, mesh=mesh, in_specs=placed, out_specs=P(("row", "col"), None), check_vma=False
    )
```

```python
import functools

import jax
import jax.numpy as jnp
from jax import lax
from jax.experimental import pallas as pl
from jax.experimental.pallas import tpu as pltpu
from jax.sharding import PartitionSpec as P

TILE = 256
RANK = 64
NRHS = 256
DPC = 2
LPC = 8

TN = (((0,), (0,)), ((), ()))


def local_kernel(half, per, near_idx, far_idx, tiles_ref, left_ref, right_ref, slab_ref, out_ref):
    step = pl.program_id(0)
    base = slab_ref.shape[0] - 2

    @pl.when(step == 0)
    def _():
        out_ref[...] = jnp.zeros_like(out_ref)

    for kk in range(per):
        k = step * per + kk
        xc = slab_ref[base + k // half, lax.rem(k, half)]
        tiles = tiles_ref[kk * DPC:(kk + 1) * DPC].reshape(DPC * TILE, TILE)
        near_f = jnp.dot(tiles, xc, preferred_element_type=jnp.float32)
        for d in range(DPC):
            r = near_idx[k * DPC + d]
            out_ref[r // half, lax.rem(r, half)] += near_f[d * TILE:(d + 1) * TILE]
        right = right_ref[kk * LPC:(kk + 1) * LPC].reshape(LPC * RANK, TILE)
        coef = jnp.dot(right, xc, preferred_element_type=jnp.float32).astype(jnp.bfloat16)
        for d in range(LPC):
            r = far_idx[k * LPC + d]
            out_ref[r // half, lax.rem(r, half)] += lax.dot_general(
                left_ref[kk * LPC + d], coef[d * RANK:(d + 1) * RANK], TN, preferred_element_type=jnp.float32)


def local_products(near_local, far_local, near_tiles, far_left, far_right, slab, count, groups):
    half = slab.shape[1]
    per = 4 if count % 4 == 0 else 1
    grid_spec = pltpu.PrefetchScalarGridSpec(
        num_scalar_prefetch=2,
        grid=(count // per,),
        in_specs=[
            pl.BlockSpec((per * DPC, TILE, TILE), lambda k, a, b: (k, 0, 0)),
            pl.BlockSpec((per * LPC, RANK, TILE), lambda k, a, b: (k, 0, 0)),
            pl.BlockSpec((per * LPC, RANK, TILE), lambda k, a, b: (k, 0, 0)),
            pl.BlockSpec(memory_space=pltpu.VMEM),
        ],
        out_specs=pl.BlockSpec(memory_space=pltpu.VMEM),
    )
    flops = 2 * TILE * TILE * NRHS * near_tiles.shape[0] + 2 * RANK * TILE * NRHS * far_left.shape[0] * 2
    return pl.pallas_call(
        functools.partial(local_kernel, half, per),
        grid_spec=grid_spec,
        out_shape=jax.ShapeDtypeStruct((groups // half, half, TILE, NRHS), jnp.float32),
        compiler_params=pltpu.CompilerParams(
            dimension_semantics=("arbitrary",), vmem_limit_bytes=48 * 1024 * 1024
        ),
        cost_estimate=pl.CostEstimate(flops=flops, bytes_accessed=16 * 1024 * 1024, transcendentals=0),
    )(near_local, far_local, near_tiles, far_left, far_right, slab)


MESH_ID = pl.DeviceIdType.MESH


def layout(nr, nc):
    i = lax.axis_index("row")
    j = lax.axis_index("col")
    half = nr // 2
    xh = i // half
    z = lax.rem(i, half)
    chips = nc // 2
    core = lax.rem(j, 2)
    chip = j // 2
    cols = [(i, 2 * lax.rem(chip + o, chips) + core) for o in range(1, chips)]
    cols.append((i, 2 * chip + 1 - core))
    right = (xh * half + lax.rem(z + 1, half), j)
    left = (xh * half + lax.rem(z + half - 1, half), j)
    partner = (lax.rem(i + half, nr), j)
    return i, j, half, xh, z, cols, right, left, partner


def enter(devices):
    barrier = pltpu.get_barrier_semaphore()
    for dev in devices:
        pl.semaphore_signal(barrier, 1, device_id=dev, device_id_type=MESH_ID)
    pl.semaphore_wait(barrier, len(devices))


def remote(src, dst, ssem, rsem, dev):
    return pltpu.make_async_remote_copy(src, dst, ssem, rsem, device_id=dev, device_id_type=MESH_ID)


def gather_kernel(nr, nc, x_ref, slab_ref, col_send, col_recv, ring_send, ring_recv, local_sem):
    i, j, half, xh, z, cols, right, left, partner = layout(nr, nc)
    cw = half // 2
    ccw = half - 1 - cw
    enter(cols + [right, left, partner])
    chips = nc // 2
    core = lax.rem(j, 2)
    chip = j // 2
    base = nc // half
    mine = slab_ref.at[j // half, lax.rem(j, half)]
    other = remote(x_ref, slab_ref.at[base + xh, z], ring_send.at[0], ring_recv.at[0], partner)
    other.start()
    col_copies = [remote(x_ref, mine, col_send.at[n], col_recv.at[n], dev) for n, dev in enumerate(cols)]
    for c in col_copies:
        c.start()
    own_row = pltpu.make_async_copy(x_ref, mine, local_sem.at[0])
    own_col = pltpu.make_async_copy(x_ref, slab_ref.at[base + xh, z], local_sem.at[1])
    own_row.start()
    own_col.start()
    mate = cols[-1]
    ring = []
    state = {}

    def ring_step(t):
        if t == 1:
            own_col.wait()
            other.wait()
        for way in range(2):
            if way == 1 and t > ccw:
                continue
            if way == 0:
                origin = lax.rem(z - t + 1 + half, half)
                sem, dev = t, right
            else:
                origin = lax.rem(z + t - 1, half)
                sem, dev = cw + t, left
            if t > 1:
                state[way].wait_recv()
            c = remote(slab_ref.at[base:base + 2, origin], slab_ref.at[base:base + 2, origin], ring_send.at[sem], ring_recv.at[sem], dev)
            c.start()
            ring.append(c)
            state[way] = c

    def col_step(o):
        origin = 2 * lax.rem(chip + chips - o, chips) + core
        col_copies[o - 1].wait_recv()
        c = remote(slab_ref.at[origin // half, lax.rem(origin, half)], slab_ref.at[origin // half, lax.rem(origin, half)], col_send.at[chips + o - 1],
                   col_recv.at[chips + o - 1], mate)
        c.start()
        col_copies.append(c)

    for n in range(max(cw, chips - 1)):
        if n < cw:
            ring_step(n + 1)
        if n < chips - 1:
            col_step(n + 1)
    for c in ring:
        c.wait_send()
    state[0].wait_recv()
    state[1].wait_recv()
    for c in col_copies:
        c.wait_send()
    for c in col_copies[chips - 1:]:
        c.wait_recv()
    own_row.wait()


def gather_slabs(x, nr, nc):
    tile = x.shape
    half = nr // 2
    return pl.pallas_call(
        functools.partial(gather_kernel, nr, nc),
        out_shape=jax.ShapeDtypeStruct((nc // half + 2, half) + tile, x.dtype),
        in_specs=[pl.BlockSpec(memory_space=pl.ANY)],
        out_specs=pl.BlockSpec(memory_space=pltpu.VMEM),
        scratch_shapes=[
            pltpu.SemaphoreType.DMA((nc - 1,)),
            pltpu.SemaphoreType.DMA((nc - 1,)),
            pltpu.SemaphoreType.DMA((half,)),
            pltpu.SemaphoreType.DMA((half,)),
            pltpu.SemaphoreType.DMA((2,)),
        ],
        compiler_params=pltpu.CompilerParams(collective_id=0, has_side_effects=True),
    )(x)


def scatter_kernel(nr, nc, near_idx, far_idx, p_ref, slab_ref, tiles_hbm, left_hbm, right_hbm, out_ref,
                   tiles_v, left_v, right_v, b_buf, near_x, far_t, recv_f, pre, stage, ring_in, ring_out, x_in, x_out,
                   col_send, col_recv, ring_send, ring_recv, local_sem):
    i, j, half, xh, z, cols, right, left, partner = layout(nr, nc)
    cw = half // 2
    ccw = half - 1 - cw
    loads = [pltpu.make_async_copy(src, dst, local_sem.at[n])
             for n, (src, dst) in enumerate([(tiles_hbm, tiles_v), (right_hbm, right_v), (left_hbm, left_v)])]
    for c in loads:
        c.start()
    enter(cols + [right, left, partner])
    chips = nc // 2
    core = lax.rem(j, 2)
    chip = j // 2
    mate = cols[-1]
    handed = [2 * lax.rem(chip + o, chips) + 1 - core for o in range(1, chips)] + [mate[1]]
    col_copies = [remote(p_ref.at[m // half, lax.rem(m, half)], pre.at[n], col_send.at[n], col_recv.at[n], mate) for n, m in enumerate(handed)]
    for c in col_copies:
        c.start()
    sends = []
    arrivals = {}
    for c in loads:
        c.wait()

    def back(xhp, target):
        k = xhp * half + target
        tiles = tiles_v[pl.ds(k * DPC, DPC)].reshape(DPC * TILE, TILE)
        for d in range(DPC):
            near_x[d * TILE:(d + 1) * TILE] = slab_ref[near_idx[k * DPC + d]]
        rfac = right_v[pl.ds(k * LPC, LPC)].reshape(LPC * RANK, TILE)
        for d in range(LPC):
            far_t[d * RANK:(d + 1) * RANK] = jnp.dot(
                left_v[k * LPC + d], slab_ref[far_idx[k * LPC + d]], preferred_element_type=jnp.float32
            ).astype(jnp.bfloat16)
        acc = lax.dot_general(tiles, near_x[...], TN, preferred_element_type=jnp.float32)
        acc += lax.dot_general(rfac, far_t[...], TN, preferred_element_type=jnp.float32)
        b_buf[xhp, target] = acc

    def ring_step(t):
        for way in range(2):
            if way == 1 and t > ccw:
                continue
            if way == 0:
                target = lax.rem(z + cw + 1 - t, half)
                slot, dev = t - 1, right
            else:
                target = lax.rem(z + half - (ccw + 1 - t), half)
                slot, dev = cw + t - 1, left
            back(0, target)
            back(1, target)
            if t == 1:
                src = b_buf.at[:, target]
            else:
                arrivals[(way, t - 1)].wait_recv()
                ring_out[slot] = ring_in[slot - 1] + b_buf[:, target]
                src = ring_out.at[slot]
            c = remote(src, ring_in.at[slot], ring_send.at[slot], ring_recv.at[slot], dev)
            c.start()
            sends.append(c)
            arrivals[(way, t)] = c

    def col_step(o):
        dev = cols[o - 1]
        col_copies[o - 1].wait_recv()
        stage[o - 1] = p_ref[dev[1] // half, lax.rem(dev[1], half)] + pre[o - 1]
        c = remote(stage.at[o - 1], recv_f.at[o - 1], col_send.at[chips + o - 1], col_recv.at[chips + o - 1], dev)
        c.start()
        col_copies.append(c)

    for n in range(max(cw, chips - 1)):
        if n < cw:
            ring_step(n + 1)
        if n < chips - 1:
            col_step(n + 1)
    back(0, z)
    back(1, z)
    col_copies[chips - 1].wait_recv()
    arrivals[(0, cw)].wait_recv()
    arrivals[(1, ccw)].wait_recv()
    away = 1 - xh
    x_out[...] = ring_in[cw - 1, away] + ring_in[cw + ccw - 1, away] + b_buf[away, z]
    cross = remote(x_out, x_in, ring_send.at[half - 1], ring_recv.at[half - 1], partner)
    cross.start()
    for c in sends:
        c.wait_send()
    for c in col_copies:
        c.wait_send()
    for c in col_copies[chips:]:
        c.wait_recv()
    cross.wait()
    acc = ring_in[cw - 1, xh] + ring_in[cw + ccw - 1, xh] + b_buf[xh, z] + x_in[...] + p_ref[j // half, lax.rem(j, half)] + pre[chips - 1]
    for n in range(chips - 1):
        acc = acc + recv_f[n]
    out_ref[...] = acc.astype(out_ref.dtype)


def scatter_sum(partial, slab, near_local, far_local, near_tiles, far_left, far_right, nr, nc):
    tile = partial.shape[2:]
    half = nr // 2
    cw = half // 2
    steps = half - 1
    vmem = pltpu.VMEM
    return pl.pallas_call(
        functools.partial(scatter_kernel, nr, nc),
        out_shape=jax.ShapeDtypeStruct(tile, jnp.bfloat16),
        in_specs=[pl.BlockSpec(memory_space=pltpu.SMEM)] * 2
        + [pl.BlockSpec(memory_space=vmem)] * 2
        + [pl.BlockSpec(memory_space=pl.ANY)] * 3,
        out_specs=pl.BlockSpec(memory_space=vmem),
        scratch_shapes=[
            vmem(near_tiles.shape, near_tiles.dtype),
            vmem(far_left.shape, far_left.dtype),
            vmem(far_right.shape, far_right.dtype),
            vmem((2, half) + tile, jnp.float32),
            vmem((DPC * TILE, NRHS), jnp.bfloat16),
            vmem((LPC * RANK, NRHS), jnp.bfloat16),
            vmem((nc // 2 - 1,) + tile, jnp.float32),
            vmem((nc // 2,) + tile, jnp.float32),
            vmem((nc // 2 - 1,) + tile, jnp.float32),
            vmem((steps, 2) + tile, jnp.float32),
            vmem((steps, 2) + tile, jnp.float32),
            vmem(tile, jnp.float32),
            vmem(tile, jnp.float32),
            pltpu.SemaphoreType.DMA((nc - 1,)),
            pltpu.SemaphoreType.DMA((nc - 1,)),
            pltpu.SemaphoreType.DMA((half,)),
            pltpu.SemaphoreType.DMA((half,)),
            pltpu.SemaphoreType.DMA((3,)),
        ],
        compiler_params=pltpu.CompilerParams(
            collective_id=1, has_side_effects=True, vmem_limit_bytes=40 * 1024 * 1024),
    )(near_local, far_local, partial, slab.reshape((-1,) + tile), near_tiles, far_left, far_right)


def per_device(panel_values, near_tiles, far_left, far_right, near_rows, far_rows):
    n_row = lax.axis_size("row")
    n_col = lax.axis_size("col")
    clusters = panel_values.shape[0] // TILE
    groups = n_col * clusters
    colcount = n_row * clusters
    row_base = lax.axis_index("row") * groups
    near_local = near_rows - row_base
    far_local = far_rows - row_base
    slab = gather_slabs(panel_values, n_row, n_col)
    partial = local_products(near_local, far_local, near_tiles, far_left, far_right, slab, colcount, groups)
    return scatter_sum(partial, slab, near_local, far_local, near_tiles, far_left, far_right, n_row, n_col)


def solution(mesh):
    placed = (
        P(("row", "col"), None),
        P(("row", "col"), None, None),
        P(("row", "col"), None, None),
        P(("row", "col"), None, None),
        P(("row", "col")),
        P(("row", "col")),
    )
    return jax.shard_map(
        per_device, mesh=mesh, in_specs=placed, out_specs=P(("row", "col"), None), check_vma=False
    )
```

```python
import functools

import jax
import jax.numpy as jnp
from jax import lax
from jax.experimental import pallas as pl
from jax.experimental.pallas import tpu as pltpu
from jax.sharding import PartitionSpec as P

TILE = 256
RANK = 64
NRHS = 256
DPC = 2
LPC = 8

TN = (((0,), (0,)), ((), ()))


def local_kernel(half, per, near_idx, far_idx, tiles_ref, left_ref, right_ref, slab_ref, out_ref):
    step = pl.program_id(0)
    base = slab_ref.shape[0] - 2

    @pl.when(step == 0)
    def _():
        out_ref[...] = jnp.zeros_like(out_ref)

    for kk in range(per):
        k = step * per + kk
        xc = slab_ref[base + k // half, lax.rem(k, half)]
        tiles = tiles_ref[kk * DPC:(kk + 1) * DPC].reshape(DPC * TILE, TILE)
        near_f = jnp.dot(tiles, xc, preferred_element_type=jnp.float32)
        for d in range(DPC):
            r = near_idx[k * DPC + d]
            out_ref[r // half, lax.rem(r, half)] += near_f[d * TILE:(d + 1) * TILE]
        right = right_ref[kk * LPC:(kk + 1) * LPC].reshape(LPC * RANK, TILE)
        coef = jnp.dot(right, xc, preferred_element_type=jnp.float32).astype(jnp.bfloat16)
        for d in range(LPC):
            r = far_idx[k * LPC + d]
            out_ref[r // half, lax.rem(r, half)] += lax.dot_general(
                left_ref[kk * LPC + d], coef[d * RANK:(d + 1) * RANK], TN, preferred_element_type=jnp.float32)


def local_products(near_local, far_local, near_tiles, far_left, far_right, slab, count, groups):
    half = slab.shape[1]
    per = 4 if count % 4 == 0 else 1
    grid_spec = pltpu.PrefetchScalarGridSpec(
        num_scalar_prefetch=2,
        grid=(count // per,),
        in_specs=[
            pl.BlockSpec((per * DPC, TILE, TILE), lambda k, a, b: (k, 0, 0)),
            pl.BlockSpec((per * LPC, RANK, TILE), lambda k, a, b: (k, 0, 0)),
            pl.BlockSpec((per * LPC, RANK, TILE), lambda k, a, b: (k, 0, 0)),
            pl.BlockSpec(memory_space=pltpu.VMEM),
        ],
        out_specs=pl.BlockSpec(memory_space=pltpu.VMEM),
    )
    flops = 2 * TILE * TILE * NRHS * near_tiles.shape[0] + 2 * RANK * TILE * NRHS * far_left.shape[0] * 2
    return pl.pallas_call(
        functools.partial(local_kernel, half, per),
        grid_spec=grid_spec,
        out_shape=jax.ShapeDtypeStruct((groups // half, half, TILE, NRHS), jnp.float32),
        compiler_params=pltpu.CompilerParams(
            dimension_semantics=("arbitrary",), vmem_limit_bytes=24 * 1024 * 1024
        ),
        cost_estimate=pl.CostEstimate(flops=flops, bytes_accessed=16 * 1024 * 1024, transcendentals=0),
    )(near_local, far_local, near_tiles, far_left, far_right, slab)


MESH_ID = pl.DeviceIdType.MESH


def layout(nr, nc):
    i = lax.axis_index("row")
    j = lax.axis_index("col")
    half = nr // 2
    xh = i // half
    z = lax.rem(i, half)
    chips = nc // 2
    core = lax.rem(j, 2)
    chip = j // 2
    cols = [(i, 2 * lax.rem(chip + o, chips) + core) for o in range(1, chips)]
    cols.append((i, 2 * chip + 1 - core))
    right = (xh * half + lax.rem(z + 1, half), j)
    left = (xh * half + lax.rem(z + half - 1, half), j)
    partner = (lax.rem(i + half, nr), j)
    return i, j, half, xh, z, cols, right, left, partner


def enter(devices):
    barrier = pltpu.get_barrier_semaphore()
    for dev in devices:
        pl.semaphore_signal(barrier, 1, device_id=dev, device_id_type=MESH_ID)
    pl.semaphore_wait(barrier, len(devices))


def remote(src, dst, ssem, rsem, dev):
    return pltpu.make_async_remote_copy(src, dst, ssem, rsem, device_id=dev, device_id_type=MESH_ID)


def gather_kernel(nr, nc, x_ref, slab_ref, col_send, col_recv, ring_send, ring_recv, local_sem):
    i, j, half, xh, z, cols, right, left, partner = layout(nr, nc)
    cw = half // 2
    ccw = half - 1 - cw
    enter(cols + [right, left, partner])
    chips = nc // 2
    core = lax.rem(j, 2)
    chip = j // 2
    base = nc // half
    mine = slab_ref.at[j // half, lax.rem(j, half)]
    other = remote(x_ref, slab_ref.at[base + xh, z], ring_send.at[0], ring_recv.at[0], partner)
    other.start()
    col_copies = [remote(x_ref, mine, col_send.at[n], col_recv.at[n], dev) for n, dev in enumerate(cols)]
    for c in col_copies:
        c.start()
    own_row = pltpu.make_async_copy(x_ref, mine, local_sem.at[0])
    own_col = pltpu.make_async_copy(x_ref, slab_ref.at[base + xh, z], local_sem.at[1])
    own_row.start()
    own_col.start()
    mate = cols[-1]
    ring = []
    state = {}

    def ring_step(t):
        if t == 1:
            own_col.wait()
            other.wait()
        for way in range(2):
            if way == 1 and t > ccw:
                continue
            if way == 0:
                origin = lax.rem(z - t + 1 + half, half)
                sem, dev = t, right
            else:
                origin = lax.rem(z + t - 1, half)
                sem, dev = cw + t, left
            if t > 1:
                state[way].wait_recv()
            c = remote(slab_ref.at[base:base + 2, origin], slab_ref.at[base:base + 2, origin], ring_send.at[sem], ring_recv.at[sem], dev)
            c.start()
            ring.append(c)
            state[way] = c

    def col_step(o):
        origin = 2 * lax.rem(chip + chips - o, chips) + core
        col_copies[o - 1].wait_recv()
        c = remote(slab_ref.at[origin // half, lax.rem(origin, half)], slab_ref.at[origin // half, lax.rem(origin, half)], col_send.at[chips + o - 1],
                   col_recv.at[chips + o - 1], mate)
        c.start()
        col_copies.append(c)

    for n in range(max(cw, chips - 1)):
        if n < cw:
            ring_step(n + 1)
        if n < chips - 1:
            col_step(n + 1)
    for c in ring:
        c.wait_send()
    state[0].wait_recv()
    state[1].wait_recv()
    for c in col_copies:
        c.wait_send()
    for c in col_copies[chips - 1:]:
        c.wait_recv()
    own_row.wait()


def gather_slabs(x, nr, nc):
    tile = x.shape
    half = nr // 2
    return pl.pallas_call(
        functools.partial(gather_kernel, nr, nc),
        out_shape=jax.ShapeDtypeStruct((nc // half + 2, half) + tile, x.dtype),
        in_specs=[pl.BlockSpec(memory_space=pl.ANY)],
        out_specs=pl.BlockSpec(memory_space=pltpu.VMEM),
        scratch_shapes=[
            pltpu.SemaphoreType.DMA((nc - 1,)),
            pltpu.SemaphoreType.DMA((nc - 1,)),
            pltpu.SemaphoreType.DMA((half,)),
            pltpu.SemaphoreType.DMA((half,)),
            pltpu.SemaphoreType.DMA((2,)),
        ],
        compiler_params=pltpu.CompilerParams(
            collective_id=0, has_side_effects=True, vmem_limit_bytes=16 * 1024 * 1024),
    )(x)


def scatter_kernel(nr, nc, near_idx, far_idx, p_ref, slab_ref, tiles_hbm, left_hbm, right_hbm, out_ref,
                   tiles_v, left_v, right_v, b_buf, near_x, far_t, recv_f, pre, stage, ring_in, ring_out, x_in, x_out,
                   col_send, col_recv, ring_send, ring_recv, local_sem):
    i, j, half, xh, z, cols, right, left, partner = layout(nr, nc)
    cw = half // 2
    ccw = half - 1 - cw
    loads = [pltpu.make_async_copy(src, dst, local_sem.at[n])
             for n, (src, dst) in enumerate([(tiles_hbm, tiles_v), (right_hbm, right_v), (left_hbm, left_v)])]
    for c in loads:
        c.start()
    enter(cols + [right, left, partner])
    chips = nc // 2
    core = lax.rem(j, 2)
    chip = j // 2
    mate = cols[-1]
    handed = [2 * lax.rem(chip + o, chips) + 1 - core for o in range(1, chips)] + [mate[1]]
    col_copies = [remote(p_ref.at[m // half, lax.rem(m, half)], pre.at[n], col_send.at[n], col_recv.at[n], mate) for n, m in enumerate(handed)]
    for c in col_copies:
        c.start()
    sends = []
    arrivals = {}
    for c in loads:
        c.wait()

    def back(xhp, target):
        k = xhp * half + target
        tiles = tiles_v[pl.ds(k * DPC, DPC)].reshape(DPC * TILE, TILE)
        for d in range(DPC):
            near_x[d * TILE:(d + 1) * TILE] = slab_ref[near_idx[k * DPC + d]]
        rfac = right_v[pl.ds(k * LPC, LPC)].reshape(LPC * RANK, TILE)
        for d in range(LPC):
            far_t[d * RANK:(d + 1) * RANK] = jnp.dot(
                left_v[k * LPC + d], slab_ref[far_idx[k * LPC + d]], preferred_element_type=jnp.float32
            ).astype(jnp.bfloat16)
        acc = lax.dot_general(tiles, near_x[...], TN, preferred_element_type=jnp.float32)
        acc += lax.dot_general(rfac, far_t[...], TN, preferred_element_type=jnp.float32)
        b_buf[xhp, target] = acc

    def ring_step(t):
        for way in range(2):
            if way == 1 and t > ccw:
                continue
            if way == 0:
                target = lax.rem(z + cw + 1 - t, half)
                slot, dev = t - 1, right
            else:
                target = lax.rem(z + half - (ccw + 1 - t), half)
                slot, dev = cw + t - 1, left
            back(0, target)
            back(1, target)
            if t == 1:
                src = b_buf.at[:, target]
            else:
                arrivals[(way, t - 1)].wait_recv()
                ring_out[slot] = ring_in[slot - 1] + b_buf[:, target]
                src = ring_out.at[slot]
            c = remote(src, ring_in.at[slot], ring_send.at[slot], ring_recv.at[slot], dev)
            c.start()
            sends.append(c)
            arrivals[(way, t)] = c

    def col_step(o):
        dev = cols[o - 1]
        col_copies[o - 1].wait_recv()
        stage[o - 1] = p_ref[dev[1] // half, lax.rem(dev[1], half)] + pre[o - 1]
        c = remote(stage.at[o - 1], recv_f.at[o - 1], col_send.at[chips + o - 1], col_recv.at[chips + o - 1], dev)
        c.start()
        col_copies.append(c)

    for n in range(max(cw, chips - 1)):
        if n < cw:
            ring_step(n + 1)
        if n < chips - 1:
            col_step(n + 1)
    back(0, z)
    back(1, z)
    col_copies[chips - 1].wait_recv()
    arrivals[(0, cw)].wait_recv()
    arrivals[(1, ccw)].wait_recv()
    away = 1 - xh
    x_out[...] = ring_in[cw - 1, away] + ring_in[cw + ccw - 1, away] + b_buf[away, z]
    cross = remote(x_out, x_in, ring_send.at[half - 1], ring_recv.at[half - 1], partner)
    cross.start()
    for c in sends:
        c.wait_send()
    for c in col_copies:
        c.wait_send()
    for c in col_copies[chips:]:
        c.wait_recv()
    cross.wait()
    acc = ring_in[cw - 1, xh] + ring_in[cw + ccw - 1, xh] + b_buf[xh, z] + x_in[...] + p_ref[j // half, lax.rem(j, half)] + pre[chips - 1]
    for n in range(chips - 1):
        acc = acc + recv_f[n]
    out_ref[...] = acc.astype(out_ref.dtype)


def scatter_sum(partial, slab, near_local, far_local, near_tiles, far_left, far_right, nr, nc):
    tile = partial.shape[2:]
    half = nr // 2
    cw = half // 2
    steps = half - 1
    vmem = pltpu.VMEM
    return pl.pallas_call(
        functools.partial(scatter_kernel, nr, nc),
        out_shape=jax.ShapeDtypeStruct(tile, jnp.bfloat16),
        in_specs=[pl.BlockSpec(memory_space=pltpu.SMEM)] * 2
        + [pl.BlockSpec(memory_space=vmem)] * 2
        + [pl.BlockSpec(memory_space=pl.ANY)] * 3,
        out_specs=pl.BlockSpec(memory_space=vmem),
        scratch_shapes=[
            vmem(near_tiles.shape, near_tiles.dtype),
            vmem(far_left.shape, far_left.dtype),
            vmem(far_right.shape, far_right.dtype),
            vmem((2, half) + tile, jnp.float32),
            vmem((DPC * TILE, NRHS), jnp.bfloat16),
            vmem((LPC * RANK, NRHS), jnp.bfloat16),
            vmem((nc // 2 - 1,) + tile, jnp.float32),
            vmem((nc // 2,) + tile, jnp.float32),
            vmem((nc // 2 - 1,) + tile, jnp.float32),
            vmem((steps, 2) + tile, jnp.float32),
            vmem((steps, 2) + tile, jnp.float32),
            vmem(tile, jnp.float32),
            vmem(tile, jnp.float32),
            pltpu.SemaphoreType.DMA((nc - 1,)),
            pltpu.SemaphoreType.DMA((nc - 1,)),
            pltpu.SemaphoreType.DMA((half,)),
            pltpu.SemaphoreType.DMA((half,)),
            pltpu.SemaphoreType.DMA((3,)),
        ],
        compiler_params=pltpu.CompilerParams(
            collective_id=1, has_side_effects=True, vmem_limit_bytes=40 * 1024 * 1024),
    )(near_local, far_local, partial, slab.reshape((-1,) + tile), near_tiles, far_left, far_right)


def per_device(panel_values, near_tiles, far_left, far_right, near_rows, far_rows):
    n_row = lax.axis_size("row")
    n_col = lax.axis_size("col")
    clusters = panel_values.shape[0] // TILE
    groups = n_col * clusters
    colcount = n_row * clusters
    row_base = lax.axis_index("row") * groups
    near_local = near_rows - row_base
    far_local = far_rows - row_base
    slab = gather_slabs(panel_values, n_row, n_col)
    partial = local_products(near_local, far_local, near_tiles, far_left, far_right, slab, colcount, groups)
    return scatter_sum(partial, slab, near_local, far_local, near_tiles, far_left, far_right, n_row, n_col)


def solution(mesh):
    placed = (
        P(("row", "col"), None),
        P(("row", "col"), None, None),
        P(("row", "col"), None, None),
        P(("row", "col"), None, None),
        P(("row", "col")),
        P(("row", "col")),
    )
    return jax.shard_map(
        per_device, mesh=mesh, in_specs=placed, out_specs=P(("row", "col"), None), check_vma=False
    )
```

```python
import functools

import jax
import jax.numpy as jnp
from jax import lax
from jax.experimental import pallas as pl
from jax.experimental.pallas import tpu as pltpu
from jax.sharding import PartitionSpec as P

TILE = 256
RANK = 64
NRHS = 256
DPC = 2
LPC = 8

TN = (((0,), (0,)), ((), ()))


def local_kernel(half, per, near_idx, far_idx, tiles_ref, left_ref, right_ref, slab_ref, out_ref):
    step = pl.program_id(0)
    base = slab_ref.shape[0] - 2

    @pl.when(step == 0)
    def _():
        out_ref[...] = jnp.zeros_like(out_ref)

    for kk in range(per):
        k = step * per + kk
        xc = slab_ref[base + k // half, lax.rem(k, half)]
        tiles = tiles_ref[kk * DPC:(kk + 1) * DPC].reshape(DPC * TILE, TILE)
        near_f = jnp.dot(tiles, xc, preferred_element_type=jnp.float32)
        for d in range(DPC):
            r = near_idx[k * DPC + d]
            out_ref[r // half, lax.rem(r, half)] += near_f[d * TILE:(d + 1) * TILE]
        right = right_ref[kk * LPC:(kk + 1) * LPC].reshape(LPC * RANK, TILE)
        coef = jnp.dot(right, xc, preferred_element_type=jnp.float32).astype(jnp.bfloat16)
        for d in range(LPC):
            r = far_idx[k * LPC + d]
            out_ref[r // half, lax.rem(r, half)] += lax.dot_general(
                left_ref[kk * LPC + d], coef[d * RANK:(d + 1) * RANK], TN, preferred_element_type=jnp.float32)


def local_products(near_local, far_local, near_tiles, far_left, far_right, slab, count, groups):
    half = slab.shape[1]
    per = 4 if count % 4 == 0 else 1
    grid_spec = pltpu.PrefetchScalarGridSpec(
        num_scalar_prefetch=2,
        grid=(count // per,),
        in_specs=[
            pl.BlockSpec((per * DPC, TILE, TILE), lambda k, a, b: (k, 0, 0)),
            pl.BlockSpec((per * LPC, RANK, TILE), lambda k, a, b: (k, 0, 0)),
            pl.BlockSpec((per * LPC, RANK, TILE), lambda k, a, b: (k, 0, 0)),
            pl.BlockSpec(memory_space=pltpu.VMEM),
        ],
        out_specs=pl.BlockSpec(memory_space=pltpu.VMEM),
    )
    flops = 2 * TILE * TILE * NRHS * near_tiles.shape[0] + 2 * RANK * TILE * NRHS * far_left.shape[0] * 2
    return pl.pallas_call(
        functools.partial(local_kernel, half, per),
        grid_spec=grid_spec,
        out_shape=jax.ShapeDtypeStruct((groups // half, half, TILE, NRHS), jnp.float32),
        compiler_params=pltpu.CompilerParams(
            dimension_semantics=("arbitrary",), vmem_limit_bytes=24 * 1024 * 1024
        ),
        cost_estimate=pl.CostEstimate(flops=flops, bytes_accessed=16 * 1024 * 1024, transcendentals=0),
    )(near_local, far_local, near_tiles, far_left, far_right, slab)


MESH_ID = pl.DeviceIdType.MESH


def layout(nr, nc):
    i = lax.axis_index("row")
    j = lax.axis_index("col")
    half = nr // 2
    xh = i // half
    z = lax.rem(i, half)
    chips = nc // 2
    core = lax.rem(j, 2)
    chip = j // 2
    cols = [(i, 2 * lax.rem(chip + o, chips) + core) for o in range(1, chips)]
    cols.append((i, 2 * chip + 1 - core))
    right = (xh * half + lax.rem(z + 1, half), j)
    left = (xh * half + lax.rem(z + half - 1, half), j)
    partner = (lax.rem(i + half, nr), j)
    return i, j, half, xh, z, cols, right, left, partner


def enter(devices):
    barrier = pltpu.get_barrier_semaphore()
    for dev in devices:
        pl.semaphore_signal(barrier, 1, device_id=dev, device_id_type=MESH_ID)
    pl.semaphore_wait(barrier, len(devices))


def remote(src, dst, ssem, rsem, dev):
    return pltpu.make_async_remote_copy(src, dst, ssem, rsem, device_id=dev, device_id_type=MESH_ID)


def gather_kernel(nr, nc, x_ref, slab_ref, col_send, col_recv, ring_send, ring_recv, local_sem):
    i, j, half, xh, z, cols, right, left, partner = layout(nr, nc)
    cw = half // 2
    ccw = half - 1 - cw
    enter(cols + [right, left, partner])
    chips = nc // 2
    core = lax.rem(j, 2)
    chip = j // 2
    base = nc // half
    mine = slab_ref.at[j // half, lax.rem(j, half)]
    other = remote(x_ref, slab_ref.at[base + xh, z], ring_send.at[0], ring_recv.at[0], partner)
    other.start()
    col_copies = [remote(x_ref, mine, col_send.at[n], col_recv.at[n], dev) for n, dev in enumerate(cols)]
    for c in col_copies:
        c.start()
    own_row = pltpu.make_async_copy(x_ref, mine, local_sem.at[0])
    own_col = pltpu.make_async_copy(x_ref, slab_ref.at[base + xh, z], local_sem.at[1])
    own_row.start()
    own_col.start()
    mate = cols[-1]
    ring = []
    state = {}

    def ring_step(t):
        if t == 1:
            own_col.wait()
            other.wait()
        for way in range(2):
            if way == 1 and t > ccw:
                continue
            if way == 0:
                origin = lax.rem(z - t + 1 + half, half)
                sem, dev = t, right
            else:
                origin = lax.rem(z + t - 1, half)
                sem, dev = cw + t, left
            if t > 1:
                state[way].wait_recv()
            c = remote(slab_ref.at[base:base + 2, origin], slab_ref.at[base:base + 2, origin], ring_send.at[sem], ring_recv.at[sem], dev)
            c.start()
            ring.append(c)
            state[way] = c

    def col_step(o):
        origin = 2 * lax.rem(chip + chips - o, chips) + core
        col_copies[o - 1].wait_recv()
        c = remote(slab_ref.at[origin // half, lax.rem(origin, half)], slab_ref.at[origin // half, lax.rem(origin, half)], col_send.at[chips + o - 1],
                   col_recv.at[chips + o - 1], mate)
        c.start()
        col_copies.append(c)

    for n in range(max(cw, chips - 1)):
        if n < cw:
            ring_step(n + 1)
        if n < chips - 1:
            col_step(n + 1)
    for c in ring:
        c.wait_send()
    state[0].wait_recv()
    state[1].wait_recv()
    for c in col_copies:
        c.wait_send()
    for c in col_copies[chips - 1:]:
        c.wait_recv()
    own_row.wait()


def gather_slabs(x, nr, nc):
    tile = x.shape
    half = nr // 2
    return pl.pallas_call(
        functools.partial(gather_kernel, nr, nc),
        out_shape=jax.ShapeDtypeStruct((nc // half + 2, half) + tile, x.dtype),
        in_specs=[pl.BlockSpec(memory_space=pl.ANY)],
        out_specs=pl.BlockSpec(memory_space=pltpu.VMEM),
        scratch_shapes=[
            pltpu.SemaphoreType.DMA((nc - 1,)),
            pltpu.SemaphoreType.DMA((nc - 1,)),
            pltpu.SemaphoreType.DMA((half,)),
            pltpu.SemaphoreType.DMA((half,)),
            pltpu.SemaphoreType.DMA((2,)),
        ],
        compiler_params=pltpu.CompilerParams(
            collective_id=0, has_side_effects=True, vmem_limit_bytes=16 * 1024 * 1024),
    )(x)


def scatter_kernel(nr, nc, near_idx, far_idx, p_ref, slab_ref, tiles_hbm, left_hbm, right_hbm, out_ref,
                   tiles_v, left_v, right_v, b_buf, near_x, far_t, recv_f, pre, stage, ring_in, ring_out, x_in, x_out,
                   col_send, col_recv, ring_send, ring_recv, local_sem):
    i, j, half, xh, z, cols, right, left, partner = layout(nr, nc)
    cw = half // 2
    ccw = half - 1 - cw
    loads = [pltpu.make_async_copy(src, dst, local_sem.at[n])
             for n, (src, dst) in enumerate([(tiles_hbm, tiles_v), (right_hbm, right_v), (left_hbm, left_v)])]
    for c in loads:
        c.start()
    enter(cols + [right, left, partner])
    chips = nc // 2
    core = lax.rem(j, 2)
    chip = j // 2
    mate = cols[-1]
    handed = [2 * lax.rem(chip + o, chips) + 1 - core for o in range(1, chips)] + [mate[1]]
    col_copies = [remote(p_ref.at[m // half, lax.rem(m, half)], pre.at[n], col_send.at[n], col_recv.at[n], mate) for n, m in enumerate(handed)]
    sends = []
    arrivals = {}
    for c in loads:
        c.wait()

    def back(xhp, target):
        k = xhp * half + target
        tiles = tiles_v[pl.ds(k * DPC, DPC)].reshape(DPC * TILE, TILE)
        for d in range(DPC):
            near_x[d * TILE:(d + 1) * TILE] = slab_ref[near_idx[k * DPC + d]]
        rfac = right_v[pl.ds(k * LPC, LPC)].reshape(LPC * RANK, TILE)
        for d in range(LPC):
            far_t[d * RANK:(d + 1) * RANK] = jnp.dot(
                left_v[k * LPC + d], slab_ref[far_idx[k * LPC + d]], preferred_element_type=jnp.float32
            ).astype(jnp.bfloat16)
        acc = lax.dot_general(tiles, near_x[...], TN, preferred_element_type=jnp.float32)
        acc += lax.dot_general(rfac, far_t[...], TN, preferred_element_type=jnp.float32)
        b_buf[xhp, target] = acc

    def ring_step(t):
        for way in range(2):
            if way == 1 and t > ccw:
                continue
            if way == 0:
                target = lax.rem(z + cw + 1 - t, half)
                slot, dev = t - 1, right
            else:
                target = lax.rem(z + half - (ccw + 1 - t), half)
                slot, dev = cw + t - 1, left
            back(0, target)
            back(1, target)
            if t == 1:
                src = b_buf.at[:, target]
            else:
                arrivals[(way, t - 1)].wait_recv()
                ring_out[slot] = ring_in[slot - 1] + b_buf[:, target]
                src = ring_out.at[slot]
            c = remote(src, ring_in.at[slot], ring_send.at[slot], ring_recv.at[slot], dev)
            c.start()
            sends.append(c)
            arrivals[(way, t)] = c

    def col_step(o):
        dev = cols[o - 1]
        col_copies[o - 1].wait_recv()
        stage[o - 1] = p_ref[dev[1] // half, lax.rem(dev[1], half)] + pre[o - 1]
        c = remote(stage.at[o - 1], recv_f.at[o - 1], col_send.at[chips + o - 1], col_recv.at[chips + o - 1], dev)
        c.start()
        col_copies.append(c)

    for n in range(max(cw, chips - 1)):
        if n < cw:
            ring_step(n + 1)
        if n == 0:
            for c in col_copies:
                c.start()
        if n < chips - 1:
            col_step(n + 1)
    back(0, z)
    back(1, z)
    col_copies[chips - 1].wait_recv()
    arrivals[(0, cw)].wait_recv()
    arrivals[(1, ccw)].wait_recv()
    away = 1 - xh
    x_out[...] = ring_in[cw - 1, away] + ring_in[cw + ccw - 1, away] + b_buf[away, z]
    cross = remote(x_out, x_in, ring_send.at[half - 1], ring_recv.at[half - 1], partner)
    cross.start()
    for c in sends:
        c.wait_send()
    for c in col_copies:
        c.wait_send()
    for c in col_copies[chips:]:
        c.wait_recv()
    cross.wait()
    acc = ring_in[cw - 1, xh] + ring_in[cw + ccw - 1, xh] + b_buf[xh, z] + x_in[...] + p_ref[j // half, lax.rem(j, half)] + pre[chips - 1]
    for n in range(chips - 1):
        acc = acc + recv_f[n]
    out_ref[...] = acc.astype(out_ref.dtype)


def scatter_sum(partial, slab, near_local, far_local, near_tiles, far_left, far_right, nr, nc):
    tile = partial.shape[2:]
    half = nr // 2
    cw = half // 2
    steps = half - 1
    vmem = pltpu.VMEM
    return pl.pallas_call(
        functools.partial(scatter_kernel, nr, nc),
        out_shape=jax.ShapeDtypeStruct(tile, jnp.bfloat16),
        in_specs=[pl.BlockSpec(memory_space=pltpu.SMEM)] * 2
        + [pl.BlockSpec(memory_space=vmem)] * 2
        + [pl.BlockSpec(memory_space=pl.ANY)] * 3,
        out_specs=pl.BlockSpec(memory_space=vmem),
        scratch_shapes=[
            vmem(near_tiles.shape, near_tiles.dtype),
            vmem(far_left.shape, far_left.dtype),
            vmem(far_right.shape, far_right.dtype),
            vmem((2, half) + tile, jnp.float32),
            vmem((DPC * TILE, NRHS), jnp.bfloat16),
            vmem((LPC * RANK, NRHS), jnp.bfloat16),
            vmem((nc // 2 - 1,) + tile, jnp.float32),
            vmem((nc // 2,) + tile, jnp.float32),
            vmem((nc // 2 - 1,) + tile, jnp.float32),
            vmem((steps, 2) + tile, jnp.float32),
            vmem((steps, 2) + tile, jnp.float32),
            vmem(tile, jnp.float32),
            vmem(tile, jnp.float32),
            pltpu.SemaphoreType.DMA((nc - 1,)),
            pltpu.SemaphoreType.DMA((nc - 1,)),
            pltpu.SemaphoreType.DMA((half,)),
            pltpu.SemaphoreType.DMA((half,)),
            pltpu.SemaphoreType.DMA((3,)),
        ],
        compiler_params=pltpu.CompilerParams(
            collective_id=1, has_side_effects=True, vmem_limit_bytes=40 * 1024 * 1024),
    )(near_local, far_local, partial, slab.reshape((-1,) + tile), near_tiles, far_left, far_right)


def per_device(panel_values, near_tiles, far_left, far_right, near_rows, far_rows):
    n_row = lax.axis_size("row")
    n_col = lax.axis_size("col")
    clusters = panel_values.shape[0] // TILE
    groups = n_col * clusters
    colcount = n_row * clusters
    row_base = lax.axis_index("row") * groups
    near_local = near_rows - row_base
    far_local = far_rows - row_base
    slab = gather_slabs(panel_values, n_row, n_col)
    partial = local_products(near_local, far_local, near_tiles, far_left, far_right, slab, colcount, groups)
    return scatter_sum(partial, slab, near_local, far_local, near_tiles, far_left, far_right, n_row, n_col)


def solution(mesh):
    placed = (
        P(("row", "col"), None),
        P(("row", "col"), None, None),
        P(("row", "col"), None, None),
        P(("row", "col"), None, None),
        P(("row", "col")),
        P(("row", "col")),
    )
    return jax.shard_map(
        per_device, mesh=mesh, in_specs=placed, out_specs=P(("row", "col"), None), check_vma=False
    )
```

```python
import functools

import jax
import jax.numpy as jnp
from jax import lax
from jax.experimental import pallas as pl
from jax.experimental.pallas import tpu as pltpu
from jax.sharding import PartitionSpec as P

TILE = 256
RANK = 64
NRHS = 256
DPC = 2
LPC = 8

TN = (((0,), (0,)), ((), ()))


def local_kernel(half, per, near_idx, far_idx, tiles_ref, left_ref, right_ref, slab_ref, out_ref):
    step = pl.program_id(0)
    base = slab_ref.shape[0] - 2

    @pl.when(step == 0)
    def _():
        out_ref[...] = jnp.zeros_like(out_ref)

    for kk in range(per):
        k = step * per + kk
        xc = slab_ref[base + k // half, lax.rem(k, half)]
        tiles = tiles_ref[kk * DPC:(kk + 1) * DPC].reshape(DPC * TILE, TILE)
        near_f = jnp.dot(tiles, xc, preferred_element_type=jnp.float32)
        for d in range(DPC):
            r = near_idx[k * DPC + d]
            out_ref[r // half, lax.rem(r, half)] += near_f[d * TILE:(d + 1) * TILE]
        right = right_ref[kk * LPC:(kk + 1) * LPC].reshape(LPC * RANK, TILE)
        coef = jnp.dot(right, xc, preferred_element_type=jnp.float32).astype(jnp.bfloat16)
        for d in range(LPC):
            r = far_idx[k * LPC + d]
            out_ref[r // half, lax.rem(r, half)] += lax.dot_general(
                left_ref[kk * LPC + d], coef[d * RANK:(d + 1) * RANK], TN, preferred_element_type=jnp.float32)


def local_products(near_local, far_local, near_tiles, far_left, far_right, slab, count, groups):
    half = slab.shape[1]
    per = 8 if count % 8 == 0 else 1
    grid_spec = pltpu.PrefetchScalarGridSpec(
        num_scalar_prefetch=2,
        grid=(count // per,),
        in_specs=[
            pl.BlockSpec((per * DPC, TILE, TILE), lambda k, a, b: (k, 0, 0)),
            pl.BlockSpec((per * LPC, RANK, TILE), lambda k, a, b: (k, 0, 0)),
            pl.BlockSpec((per * LPC, RANK, TILE), lambda k, a, b: (k, 0, 0)),
            pl.BlockSpec(memory_space=pltpu.VMEM),
        ],
        out_specs=pl.BlockSpec(memory_space=pltpu.VMEM),
    )
    flops = 2 * TILE * TILE * NRHS * near_tiles.shape[0] + 2 * RANK * TILE * NRHS * far_left.shape[0] * 2
    return pl.pallas_call(
        functools.partial(local_kernel, half, per),
        grid_spec=grid_spec,
        out_shape=jax.ShapeDtypeStruct((groups // half, half, TILE, NRHS), jnp.float32),
        compiler_params=pltpu.CompilerParams(
            dimension_semantics=("arbitrary",), vmem_limit_bytes=24 * 1024 * 1024
        ),
        cost_estimate=pl.CostEstimate(flops=flops, bytes_accessed=16 * 1024 * 1024, transcendentals=0),
    )(near_local, far_local, near_tiles, far_left, far_right, slab)


MESH_ID = pl.DeviceIdType.MESH


def layout(nr, nc):
    i = lax.axis_index("row")
    j = lax.axis_index("col")
    half = nr // 2
    xh = i // half
    z = lax.rem(i, half)
    chips = nc // 2
    core = lax.rem(j, 2)
    chip = j // 2
    cols = [(i, 2 * lax.rem(chip + o, chips) + core) for o in range(1, chips)]
    cols.append((i, 2 * chip + 1 - core))
    right = (xh * half + lax.rem(z + 1, half), j)
    left = (xh * half + lax.rem(z + half - 1, half), j)
    partner = (lax.rem(i + half, nr), j)
    return i, j, half, xh, z, cols, right, left, partner


def enter(devices):
    barrier = pltpu.get_barrier_semaphore()
    for dev in devices:
        pl.semaphore_signal(barrier, 1, device_id=dev, device_id_type=MESH_ID)
    pl.semaphore_wait(barrier, len(devices))


def remote(src, dst, ssem, rsem, dev):
    return pltpu.make_async_remote_copy(src, dst, ssem, rsem, device_id=dev, device_id_type=MESH_ID)


def gather_kernel(nr, nc, x_ref, slab_ref, col_send, col_recv, ring_send, ring_recv, local_sem):
    i, j, half, xh, z, cols, right, left, partner = layout(nr, nc)
    cw = half // 2
    ccw = half - 1 - cw
    enter(cols + [right, left, partner])
    chips = nc // 2
    core = lax.rem(j, 2)
    chip = j // 2
    base = nc // half
    mine = slab_ref.at[j // half, lax.rem(j, half)]
    other = remote(x_ref, slab_ref.at[base + xh, z], ring_send.at[0], ring_recv.at[0], partner)
    other.start()
    col_copies = [remote(x_ref, mine, col_send.at[n], col_recv.at[n], dev) for n, dev in enumerate(cols)]
    for c in col_copies:
        c.start()
    own_row = pltpu.make_async_copy(x_ref, mine, local_sem.at[0])
    own_col = pltpu.make_async_copy(x_ref, slab_ref.at[base + xh, z], local_sem.at[1])
    own_row.start()
    own_col.start()
    mate = cols[-1]
    ring = []
    state = {}

    def ring_step(t):
        if t == 1:
            own_col.wait()
            other.wait()
        for way in range(2):
            if way == 1 and t > ccw:
                continue
            if way == 0:
                origin = lax.rem(z - t + 1 + half, half)
                sem, dev = t, right
            else:
                origin = lax.rem(z + t - 1, half)
                sem, dev = cw + t, left
            if t > 1:
                state[way].wait_recv()
            c = remote(slab_ref.at[base:base + 2, origin], slab_ref.at[base:base + 2, origin], ring_send.at[sem], ring_recv.at[sem], dev)
            c.start()
            ring.append(c)
            state[way] = c

    def col_step(o):
        origin = 2 * lax.rem(chip + chips - o, chips) + core
        col_copies[o - 1].wait_recv()
        c = remote(slab_ref.at[origin // half, lax.rem(origin, half)], slab_ref.at[origin // half, lax.rem(origin, half)], col_send.at[chips + o - 1],
                   col_recv.at[chips + o - 1], mate)
        c.start()
        col_copies.append(c)

    for n in range(max(cw, chips - 1)):
        if n < cw:
            ring_step(n + 1)
        if n < chips - 1:
            col_step(n + 1)
    for c in ring:
        c.wait_send()
    state[0].wait_recv()
    state[1].wait_recv()
    for c in col_copies:
        c.wait_send()
    for c in col_copies[chips - 1:]:
        c.wait_recv()
    own_row.wait()


def gather_slabs(x, nr, nc):
    tile = x.shape
    half = nr // 2
    return pl.pallas_call(
        functools.partial(gather_kernel, nr, nc),
        out_shape=jax.ShapeDtypeStruct((nc // half + 2, half) + tile, x.dtype),
        in_specs=[pl.BlockSpec(memory_space=pl.ANY)],
        out_specs=pl.BlockSpec(memory_space=pltpu.VMEM),
        scratch_shapes=[
            pltpu.SemaphoreType.DMA((nc - 1,)),
            pltpu.SemaphoreType.DMA((nc - 1,)),
            pltpu.SemaphoreType.DMA((half,)),
            pltpu.SemaphoreType.DMA((half,)),
            pltpu.SemaphoreType.DMA((2,)),
        ],
        compiler_params=pltpu.CompilerParams(
            collective_id=0, has_side_effects=True, vmem_limit_bytes=16 * 1024 * 1024),
    )(x)


def scatter_kernel(nr, nc, near_idx, far_idx, p_ref, slab_ref, tiles_hbm, left_hbm, right_hbm, out_ref,
                   tiles_v, left_v, right_v, b_buf, near_x, far_t, recv_f, pre, stage, ring_in, ring_out, x_in, x_out,
                   col_send, col_recv, ring_send, ring_recv, local_sem):
    i, j, half, xh, z, cols, right, left, partner = layout(nr, nc)
    cw = half // 2
    ccw = half - 1 - cw
    loads = [pltpu.make_async_copy(src, dst, local_sem.at[n])
             for n, (src, dst) in enumerate([(tiles_hbm, tiles_v), (right_hbm, right_v), (left_hbm, left_v)])]
    for c in loads:
        c.start()
    enter(cols + [right, left, partner])
    chips = nc // 2
    core = lax.rem(j, 2)
    chip = j // 2
    mate = cols[-1]
    handed = [2 * lax.rem(chip + o, chips) + 1 - core for o in range(1, chips)] + [mate[1]]
    col_copies = [remote(p_ref.at[m // half, lax.rem(m, half)], pre.at[n], col_send.at[n], col_recv.at[n], mate) for n, m in enumerate(handed)]
    sends = []
    arrivals = {}
    for c in loads:
        c.wait()

    def back(xhp, target):
        k = xhp * half + target
        tiles = tiles_v[pl.ds(k * DPC, DPC)].reshape(DPC * TILE, TILE)
        for d in range(DPC):
            near_x[d * TILE:(d + 1) * TILE] = slab_ref[near_idx[k * DPC + d]]
        rfac = right_v[pl.ds(k * LPC, LPC)].reshape(LPC * RANK, TILE)
        for d in range(LPC):
            far_t[d * RANK:(d + 1) * RANK] = jnp.dot(
                left_v[k * LPC + d], slab_ref[far_idx[k * LPC + d]], preferred_element_type=jnp.float32
            ).astype(jnp.bfloat16)
        acc = lax.dot_general(tiles, near_x[...], TN, preferred_element_type=jnp.float32)
        acc += lax.dot_general(rfac, far_t[...], TN, preferred_element_type=jnp.float32)
        b_buf[xhp, target] = acc

    def ring_step(t):
        for way in range(2):
            if way == 1 and t > ccw:
                continue
            if way == 0:
                target = lax.rem(z + cw + 1 - t, half)
                slot, dev = t - 1, right
            else:
                target = lax.rem(z + half - (ccw + 1 - t), half)
                slot, dev = cw + t - 1, left
            back(0, target)
            back(1, target)
            if t == 1:
                src = b_buf.at[:, target]
            else:
                arrivals[(way, t - 1)].wait_recv()
                ring_out[slot] = ring_in[slot - 1] + b_buf[:, target]
                src = ring_out.at[slot]
            c = remote(src, ring_in.at[slot], ring_send.at[slot], ring_recv.at[slot], dev)
            c.start()
            sends.append(c)
            arrivals[(way, t)] = c

    def col_step(o):
        dev = cols[o - 1]
        col_copies[o - 1].wait_recv()
        stage[o - 1] = p_ref[dev[1] // half, lax.rem(dev[1], half)] + pre[o - 1]
        c = remote(stage.at[o - 1], recv_f.at[o - 1], col_send.at[chips + o - 1], col_recv.at[chips + o - 1], dev)
        c.start()
        col_copies.append(c)

    for n in range(max(cw, chips - 1)):
        if n < cw:
            ring_step(n + 1)
        if n == 0:
            for c in col_copies:
                c.start()
        if n < chips - 1:
            col_step(n + 1)
    back(0, z)
    back(1, z)
    col_copies[chips - 1].wait_recv()
    arrivals[(0, cw)].wait_recv()
    arrivals[(1, ccw)].wait_recv()
    away = 1 - xh
    x_out[...] = ring_in[cw - 1, away] + ring_in[cw + ccw - 1, away] + b_buf[away, z]
    cross = remote(x_out, x_in, ring_send.at[half - 1], ring_recv.at[half - 1], partner)
    cross.start()
    for c in sends:
        c.wait_send()
    for c in col_copies:
        c.wait_send()
    for c in col_copies[chips:]:
        c.wait_recv()
    cross.wait()
    acc = ring_in[cw - 1, xh] + ring_in[cw + ccw - 1, xh] + b_buf[xh, z] + x_in[...] + p_ref[j // half, lax.rem(j, half)] + pre[chips - 1]
    for n in range(chips - 1):
        acc = acc + recv_f[n]
    out_ref[...] = acc.astype(out_ref.dtype)


def scatter_sum(partial, slab, near_local, far_local, near_tiles, far_left, far_right, nr, nc):
    tile = partial.shape[2:]
    half = nr // 2
    cw = half // 2
    steps = half - 1
    vmem = pltpu.VMEM
    return pl.pallas_call(
        functools.partial(scatter_kernel, nr, nc),
        out_shape=jax.ShapeDtypeStruct(tile, jnp.bfloat16),
        in_specs=[pl.BlockSpec(memory_space=pltpu.SMEM)] * 2
        + [pl.BlockSpec(memory_space=vmem)] * 2
        + [pl.BlockSpec(memory_space=pl.ANY)] * 3,
        out_specs=pl.BlockSpec(memory_space=vmem),
        scratch_shapes=[
            vmem(near_tiles.shape, near_tiles.dtype),
            vmem(far_left.shape, far_left.dtype),
            vmem(far_right.shape, far_right.dtype),
            vmem((2, half) + tile, jnp.float32),
            vmem((DPC * TILE, NRHS), jnp.bfloat16),
            vmem((LPC * RANK, NRHS), jnp.bfloat16),
            vmem((nc // 2 - 1,) + tile, jnp.float32),
            vmem((nc // 2,) + tile, jnp.float32),
            vmem((nc // 2 - 1,) + tile, jnp.float32),
            vmem((steps, 2) + tile, jnp.float32),
            vmem((steps, 2) + tile, jnp.float32),
            vmem(tile, jnp.float32),
            vmem(tile, jnp.float32),
            pltpu.SemaphoreType.DMA((nc - 1,)),
            pltpu.SemaphoreType.DMA((nc - 1,)),
            pltpu.SemaphoreType.DMA((half,)),
            pltpu.SemaphoreType.DMA((half,)),
            pltpu.SemaphoreType.DMA((3,)),
        ],
        compiler_params=pltpu.CompilerParams(
            collective_id=1, has_side_effects=True, vmem_limit_bytes=40 * 1024 * 1024),
    )(near_local, far_local, partial, slab.reshape((-1,) + tile), near_tiles, far_left, far_right)


def per_device(panel_values, near_tiles, far_left, far_right, near_rows, far_rows):
    n_row = lax.axis_size("row")
    n_col = lax.axis_size("col")
    clusters = panel_values.shape[0] // TILE
    groups = n_col * clusters
    colcount = n_row * clusters
    row_base = lax.axis_index("row") * groups
    near_local = near_rows - row_base
    far_local = far_rows - row_base
    slab = gather_slabs(panel_values, n_row, n_col)
    partial = local_products(near_local, far_local, near_tiles, far_left, far_right, slab, colcount, groups)
    return scatter_sum(partial, slab, near_local, far_local, near_tiles, far_left, far_right, n_row, n_col)


def solution(mesh):
    placed = (
        P(("row", "col"), None),
        P(("row", "col"), None, None),
        P(("row", "col"), None, None),
        P(("row", "col"), None, None),
        P(("row", "col")),
        P(("row", "col")),
    )
    return jax.shard_map(
        per_device, mesh=mesh, in_specs=placed, out_specs=P(("row", "col"), None), check_vma=False
    )
```

```python
import functools

import jax
import jax.numpy as jnp
from jax import lax
from jax.experimental import pallas as pl
from jax.experimental.pallas import tpu as pltpu
from jax.sharding import PartitionSpec as P

TILE = 256
RANK = 64
NRHS = 256
DPC = 2
LPC = 8

TN = (((0,), (0,)), ((), ()))


def local_kernel(half, per, near_idx, far_idx, tiles_ref, left_ref, right_ref, slab_ref, out_ref):
    step = pl.program_id(0)
    base = slab_ref.shape[0] - 2

    @pl.when(step == 0)
    def _():
        out_ref[...] = jnp.zeros_like(out_ref)

    for kk in range(per):
        k = step * per + kk
        xc = slab_ref[base + k // half, lax.rem(k, half)]
        tiles = tiles_ref[kk * DPC:(kk + 1) * DPC].reshape(DPC * TILE, TILE)
        near_f = jnp.dot(tiles, xc, preferred_element_type=jnp.float32)
        for d in range(DPC):
            r = near_idx[k * DPC + d]
            out_ref[r // half, lax.rem(r, half)] += near_f[d * TILE:(d + 1) * TILE]
        right = right_ref[kk * LPC:(kk + 1) * LPC].reshape(LPC * RANK, TILE)
        coef = jnp.dot(right, xc, preferred_element_type=jnp.float32).astype(jnp.bfloat16)
        for d in range(LPC):
            r = far_idx[k * LPC + d]
            out_ref[r // half, lax.rem(r, half)] += lax.dot_general(
                left_ref[kk * LPC + d], coef[d * RANK:(d + 1) * RANK], TN, preferred_element_type=jnp.float32)


def local_products(near_local, far_local, near_tiles, far_left, far_right, slab, count, groups):
    half = slab.shape[1]
    per = 8 if count % 8 == 0 else 1
    grid_spec = pltpu.PrefetchScalarGridSpec(
        num_scalar_prefetch=2,
        grid=(count // per,),
        in_specs=[
            pl.BlockSpec((per * DPC, TILE, TILE), lambda k, a, b: (k, 0, 0)),
            pl.BlockSpec((per * LPC, RANK, TILE), lambda k, a, b: (k, 0, 0)),
            pl.BlockSpec((per * LPC, RANK, TILE), lambda k, a, b: (k, 0, 0)),
            pl.BlockSpec(memory_space=pltpu.VMEM),
        ],
        out_specs=pl.BlockSpec(memory_space=pltpu.VMEM),
    )
    flops = 2 * TILE * TILE * NRHS * near_tiles.shape[0] + 2 * RANK * TILE * NRHS * far_left.shape[0] * 2
    return pl.pallas_call(
        functools.partial(local_kernel, half, per),
        grid_spec=grid_spec,
        out_shape=jax.ShapeDtypeStruct((groups // half, half, TILE, NRHS), jnp.float32),
        compiler_params=pltpu.CompilerParams(
            dimension_semantics=("arbitrary",), vmem_limit_bytes=24 * 1024 * 1024
        ),
        cost_estimate=pl.CostEstimate(flops=flops, bytes_accessed=16 * 1024 * 1024, transcendentals=0),
    )(near_local, far_local, near_tiles, far_left, far_right, slab)


MESH_ID = pl.DeviceIdType.MESH


def layout(nr, nc):
    i = lax.axis_index("row")
    j = lax.axis_index("col")
    half = nr // 2
    xh = i // half
    z = lax.rem(i, half)
    chips = nc // 2
    core = lax.rem(j, 2)
    chip = j // 2
    cols = [(i, 2 * lax.rem(chip + o, chips) + core) for o in range(1, chips)]
    cols.append((i, 2 * chip + 1 - core))
    right = (xh * half + lax.rem(z + 1, half), j)
    left = (xh * half + lax.rem(z + half - 1, half), j)
    partner = (lax.rem(i + half, nr), j)
    return i, j, half, xh, z, cols, right, left, partner


def enter(devices):
    barrier = pltpu.get_barrier_semaphore()
    for dev in devices:
        pl.semaphore_signal(barrier, 1, device_id=dev, device_id_type=MESH_ID)
    pl.semaphore_wait(barrier, len(devices))


def remote(src, dst, ssem, rsem, dev):
    return pltpu.make_async_remote_copy(src, dst, ssem, rsem, device_id=dev, device_id_type=MESH_ID)


def gather_kernel(nr, nc, x_ref, slab_ref, col_send, col_recv, ring_send, ring_recv, local_sem):
    i, j, half, xh, z, cols, right, left, partner = layout(nr, nc)
    cw = half // 2
    ccw = half - 1 - cw
    enter(cols + [right, left, partner])
    chips = nc // 2
    core = lax.rem(j, 2)
    chip = j // 2
    base = nc // half
    mine = slab_ref.at[j // half, lax.rem(j, half)]
    other = remote(x_ref, slab_ref.at[base + xh, z], ring_send.at[0], ring_recv.at[0], partner)
    other.start()
    own_col = pltpu.make_async_copy(x_ref, slab_ref.at[base + xh, z], local_sem.at[1])
    own_col.start()
    col_copies = [remote(x_ref, mine, col_send.at[n], col_recv.at[n], dev) for n, dev in enumerate(cols)]
    for c in col_copies:
        c.start()
    own_row = pltpu.make_async_copy(x_ref, mine, local_sem.at[0])
    own_row.start()
    mate = cols[-1]
    ring = []
    state = {}

    def ring_step(t):
        if t == 1:
            own_col.wait()
            other.wait()
        for way in range(2):
            if way == 1 and t > ccw:
                continue
            if way == 0:
                origin = lax.rem(z - t + 1 + half, half)
                sem, dev = t, right
            else:
                origin = lax.rem(z + t - 1, half)
                sem, dev = cw + t, left
            if t > 1:
                state[way].wait_recv()
            c = remote(slab_ref.at[base:base + 2, origin], slab_ref.at[base:base + 2, origin], ring_send.at[sem], ring_recv.at[sem], dev)
            c.start()
            ring.append(c)
            state[way] = c

    def col_step(o):
        origin = 2 * lax.rem(chip + chips - o, chips) + core
        col_copies[o - 1].wait_recv()
        c = remote(slab_ref.at[origin // half, lax.rem(origin, half)], slab_ref.at[origin // half, lax.rem(origin, half)], col_send.at[chips + o - 1],
                   col_recv.at[chips + o - 1], mate)
        c.start()
        col_copies.append(c)

    for n in range(max(cw, chips - 1)):
        if n < cw:
            ring_step(n + 1)
        if n < chips - 1:
            col_step(n + 1)
    for c in ring:
        c.wait_send()
    state[0].wait_recv()
    state[1].wait_recv()
    for c in col_copies:
        c.wait_send()
    for c in col_copies[chips - 1:]:
        c.wait_recv()
    own_row.wait()


def gather_slabs(x, nr, nc):
    tile = x.shape
    half = nr // 2
    return pl.pallas_call(
        functools.partial(gather_kernel, nr, nc),
        out_shape=jax.ShapeDtypeStruct((nc // half + 2, half) + tile, x.dtype),
        in_specs=[pl.BlockSpec(memory_space=pl.ANY)],
        out_specs=pl.BlockSpec(memory_space=pltpu.VMEM),
        scratch_shapes=[
            pltpu.SemaphoreType.DMA((nc - 1,)),
            pltpu.SemaphoreType.DMA((nc - 1,)),
            pltpu.SemaphoreType.DMA((half,)),
            pltpu.SemaphoreType.DMA((half,)),
            pltpu.SemaphoreType.DMA((2,)),
        ],
        compiler_params=pltpu.CompilerParams(
            collective_id=0, has_side_effects=True, vmem_limit_bytes=16 * 1024 * 1024),
    )(x)


def scatter_kernel(nr, nc, near_idx, far_idx, p_ref, slab_ref, tiles_hbm, left_hbm, right_hbm, out_ref,
                   tiles_v, left_v, right_v, b_buf, near_x, far_t, recv_f, pre, stage, ring_in, ring_out, x_in, x_out,
                   col_send, col_recv, ring_send, ring_recv, local_sem):
    i, j, half, xh, z, cols, right, left, partner = layout(nr, nc)
    cw = half // 2
    ccw = half - 1 - cw
    loads = [pltpu.make_async_copy(src, dst, local_sem.at[n])
             for n, (src, dst) in enumerate([(tiles_hbm, tiles_v), (right_hbm, right_v), (left_hbm, left_v)])]
    for c in loads:
        c.start()
    enter(cols + [right, left, partner])
    chips = nc // 2
    core = lax.rem(j, 2)
    chip = j // 2
    mate = cols[-1]
    handed = [2 * lax.rem(chip + o, chips) + 1 - core for o in range(1, chips)] + [mate[1]]
    col_copies = [remote(p_ref.at[m // half, lax.rem(m, half)], pre.at[n], col_send.at[n], col_recv.at[n], mate) for n, m in enumerate(handed)]
    sends = []
    arrivals = {}
    for c in loads:
        c.wait()

    def back(xhp, target):
        k = xhp * half + target
        tiles = tiles_v[pl.ds(k * DPC, DPC)].reshape(DPC * TILE, TILE)
        for d in range(DPC):
            near_x[d * TILE:(d + 1) * TILE] = slab_ref[near_idx[k * DPC + d]]
        rfac = right_v[pl.ds(k * LPC, LPC)].reshape(LPC * RANK, TILE)
        for d in range(LPC):
            far_t[d * RANK:(d + 1) * RANK] = jnp.dot(
                left_v[k * LPC + d], slab_ref[far_idx[k * LPC + d]], preferred_element_type=jnp.float32
            ).astype(jnp.bfloat16)
        acc = lax.dot_general(tiles, near_x[...], TN, preferred_element_type=jnp.float32)
        acc += lax.dot_general(rfac, far_t[...], TN, preferred_element_type=jnp.float32)
        b_buf[xhp, target] = acc

    def ring_step(t):
        for way in range(2):
            if way == 1 and t > ccw:
                continue
            if way == 0:
                target = lax.rem(z + cw + 1 - t, half)
                slot, dev = t - 1, right
            else:
                target = lax.rem(z + half - (ccw + 1 - t), half)
                slot, dev = cw + t - 1, left
            back(0, target)
            back(1, target)
            if t == 1:
                src = b_buf.at[:, target]
            else:
                arrivals[(way, t - 1)].wait_recv()
                ring_out[slot] = ring_in[slot - 1] + b_buf[:, target]
                src = ring_out.at[slot]
            c = remote(src, ring_in.at[slot], ring_send.at[slot], ring_recv.at[slot], dev)
            c.start()
            sends.append(c)
            arrivals[(way, t)] = c

    def col_step(o):
        dev = cols[o - 1]
        col_copies[o - 1].wait_recv()
        stage[o - 1] = p_ref[dev[1] // half, lax.rem(dev[1], half)] + pre[o - 1]
        c = remote(stage.at[o - 1], recv_f.at[o - 1], col_send.at[chips + o - 1], col_recv.at[chips + o - 1], dev)
        c.start()
        col_copies.append(c)

    for n in range(max(cw, chips - 1)):
        if n < cw:
            ring_step(n + 1)
        if n == 0:
            for c in col_copies:
                c.start()
        if n < chips - 1:
            col_step(n + 1)
    back(0, z)
    back(1, z)
    col_copies[chips - 1].wait_recv()
    arrivals[(0, cw)].wait_recv()
    arrivals[(1, ccw)].wait_recv()
    away = 1 - xh
    x_out[...] = ring_in[cw - 1, away] + ring_in[cw + ccw - 1, away] + b_buf[away, z]
    cross = remote(x_out, x_in, ring_send.at[half - 1], ring_recv.at[half - 1], partner)
    cross.start()
    for c in sends:
        c.wait_send()
    for c in col_copies:
        c.wait_send()
    for c in col_copies[chips:]:
        c.wait_recv()
    cross.wait()
    acc = ring_in[cw - 1, xh] + ring_in[cw + ccw - 1, xh] + b_buf[xh, z] + x_in[...] + p_ref[j // half, lax.rem(j, half)] + pre[chips - 1]
    for n in range(chips - 1):
        acc = acc + recv_f[n]
    out_ref[...] = acc.astype(out_ref.dtype)


def scatter_sum(partial, slab, near_local, far_local, near_tiles, far_left, far_right, nr, nc):
    tile = partial.shape[2:]
    half = nr // 2
    cw = half // 2
    steps = half - 1
    vmem = pltpu.VMEM
    return pl.pallas_call(
        functools.partial(scatter_kernel, nr, nc),
        out_shape=jax.ShapeDtypeStruct(tile, jnp.bfloat16),
        in_specs=[pl.BlockSpec(memory_space=pltpu.SMEM)] * 2
        + [pl.BlockSpec(memory_space=vmem)] * 2
        + [pl.BlockSpec(memory_space=pl.ANY)] * 3,
        out_specs=pl.BlockSpec(memory_space=vmem),
        scratch_shapes=[
            vmem(near_tiles.shape, near_tiles.dtype),
            vmem(far_left.shape, far_left.dtype),
            vmem(far_right.shape, far_right.dtype),
            vmem((2, half) + tile, jnp.float32),
            vmem((DPC * TILE, NRHS), jnp.bfloat16),
            vmem((LPC * RANK, NRHS), jnp.bfloat16),
            vmem((nc // 2 - 1,) + tile, jnp.float32),
            vmem((nc // 2,) + tile, jnp.float32),
            vmem((nc // 2 - 1,) + tile, jnp.float32),
            vmem((steps, 2) + tile, jnp.float32),
            vmem((steps, 2) + tile, jnp.float32),
            vmem(tile, jnp.float32),
            vmem(tile, jnp.float32),
            pltpu.SemaphoreType.DMA((nc - 1,)),
            pltpu.SemaphoreType.DMA((nc - 1,)),
            pltpu.SemaphoreType.DMA((half,)),
            pltpu.SemaphoreType.DMA((half,)),
            pltpu.SemaphoreType.DMA((3,)),
        ],
        compiler_params=pltpu.CompilerParams(
            collective_id=1, has_side_effects=True, vmem_limit_bytes=40 * 1024 * 1024),
    )(near_local, far_local, partial, slab.reshape((-1,) + tile), near_tiles, far_left, far_right)


def per_device(panel_values, near_tiles, far_left, far_right, near_rows, far_rows):
    n_row = lax.axis_size("row")
    n_col = lax.axis_size("col")
    clusters = panel_values.shape[0] // TILE
    groups = n_col * clusters
    colcount = n_row * clusters
    row_base = lax.axis_index("row") * groups
    near_local = near_rows - row_base
    far_local = far_rows - row_base
    slab = gather_slabs(panel_values, n_row, n_col)
    partial = local_products(near_local, far_local, near_tiles, far_left, far_right, slab, colcount, groups)
    return scatter_sum(partial, slab, near_local, far_local, near_tiles, far_left, far_right, n_row, n_col)


def solution(mesh):
    placed = (
        P(("row", "col"), None),
        P(("row", "col"), None, None),
        P(("row", "col"), None, None),
        P(("row", "col"), None, None),
        P(("row", "col")),
        P(("row", "col")),
    )
    return jax.shard_map(
        per_device, mesh=mesh, in_specs=placed, out_specs=P(("row", "col"), None), check_vma=False
    )
```
